32 devices in a mesh: dp: 2 (over y), fsdp: 16 (over z, x, core).
Axes of the slice: x: 2, y: 2, z: 4, core: 2. Of those that a mesh axis runs over, the one named last changes fastest.
Arguments:
- block_input: bfloat16 [64, 512, 768], P(('dp', 'fsdp')), may hold values from -6 to 6
- segment_ids: int32 [64, 512], P(('dp', 'fsdp')), may hold values from 0 to 7, never falling along the last dimension, each value on 1 to 192 neighbouring positions
- cotangent: bfloat16 [64, 512, 768], P(('dp', 'fsdp')), may hold values from -12 to 12
- w_query: bfloat16 [768, 768], P(('dp', 'fsdp')), may hold values from -0.3125 to 0.3125
- b_query: bfloat16 [768], P(('dp', 'fsdp')), may hold values from -3 to 3
- w_key: bfloat16 [768, 768], P(('dp', 'fsdp')), may hold values from -0.3125 to 0.3125
- w_value: bfloat16 [768, 768], P(('dp', 'fsdp')), may hold values from -0.21875 to 0.21875
- b_value: bfloat16 [768], P(('dp', 'fsdp')), may hold values from -3 to 3
- w_out: bfloat16 [768, 768], P(('dp', 'fsdp')), may hold values from -1.25 to 1.25
- b_out: bfloat16 [768], P(('dp', 'fsdp')), may hold values from -3 to 3
- gain_one: bfloat16 [768], P(('dp', 'fsdp')), may hold values from 0.25 to 1.75
- shift_one: bfloat16 [768], P(('dp', 'fsdp')), may hold values from -3 to 3
- w_inner: bfloat16 [768, 3072], P(('dp', 'fsdp')), may hold values from -0.21875 to 0.21875
- b_inner: bfloat16 [3072], P(('dp', 'fsdp')), may hold values from -3 to 3
- w_outer: bfloat16 [3072, 768], P(('dp', 'fsdp')), may hold values from -0.15625 to 0.15625
- b_outer: bfloat16 [768], P(('dp', 'fsdp')), may hold values from -3 to 3
- gain_two: bfloat16 [768], P(('dp', 'fsdp')), may hold values from 0.25 to 1.75
- shift_two: bfloat16 [768], P(('dp', 'fsdp')), may hold values from -3 to 3
Outputs:
- layer_out: bfloat16 [64, 512, 768], P(('dp', 'fsdp'))
- grad_input: bfloat16 [64, 512, 768], P(('dp', 'fsdp'))
- grad_w_query: float32 [768, 768], P(('dp', 'fsdp'))
- grad_b_query: float32 [768], P(('dp', 'fsdp'))
- grad_w_key: float32 [768, 768], P(('dp', 'fsdp'))
- grad_w_value: float32 [768, 768], P(('dp', 'fsdp'))
- grad_b_value: float32 [768], P(('dp', 'fsdp'))
- grad_w_out: float32 [768, 768], P(('dp', 'fsdp'))
- grad_b_out: float32 [768], P(('dp', 'fsdp'))
- grad_gain_one: float32 [768], P(('dp', 'fsdp'))
- grad_shift_one: float32 [768], P(('dp', 'fsdp'))
- grad_w_inner: float32 [768, 3072], P(('dp', 'fsdp'))
- grad_b_inner: float32 [3072], P(('dp', 'fsdp'))
- grad_w_outer: float32 [3072, 768], P(('dp', 'fsdp'))
- grad_b_outer: float32 [768], P(('dp', 'fsdp'))
- grad_gain_two: float32 [768], P(('dp', 'fsdp'))
- grad_shift_two: float32 [768], P(('dp', 'fsdp'))
The draws below stay inside these ranges and needn't reach their ends.
Inputs may be any that keep to these rules, and one draw needn't show every extreme that they name: `segment_ids`: along each row the numbers never fall; one document has 1 to 192 tokens, and some document has exactly 192.
All inputs are finite; a program needn't handle non-finite values.
Results may differ from the reference program's by a relative error of at most 0.015.
The reference program's roundings to bfloat16 on the way count: a program that leaves them out, or rounds other values in their place, can miss the bound.
Values may be sent and summed in bfloat16 or wider, within the bound.
No kernel may reach another device: no remote copies, remote signals or barrier semaphores. Data moves between devices by JAX's collectives and lax.ppermute only.
A program may use at most 192 MiB of HBM per device.

```python
import math
import jax
import jax.numpy as jnp
import numpy as np
from jax import lax

D = 768
HEADS = 12
HEAD_DIM = 64
FF = 3072
SEQ = 512
SEGS = 8
SEG_MOST = 192
SEQS = 64


def strengthened(array, key, source, target, parts, factor):
    def block_of(position):
        return (jnp.arange(array.shape[position]) // (array.shape[position] // parts)).reshape((-1,) + (1,) * (array.ndim - 1 - position))

    near = jax.random.permutation(key, parts)[block_of(target)]
    second = (block_of(target) + parts // 2) % parts
    return jnp.where((block_of(source) == near) | (block_of(source) == second), factor * array, array)


def block_scale(key, shape, shards, low, top_value):
    level = 1.0
    for position, parts in shards:
        steps = jax.random.uniform(jax.random.fold_in(jax.random.fold_in(key, 6), position), (parts,), jnp.float32, low / len(shards), top_value / len(shards))
        level = level * jnp.repeat(jnp.exp(steps), shape[position] // parts).reshape((-1,) + (1,) * (len(shape) - 1 - position))
    return level


def profile(amount, total, reach, skew):
    weights = [(1 << 20) // math.isqrt(rank ** skew) + 1 for rank in range(2, amount + 1)]
    spare, counts = total - reach - (amount - 1), [1] * (amount - 1)
    while spare > 0:
        free = [i for i in range(amount - 1) if counts[i] < reach]
        whole, left = sum([weights[i] for i in free]), spare
        for i in free:
            more = min(reach - counts[i], max(1, left * weights[i] // whole), spare)
            counts[i] = counts[i] + more
            spare = spare - more
    return np.array([reach] + counts)


def ragged_sizes(own_key, count, total, most, lean):
    if count == 2:
        one = jax.random.randint(own_key, (), max(1, total - most), min(most, total - 1) + 1)
        return jnp.stack([one, total - one])
    tallies = jnp.asarray(profile(count, total, most, lean), jnp.int32)
    twos = (count - 1) // 2
    source_of, receiver = tallies[1:1 + 2 * twos:2], tallies[2:2 + 2 * twos:2]
    slack = jnp.minimum(source_of - 1, most - receiver)
    shifted = jax.random.randint(jax.random.fold_in(own_key, 1), (twos,), 0, 1 << 20) % (slack + 1)
    tallies = tallies.at[1:1 + 2 * twos:2].set(source_of - shifted).at[2:2 + 2 * twos:2].set(receiver + shifted)
    return tallies[jax.random.permutation(jax.random.fold_in(own_key, 2), count)]


def gaussian(own_key, shape, width, limit, cuts=(), held_as=jnp.bfloat16):
    values = width * jax.random.normal(own_key, shape, jnp.float32)
    if cuts:
        values = values * block_scale(own_key, shape, cuts, -0.22, 0.18)
    return jnp.clip(values, -limit, limit).astype(held_as)


def bell_draw_with(own_key, extent, width, reach, split, heavy, kind=jnp.bfloat16):
    drawn = width * jax.random.normal(own_key, extent, jnp.float32)
    if split:
        drawn = drawn * block_scale(own_key, extent, split, -0.22, 0.18)
    return jnp.clip(strengthened(drawn, jax.random.fold_in(own_key, 3), *heavy), -reach, reach).astype(kind)


def setup_inputs(seed: int = 0) -> dict:
    arg_keys = jax.random.split(jax.random.key(seed), 19)
    return {
        "block_input": gaussian(arg_keys[0], (SEQS, SEQ, D), 1.0, 6.0, ((0, 32),)),
        "segment_ids": jax.vmap(lambda own: jnp.searchsorted(jnp.cumsum(ragged_sizes(own, SEGS, SEQ, SEG_MOST, 1)), jnp.arange(SEQ), side="right"))(jax.random.split(arg_keys[1], SEQS)).reshape((SEQS, SEQ)).astype(jnp.int32),
        "cotangent": bell_draw_with(arg_keys[2], (SEQS, SEQ, D), 1.0, 12.0, ((0, 32),), (0, 2, 32, 2.75)),
        "w_query": gaussian(arg_keys[3], (D, D), (D // 2) ** -0.5, 0.3125, ((0, 32),)),
        "b_query": gaussian(arg_keys[4], (D,), 0.5, 3.0, ((0, 32),)),
        "w_key": gaussian(arg_keys[5], (D, D), (D // 2) ** -0.5, 0.3125, ((0, 32),)),
        "w_value": gaussian(arg_keys[6], (D, D), D ** -0.5, 0.21875, ((0, 32),)),
        "b_value": gaussian(arg_keys[7], (D,), 0.5, 3.0, ((0, 32),)),
        "w_out": gaussian(arg_keys[8], (D, D), (D // 32) ** -0.5, 1.25, ((0, 32),)),
        "b_out": gaussian(arg_keys[9], (D,), 0.5, 3.0, ((0, 32),)),
        "gain_one": jnp.clip(1.0 + 0.15 * jax.random.normal(arg_keys[10], (D,), jnp.float32), 0.25, 1.75).astype(jnp.bfloat16),
        "shift_one": gaussian(arg_keys[11], (D,), 0.5, 3.0, ((0, 32),)),
        "w_inner": gaussian(arg_keys[12], (D, FF), D ** -0.5, 0.21875, ((0, 32),)),
        "b_inner": gaussian(arg_keys[13], (FF,), 0.5, 3.0, ((0, 32),)),
        "w_outer": gaussian(arg_keys[14], (FF, D), (FF // 2) ** -0.5, 0.15625, ((0, 32),)),
        "b_outer": gaussian(arg_keys[15], (D,), 0.5, 3.0, ((0, 32),)),
        "gain_two": jnp.clip(1.0 + 0.15 * jax.random.normal(arg_keys[16], (D,), jnp.float32), 0.25, 1.75).astype(jnp.bfloat16),
        "shift_two": gaussian(arg_keys[17], (D,), 0.5, 3.0, ((0, 32),)),
    }


@jax.custom_vjp
def low(v):
    return lax.optimization_barrier(v.astype(jnp.bfloat16)).astype(jnp.float32)

@jax.custom_vjp
def low_back(v):
    return v

def low_keep(v):
    return (low(v), None)

def low_pass(kept, grad):
    return (grad,)

def back_keep(v):
    return (v, None)

def back_low(kept, grad):
    return (low(grad),)
low.defvjp(low_keep, low_pass)
low_back.defvjp(back_keep, back_low)
epsilon_norm = 1e-05

def layer_norm(hidden, gain_vec, shift_vec):
    mean_val = lax.optimization_barrier(jnp.mean(hidden, axis=-1, keepdims=True))
    centred = hidden - mean_val
    variance = lax.optimization_barrier(jnp.mean(centred * centred, axis=-1, keepdims=True))
    return centred * lax.rsqrt(variance + epsilon_norm) * gain_vec + shift_vec

def matmul_high(left, right):
    return jnp.dot(left, right, precision=lax.Precision.HIGHEST)

def forward(tokens, same_segment, params):
    w_query, b_query, w_key, w_value, b_value, w_out, b_out, gain_one, shift_one, w_inner, b_inner, w_outer, b_outer, gain_two, shift_two = params
    seq_count = tokens.shape[0]
    flat_rows = tokens.reshape(seq_count * SEQ, D)
    queries = low_back(low(matmul_high(flat_rows, w_query) + b_query))
    key_rows = low_back(low(matmul_high(flat_rows, w_key)))
    values = low_back(low(matmul_high(flat_rows, w_value) + b_value))
    query_heads = queries.reshape(seq_count, SEQ, HEADS, HEAD_DIM)
    key_heads = key_rows.reshape(seq_count, SEQ, HEADS, HEAD_DIM)
    value_heads = values.reshape(seq_count, SEQ, HEADS, HEAD_DIM)
    scores = low_back(jnp.einsum('bqhd,bkhd->bhqk', query_heads, key_heads, precision=lax.Precision.HIGHEST) * HEAD_DIM ** (-0.5))
    masked = jnp.where(same_segment[:, None], scores, -1e+30)
    probs_low = low(jax.nn.softmax(masked, axis=-1))
    context = jnp.einsum('bhqk,bkhd->bqhd', probs_low, value_heads, precision=lax.Precision.HIGHEST)
    context = low_back(low(context.reshape(seq_count * SEQ, D)))
    attention = low_back(matmul_high(context, w_out) + b_out)
    hidden_one = flat_rows + attention
    normed_one = layer_norm(hidden_one, gain_one, shift_one)
    pre_act = low_back(matmul_high(low(normed_one), w_inner) + b_inner)
    activated = low(jax.nn.gelu(pre_act, approximate=True))
    branch = low_back(matmul_high(activated, w_outer) + b_outer)
    result = layer_norm(normed_one + branch, gain_two, shift_two)
    return result.reshape(seq_count, SEQ, D)

def reference(block_input, segment_ids, cotangent, w_query, b_query, w_key, w_value, b_value, w_out, b_out, gain_one, shift_one, w_inner, b_inner, w_outer, b_outer, gain_two, shift_two):
    params = tuple((weight.astype(jnp.float32) for weight in (w_query, b_query, w_key, w_value, b_value, w_out, b_out, gain_one, shift_one, w_inner, b_inner, w_outer, b_outer, gain_two, shift_two)))
    group_size = math.gcd(SEQS, 8)
    groups = SEQS // group_size
    tokens_all = block_input.astype(jnp.float32).reshape(groups, group_size, SEQ, D)
    segments_all = segment_ids.reshape(groups, group_size, SEQ)
    cotangent_all = cotangent.astype(jnp.float32).reshape(groups, group_size, SEQ, D)

    def group_step(totals, pieces):
        tokens_group, segments_group, cotangent_group = pieces
        same_segment = segments_group[:, :, None] == segments_group[:, None, :]
        result, pullback = jax.vjp(lambda tokens, weights: forward(tokens, same_segment, weights), tokens_group, params)
        d_tokens, d_params = pullback(cotangent_group)
        totals = tuple((running + fresh for running, fresh in zip(totals, d_params)))
        return (totals, (result.astype(jnp.bfloat16), d_tokens.astype(jnp.bfloat16)))
    initial = tuple((jnp.zeros_like(weight) for weight in params))
    totals, (results, d_inputs) = lax.scan(group_step, initial, (tokens_all, segments_all, cotangent_all))
    return (results.reshape(SEQS, SEQ, D), d_inputs.reshape(SEQS, SEQ, D), totals[0], totals[1], totals[2], totals[3], totals[4], totals[5], totals[6], totals[7], totals[8], totals[9], totals[10], totals[11], totals[12], totals[13], totals[14])
```

```python
from functools import partial

import jax
import jax.numpy as jnp
from jax import lax
from jax.sharding import PartitionSpec as P

D = 768
HEADS = 12
HEAD_DIM = 64
SEQ = 512


epsilon_norm = 1e-05


def layer_norm(hidden, gain_vec, shift_vec):
    mean_val = jnp.mean(hidden, axis=-1, keepdims=True)
    centred = hidden - mean_val
    variance = jnp.mean(centred * centred, axis=-1, keepdims=True)
    return centred * lax.rsqrt(variance + epsilon_norm) * gain_vec + shift_vec


def matmul(left, right):
    return jnp.dot(left, right, preferred_element_type=jnp.float32)


def to_float(vector):
    return vector.astype(jnp.float32)


def soft_probs(query_heads, key_heads, same_segment, log_total):
    scores = jnp.einsum(
        "bqhd,bkhd->bhqk", query_heads, key_heads, preferred_element_type=jnp.float32
    ) * HEAD_DIM ** (-0.5)
    masked = jnp.where(same_segment[:, None], scores, -1e30)
    return (masked, jnp.exp(masked - log_total))


def forward(tokens, same_segment, params):
    (
        w_query,
        b_query,
        w_key,
        w_value,
        b_value,
        w_out,
        b_out,
        gain_one,
        shift_one,
        w_inner,
        b_inner,
        w_outer,
        b_outer,
        gain_two,
        shift_two,
    ) = params
    seq_count = tokens.shape[0]
    row_count = seq_count * SEQ
    flat_rows = tokens.reshape(row_count, D)
    queries = (matmul(flat_rows, w_query) + to_float(b_query)).astype(jnp.bfloat16)
    key_rows = matmul(flat_rows, w_key).astype(jnp.bfloat16)
    values = (matmul(flat_rows, w_value) + to_float(b_value)).astype(jnp.bfloat16)
    query_heads = queries.reshape(seq_count, SEQ, HEADS, HEAD_DIM)
    key_heads = key_rows.reshape(seq_count, SEQ, HEADS, HEAD_DIM)
    value_heads = values.reshape(seq_count, SEQ, HEADS, HEAD_DIM)
    scores = jnp.einsum(
        "bqhd,bkhd->bhqk", query_heads, key_heads, preferred_element_type=jnp.float32
    ) * HEAD_DIM ** (-0.5)
    masked = jnp.where(same_segment[:, None], scores, -1e30)
    row_max = jnp.max(masked, axis=-1, keepdims=True)
    total = jnp.sum(jnp.exp(masked - row_max), axis=-1, keepdims=True)
    log_total = row_max + jnp.log(total)
    probs_low = jnp.exp(masked - log_total).astype(jnp.bfloat16)
    context = jnp.einsum(
        "bhqk,bkhd->bqhd", probs_low, value_heads, preferred_element_type=jnp.float32
    )
    context = context.reshape(row_count, D).astype(jnp.bfloat16)
    attention = matmul(context, w_out) + to_float(b_out)
    hidden_one = flat_rows.astype(jnp.float32) + attention
    normed_one = layer_norm(hidden_one, to_float(gain_one), to_float(shift_one))
    normed_low = normed_one.astype(jnp.bfloat16)
    pre_act = matmul(normed_low, w_inner) + to_float(b_inner)
    activated = jax.nn.gelu(pre_act, approximate=True).astype(jnp.bfloat16)
    branch = matmul(activated, w_outer) + to_float(b_outer)
    hidden_two = normed_one + branch
    result = layer_norm(hidden_two, to_float(gain_two), to_float(shift_two)).astype(jnp.bfloat16)
    kept = (
        query_heads,
        key_heads,
        value_heads,
        log_total,
        context,
        hidden_one,
        normed_low,
        pre_act,
        activated,
        hidden_two,
    )
    return (result.reshape(tokens.shape), kept)


def backward_ffn(cotangent, params, kept):
    (
        w_query,
        b_query,
        w_key,
        w_value,
        b_value,
        w_out,
        b_out,
        gain_one,
        shift_one,
        w_inner,
        b_inner,
        w_outer,
        b_outer,
        gain_two,
        shift_two,
    ) = params
    (
        query_heads,
        key_heads,
        value_heads,
        log_total,
        context,
        hidden_one,
        normed_low,
        pre_act,
        activated,
        hidden_two,
    ) = kept
    grad_rows = cotangent.reshape(hidden_two.shape).astype(jnp.float32)
    unused_two, norm_back = jax.vjp(layer_norm, hidden_two, to_float(gain_two), to_float(shift_two))
    d_hidden_two, d_gain_two, d_shift_two = norm_back(grad_rows)
    d_branch = d_hidden_two.astype(jnp.bfloat16)
    d_b_outer = jnp.sum(d_branch.astype(jnp.float32), axis=0)
    d_w_outer = jnp.einsum("nf,nd->fd", activated, d_branch, preferred_element_type=jnp.float32)
    d_activated = jnp.einsum("nd,fd->nf", d_branch, w_outer, preferred_element_type=jnp.float32)
    unused_act, gelu_back = jax.vjp(partial(jax.nn.gelu, approximate=True), pre_act)
    d_pre = gelu_back(d_activated)[0].astype(jnp.bfloat16)
    d_b_inner = jnp.sum(d_pre.astype(jnp.float32), axis=0)
    d_w_inner = jnp.einsum("nd,nf->df", normed_low, d_pre, preferred_element_type=jnp.float32)
    d_normed = d_hidden_two + jnp.einsum(
        "nf,df->nd", d_pre, w_inner, preferred_element_type=jnp.float32
    )
    return (d_normed, (d_w_inner, d_b_inner, d_w_outer, d_b_outer, d_gain_two, d_shift_two))


def backward_attention(tokens, same_segment, d_normed, params, kept):
    (
        w_query,
        b_query,
        w_key,
        w_value,
        b_value,
        w_out,
        b_out,
        gain_one,
        shift_one,
        w_inner,
        b_inner,
        w_outer,
        b_outer,
        gain_two,
        shift_two,
    ) = params
    (
        query_heads,
        key_heads,
        value_heads,
        log_total,
        context,
        hidden_one,
        normed_low,
        pre_act,
        activated,
        hidden_two,
    ) = kept
    seq_count = tokens.shape[0]
    row_count = seq_count * SEQ
    flat_rows = tokens.reshape(row_count, D)
    unused_one, norm_back = jax.vjp(layer_norm, hidden_one, to_float(gain_one), to_float(shift_one))
    d_hidden_one, d_gain_one, d_shift_one = norm_back(d_normed)
    d_attention = d_hidden_one.astype(jnp.bfloat16)
    d_b_out = jnp.sum(d_attention.astype(jnp.float32), axis=0)
    d_w_out = jnp.einsum("nd,ne->de", context, d_attention, preferred_element_type=jnp.float32)
    d_context = jnp.einsum("ne,de->nd", d_attention, w_out, preferred_element_type=jnp.float32)
    d_context = d_context.astype(jnp.bfloat16).reshape(seq_count, SEQ, HEADS, HEAD_DIM)
    masked, probs = soft_probs(query_heads, key_heads, same_segment, log_total)
    d_probs = jnp.einsum(
        "bqhd,bkhd->bhqk", d_context, value_heads, preferred_element_type=jnp.float32
    )
    d_values = jnp.einsum(
        "bhqk,bqhd->bkhd", probs.astype(jnp.bfloat16), d_context, preferred_element_type=jnp.float32
    ).astype(jnp.bfloat16)
    d_scores = probs * (d_probs - jnp.sum(probs * d_probs, axis=-1, keepdims=True))
    d_scores = d_scores.astype(jnp.bfloat16)
    score_scale = HEAD_DIM ** (-0.5)
    d_queries = (
        jnp.einsum("bhqk,bkhd->bqhd", d_scores, key_heads, preferred_element_type=jnp.float32)
        * score_scale
    ).astype(jnp.bfloat16)
    d_keys = (
        jnp.einsum("bhqk,bqhd->bkhd", d_scores, query_heads, preferred_element_type=jnp.float32)
        * score_scale
    ).astype(jnp.bfloat16)
    d_queries = d_queries.reshape(row_count, D)
    d_keys = d_keys.reshape(row_count, D)
    d_values = d_values.reshape(row_count, D)
    d_w_query = jnp.einsum("nd,ne->de", flat_rows, d_queries, preferred_element_type=jnp.float32)
    d_w_key = jnp.einsum("nd,ne->de", flat_rows, d_keys, preferred_element_type=jnp.float32)
    d_w_value = jnp.einsum("nd,ne->de", flat_rows, d_values, preferred_element_type=jnp.float32)
    d_b_query = jnp.sum(d_queries.astype(jnp.float32), axis=0)
    d_b_value = jnp.sum(d_values.astype(jnp.float32), axis=0)
    d_input = (
        d_hidden_one
        + jnp.einsum("ne,de->nd", d_queries, w_query, preferred_element_type=jnp.float32)
        + jnp.einsum("ne,de->nd", d_keys, w_key, preferred_element_type=jnp.float32)
        + jnp.einsum("ne,de->nd", d_values, w_value, preferred_element_type=jnp.float32)
    )
    d_input = d_input.astype(jnp.bfloat16).reshape(tokens.shape)
    return (
        d_input,
        (
            d_w_query,
            d_b_query,
            d_w_key,
            d_w_value,
            d_b_value,
            d_w_out,
            d_b_out,
            d_gain_one,
            d_shift_one,
        ),
    )


AXES = ("dp", "fsdp")
MATRICES = (0, 2, 3, 5, 9, 11)
VECTORS = (1, 4, 6, 7, 8, 10, 12, 13, 14)


def to_rows(array, lead):
    rows, columns = array.shape[-2:]
    if columns == D:
        return array
    blocks = [array[..., i : i + D] for i in range(0, columns, D)]
    return jnp.concatenate(blocks, axis=lead)


def gather_params(params):
    pieces = [to_rows(params[i], 0) for i in MATRICES]
    vector = jnp.concatenate([params[i] for i in VECTORS])
    pieces.append(jnp.pad(vector, (0, -vector.size % D)).reshape(-1, D))
    packed = jnp.concatenate(pieces, axis=0)
    whole = lax.all_gather(packed, AXES, axis=0, tiled=False)
    count = whole.shape[0]
    full = [None] * len(params)
    start = 0
    for i in MATRICES:
        rows, columns = params[i].shape
        blocks = []
        for _ in range(columns // D):
            blocks.append(whole[:, start : start + rows].reshape(count * rows, D))
            start += rows
        full[i] = jnp.concatenate(blocks, axis=1)
    vectors = whole[:, start:].reshape(count, -1)
    start = 0
    for i in VECTORS:
        size = params[i].size
        full[i] = vectors[:, start : start + size].reshape(-1)
        start += size
    return tuple(full)


def scatter_grads(grads):
    count = lax.axis_size(AXES)
    low = [grad.astype(jnp.bfloat16) for grad in grads]
    pieces = [to_rows(low[i].reshape(count, -1, low[i].shape[1]), 1) for i in MATRICES]
    vector = jnp.concatenate([low[i].reshape(count, -1) for i in VECTORS], axis=1)
    vector = jnp.pad(vector, ((0, 0), (0, -vector.shape[1] % D)))
    pieces.append(vector.reshape(count, -1, D))
    packed = jnp.concatenate(pieces, axis=1)
    mine = lax.psum_scatter(packed, AXES, scatter_dimension=0, tiled=False)
    mine = mine.astype(jnp.float32)
    shards = [None] * len(grads)
    start = 0
    for i in MATRICES:
        rows, columns = grads[i].shape[0] // count, grads[i].shape[1]
        blocks = []
        for _ in range(columns // D):
            blocks.append(mine[start : start + rows])
            start += rows
        shards[i] = jnp.concatenate(blocks, axis=1)
    vectors = mine[start:].reshape(-1)
    start = 0
    for i in VECTORS:
        size = grads[i].size // count
        shards[i] = vectors[start : start + size]
        start += size
    return shards


def on_device(
    block_input,
    segment_ids,
    cotangent,
    w_query,
    b_query,
    w_key,
    w_value,
    b_value,
    w_out,
    b_out,
    gain_one,
    shift_one,
    w_inner,
    b_inner,
    w_outer,
    b_outer,
    gain_two,
    shift_two,
):
    same_segment = segment_ids[:, :, None] == segment_ids[:, None, :]
    params = gather_params(
        (w_query, b_query, w_key, w_value, b_value, w_out, b_out, gain_one, shift_one)
        + (w_inner, b_inner, w_outer, b_outer, gain_two, shift_two)
    )
    result, kept = forward(block_input, same_segment, params)
    d_normed, ffn_terms = backward_ffn(cotangent, params, kept)
    d_w_inner, d_b_inner, d_w_outer, d_b_outer, d_gain_two, d_shift_two = ffn_terms
    d_input, attention_terms = backward_attention(block_input, same_segment, d_normed, params, kept)
    (
        d_w_query,
        d_b_query,
        d_w_key,
        d_w_value,
        d_b_value,
        d_w_out,
        d_b_out,
        d_gain_one,
        d_shift_one,
    ) = attention_terms
    shards = scatter_grads(
        (d_w_query, d_b_query, d_w_key, d_w_value, d_b_value, d_w_out, d_b_out, d_gain_one)
        + (d_shift_one, d_w_inner, d_b_inner, d_w_outer, d_b_outer, d_gain_two, d_shift_two)
    )
    return (
        result,
        d_input,
        shards[0],
        shards[1],
        shards[2],
        shards[3],
        shards[4],
        shards[5],
        shards[6],
        shards[7],
        shards[8],
        shards[9],
        shards[10],
        shards[11],
        shards[12],
        shards[13],
        shards[14],
    )


def solution(mesh):
    placed = (
        P(("dp", "fsdp"), None, None),
        P(("dp", "fsdp"), None),
        P(("dp", "fsdp"), None, None),
        P(("dp", "fsdp"), None),
        P(("dp", "fsdp")),
        P(("dp", "fsdp"), None),
        P(("dp", "fsdp"), None),
        P(("dp", "fsdp")),
        P(("dp", "fsdp"), None),
        P(("dp", "fsdp")),
        P(("dp", "fsdp")),
        P(("dp", "fsdp")),
        P(("dp", "fsdp"), None),
        P(("dp", "fsdp")),
        P(("dp", "fsdp"), None),
        P(("dp", "fsdp")),
        P(("dp", "fsdp")),
        P(("dp", "fsdp")),
    )
    return jax.shard_map(
        on_device,
        mesh=mesh,
        in_specs=placed,
        out_specs=(
            P(("dp", "fsdp"), None, None),
            P(("dp", "fsdp"), None, None),
            P(("dp", "fsdp"), None),
            P(("dp", "fsdp")),
            P(("dp", "fsdp"), None),
            P(("dp", "fsdp"), None),
            P(("dp", "fsdp")),
            P(("dp", "fsdp"), None),
            P(("dp", "fsdp")),
            P(("dp", "fsdp")),
            P(("dp", "fsdp")),
            P(("dp", "fsdp"), None),
            P(("dp", "fsdp")),
            P(("dp", "fsdp"), None),
            P(("dp", "fsdp")),
            P(("dp", "fsdp")),
            P(("dp", "fsdp")),
        ),
        check_vma=False,
    )
```

```python
import jax, jax.numpy as jnp
from jax import lax
from jax.experimental import pallas as pl
from jax.experimental.pallas import tpu as pltpu
from jax.sharding import PartitionSpec as P

D = 768
HEADS = 12
HEAD_DIM = 64
SEQ = 512
GROUP = 256
GROUPS = D // GROUP
TILE = 128
MOST = 192
QT = 512
KT = 256
LOW = jnp.bfloat16
F32 = jnp.float32
MIB = 1 << 20


def mm(a, b):
    return lax.dot_general(a, b, (((1,), (0,)), ((), ())), preferred_element_type=F32)


def mm_t(a, b):
    return lax.dot_general(a, b, (((1,), (1,)), ((), ())), preferred_element_type=F32)


def t_mm(a, b):
    return lax.dot_general(a, b, (((0,), (0,)), ((), ())), preferred_element_type=F32)


def near(i, tile):
    lo, hi = i * tile - MOST + 1, (i + 1) * tile + MOST - 1
    lo = max(0, lo // TILE * TILE)
    hi = min(SEQ, -(-hi // TILE) * TILE)
    return slice(lo, hi)


def attention_forward_kernel(
    x_ref, wq_ref, wk_ref, wv_ref, bq_ref, bv_ref, seg_col_ref, seg_row_ref, wo_ref, bo_ref,
    q_ref, k_ref, v_ref, ctx_ref, lse_ref, h1_ref, mask_ref,
):
    group = pl.program_id(1)
    x = x_ref[...]
    q_ref[...] = (mm(x, wq_ref[...]) + bq_ref[...]).astype(LOW)
    k_ref[...] = mm(x, wk_ref[...]).astype(LOW)
    v_ref[...] = (mm(x, wv_ref[...]) + bv_ref[...]).astype(LOW)

    @pl.when(group == 0)
    def _():
        mask_ref[...] = jnp.where(seg_col_ref[...] == seg_row_ref[0], 0.0, -1e30)

    lane = lax.broadcasted_iota(jnp.int32, (1, TILE), 1)
    scale = jnp.asarray(HEAD_DIM**-0.5, LOW)
    for pair in range(GROUP // TILE):
        lanes = slice(pair * TILE, (pair + 1) * TILE)
        for i in range(SEQ // QT):
            rows = slice(i * QT, (i + 1) * QT)
            keys = near(i, QT)
            q_pair = q_ref[rows, lanes] * scale
            v_pair = v_ref[keys, lanes]
            halves = []
            for half in range(2):
                head = 2 * pair + half
                mine = (lane // HEAD_DIM) == half
                scores = mm_t(jnp.where(mine, k_ref[keys, lanes], 0), q_pair)
                scores = scores + mask_ref[keys, rows]
                top = jnp.max(scores, axis=0, keepdims=True)
                weight = jnp.exp(scores - top)
                total = jnp.sum(weight, axis=0, keepdims=True)
                halves.append(t_mm((weight * (1.0 / total)).astype(LOW), v_pair))
                lse_ref[0, 0, head : head + 1, rows] = top + jnp.log(total)
            ctx_ref[rows, lanes] = jnp.where(lane < HEAD_DIM, halves[0], halves[1]).astype(LOW)

    @pl.when(group == 0)
    def _():
        h1_ref[...] = x.astype(F32) + bo_ref[...] + mm(ctx_ref[...], wo_ref[...])

    @pl.when(group > 0)
    def _():
        h1_ref[...] += mm(ctx_ref[...], wo_ref[...])


def attention_forward(x, seg, wq, bq, wk, wv, bv, wo, bo):
    rows = x.shape[0]
    seqs = rows // SEQ
    token = lambda b, g: (b, 0)
    mine = lambda b, g: (b, g)
    column = lambda b, g: (0, g)
    return pl.pallas_call(
        attention_forward_kernel,
        grid=(seqs, GROUPS),
        in_specs=[
            pl.BlockSpec((SEQ, D), token),
            pl.BlockSpec((D, GROUP), column),
            pl.BlockSpec((D, GROUP), column),
            pl.BlockSpec((D, GROUP), column),
            pl.BlockSpec((1, GROUP), column),
            pl.BlockSpec((1, GROUP), column),
            pl.BlockSpec((SEQ, 1), token),
            pl.BlockSpec((1, 1, SEQ), lambda b, g: (b, 0, 0)),
            pl.BlockSpec((GROUP, D), lambda b, g: (g, 0)),
            pl.BlockSpec((1, D), lambda b, g: (0, 0)),
        ],
        out_specs=[
            pl.BlockSpec((SEQ, GROUP), mine),
            pl.BlockSpec((SEQ, GROUP), mine),
            pl.BlockSpec((SEQ, GROUP), mine),
            pl.BlockSpec((SEQ, GROUP), mine),
            pl.BlockSpec((1, 1, 8, SEQ), lambda b, g: (b, g, 0, 0)),
            pl.BlockSpec((SEQ, D), token),
        ],
        out_shape=[
            jax.ShapeDtypeStruct((rows, D), LOW),
            jax.ShapeDtypeStruct((rows, D), LOW),
            jax.ShapeDtypeStruct((rows, D), LOW),
            jax.ShapeDtypeStruct((rows, D), LOW),
            jax.ShapeDtypeStruct((seqs, GROUPS, 8, SEQ), F32),
            jax.ShapeDtypeStruct((rows, D), F32),
        ],
        scratch_shapes=[pltpu.VMEM((SEQ, SEQ), F32)],
        compiler_params=pltpu.CompilerParams(vmem_limit_bytes=48 * MIB),
        cost_estimate=pl.CostEstimate(
            flops=rows * (8 * D * D + 4 * D * SEQ), bytes_accessed=20 * MIB, transcendentals=rows * SEQ * HEADS
        ),
        name="attention_forward",
    )(x, wq, wk, wv, bq, bv, seg.reshape(rows, 1), seg.reshape(seqs, 1, SEQ), wo, bo)


def attention_backward_kernel(
    x_ref, q_ref, k_ref, v_ref, ctx_ref, dctx_ref, lse_ref, seg_col_ref, seg_row_ref,
    wq_ref, wk_ref, wv_ref, dh1_ref,
    gwq_ref, gwk_ref, gwv_ref, gbq_ref, gbv_ref, dx_ref,
    xt_ref, acc_ref, ds_ref, dq_ref, dk_ref, dv_ref, wq_acc, wk_acc, wv_acc, mask_ref,
):
    group, row, seqs = pl.program_id(0), pl.program_id(1), pl.num_programs(1)

    @pl.when(group == 0)
    def _():
        xt_ref[row] = jnp.transpose(x_ref[...])
        acc_ref[row] = dh1_ref[...]
        mask_ref[row] = jnp.where(seg_col_ref[...] == seg_row_ref[0], 0.0, -1e30)

    head_of = lax.broadcasted_iota(jnp.int32, (8, GROUP), 1) // HEAD_DIM
    picks = (head_of == lax.broadcasted_iota(jnp.int32, (8, GROUP), 0)).astype(F32)
    product = ctx_ref[...].astype(F32) * dctx_ref[...].astype(F32)
    inner = lax.dot_general(
        picks, product, (((1,), (1,)), ((), ())),
        preferred_element_type=F32, precision=lax.Precision.HIGHEST,
    )
    lane = lax.broadcasted_iota(jnp.int32, (1, TILE), 1)
    scale = jnp.asarray(HEAD_DIM**-0.5, LOW)
    for pair in range(GROUP // TILE):
        lanes = slice(pair * TILE, (pair + 1) * TILE)
        dq_halves = []
        dk_halves = []
        dv_halves = []
        for half in range(2):
            mine = (lane // HEAD_DIM) == half
            head = 2 * pair + half
            dk_tiles = []
            dv_tiles = []
            for j in range(SEQ // KT):
                keys = slice(j * KT, (j + 1) * KT)
                span = near(j, KT)
                q_pair = q_ref[span, lanes] * scale
                dctx_pair = dctx_ref[span, lanes]
                scores = mm_t(jnp.where(mine, k_ref[keys, lanes], 0), q_pair)
                probs = jnp.exp(scores + mask_ref[row, keys, span] - lse_ref[0, 0, head : head + 1, span])
                d_probs = mm_t(jnp.where(mine, v_ref[keys, lanes], 0), dctx_pair)
                d_scores = (probs * (d_probs - inner[head : head + 1, span])).astype(LOW)
                ds_ref[keys, span] = d_scores
                dv_tiles.append(mm(probs.astype(LOW), dctx_pair))
                dk_tiles.append(mm(d_scores, q_pair))
            dk_halves.append(dk_tiles)
            dv_halves.append(dv_tiles)
            dq_tiles = []
            for i in range(SEQ // KT):
                span = near(i, KT)
                rows = slice(i * KT, (i + 1) * KT)
                dq_tiles.append(t_mm(ds_ref[span, rows], k_ref[span, lanes] * scale))
            dq_halves.append(dq_tiles)
        for i in range(SEQ // KT):
            rows = slice(i * KT, (i + 1) * KT)
            first = lane < HEAD_DIM
            dq_ref[rows, lanes] = jnp.where(first, dq_halves[0][i], dq_halves[1][i]).astype(LOW)
            dk_ref[rows, lanes] = jnp.where(first, dk_halves[0][i], dk_halves[1][i]).astype(LOW)
            dv_ref[rows, lanes] = jnp.where(first, dv_halves[0][i], dv_halves[1][i]).astype(LOW)
    dq, dk, dv = dq_ref[...], dk_ref[...], dv_ref[...]
    acc_ref[row] += mm_t(dq, wq_ref[...]) + mm_t(dk, wk_ref[...]) + mm_t(dv, wv_ref[...])
    xt = xt_ref[row]
    bias_q = jnp.sum(dq.astype(F32), axis=0, keepdims=True)
    bias_v = jnp.sum(dv.astype(F32), axis=0, keepdims=True)

    @pl.when(row == 0)
    def _():
        wq_acc[...] = mm(xt, dq)
        wk_acc[...] = mm(xt, dk)
        wv_acc[...] = mm(xt, dv)
        gbq_ref[...] = bias_q
        gbv_ref[...] = bias_v

    @pl.when(row > 0)
    def _():
        wq_acc[...] += mm(xt, dq)
        wk_acc[...] += mm(xt, dk)
        wv_acc[...] += mm(xt, dv)
        gbq_ref[...] += bias_q
        gbv_ref[...] += bias_v

    @pl.when(row == seqs - 1)
    def _():
        gwq_ref[...] = wq_acc[...].astype(LOW)
        gwk_ref[...] = wk_acc[...].astype(LOW)
        gwv_ref[...] = wv_acc[...].astype(LOW)

    dx_ref[...] = acc_ref[row].astype(LOW)


def attention_backward(x, seg, q, k, v, ctx, dctx, lse, wq, wk, wv, dh1):
    rows = x.shape[0]
    seqs = rows // SEQ
    token = lambda g, b: (b, 0)
    mine = lambda g, b: (b, g)
    column = lambda g, b: (0, g)
    return pl.pallas_call(
        attention_backward_kernel,
        grid=(GROUPS, seqs),
        in_specs=[pl.BlockSpec((SEQ, D), token)]
        + [pl.BlockSpec((SEQ, GROUP), mine)] * 5
        + [
            pl.BlockSpec((1, 1, 8, SEQ), lambda g, b: (b, g, 0, 0)),
            pl.BlockSpec((SEQ, 1), token),
            pl.BlockSpec((1, 1, SEQ), lambda g, b: (b, 0, 0)),
        ]
        + [pl.BlockSpec((D, GROUP), column)] * 3
        + [pl.BlockSpec((SEQ, D), token)],
        out_specs=[pl.BlockSpec((D, GROUP), column)] * 3
        + [pl.BlockSpec((1, GROUP), column)] * 2
        + [pl.BlockSpec((SEQ, D), token)],
        out_shape=[jax.ShapeDtypeStruct((D, D), LOW)] * 3
        + [jax.ShapeDtypeStruct((1, D), F32)] * 2
        + [jax.ShapeDtypeStruct((rows, D), LOW)],
        scratch_shapes=[
            pltpu.VMEM((seqs, D, SEQ), LOW),
            pltpu.VMEM((seqs, SEQ, D), F32),
            pltpu.VMEM((SEQ, SEQ), LOW),
            pltpu.VMEM((SEQ, GROUP), LOW),
            pltpu.VMEM((SEQ, GROUP), LOW),
            pltpu.VMEM((SEQ, GROUP), LOW),
            pltpu.VMEM((D, GROUP), F32),
            pltpu.VMEM((D, GROUP), F32),
            pltpu.VMEM((D, GROUP), F32),
            pltpu.VMEM((seqs, SEQ, SEQ), F32),
        ],
        compiler_params=pltpu.CompilerParams(vmem_limit_bytes=48 * MIB),
        cost_estimate=pl.CostEstimate(
            flops=rows * (12 * D * D + 10 * D * SEQ), bytes_accessed=30 * MIB, transcendentals=rows * SEQ * HEADS
        ),
        name="attention_backward",
    )(x, q, k, v, ctx, dctx, lse, seg.reshape(rows, 1), seg.reshape(seqs, 1, SEQ), wq, wk, wv, dh1)


FF = 3072
CHUNK = 768
ROWS = 256
EPS = 1e-05
ROOT = 0.7978845608028654
CUBE = 0.044715


def norm_parts(hidden):
    mean = jnp.mean(hidden, axis=1, keepdims=True)
    centred = hidden - mean
    inverse = lax.rsqrt(jnp.mean(centred * centred, axis=1, keepdims=True) + EPS)
    return centred * inverse, inverse


def norm_back(grad, gain, normed, inverse):
    scaled = grad * gain
    mean = jnp.mean(scaled, axis=1, keepdims=True)
    along = jnp.mean(scaled * normed, axis=1, keepdims=True)
    return inverse * (scaled - mean - normed * along)


def column_sum(array):
    return jnp.sum(array, axis=0, keepdims=True)


def gelu_and_slope(v):
    square = v * v
    bent = jnp.tanh(v * (ROOT + ROOT * CUBE * square))
    half = 0.5 + 0.5 * bent
    slope = half + (0.5 * v) * (1.0 - bent * bent) * (ROOT + 3.0 * ROOT * CUBE * square)
    return v * half, slope


def ffn_forward_kernel(
    h1_ref, cot_ref, wi_ref, wo_ref, bi_ref, bo_ref, g1_ref, s1_ref, g2_ref, s2_ref,
    out_ref, n1_ref, act_ref, slope_ref, db_ref, dh2_ref, gg2_ref, gs2_ref, gbo_ref,
    h2_ref,
):
    step = pl.program_id(0)
    tiles = [slice(i, i + ROWS) for i in range(0, h1_ref.shape[0], ROWS)]

    @pl.when(step == 0)
    def _():
        for rows in tiles:
            n, _ = norm_parts(h1_ref[rows, :])
            n1 = n * g1_ref[...] + s1_ref[...]
            n1_ref[rows, :] = n1.astype(LOW)
            h2_ref[rows, :] = n1 + bo_ref[...]

    for rows in tiles:
        pre = mm(n1_ref[rows, :], wi_ref[...]) + bi_ref[...]
        act, slope = gelu_and_slope(pre)
        act = act.astype(LOW)
        act_ref[rows, :] = act
        slope_ref[rows, :] = slope.astype(LOW)
        h2_ref[rows, :] += mm(act, wo_ref[...])

    @pl.when(step == pl.num_programs(0) - 1)
    def _():
        sums = [jnp.zeros((1, D), F32)] * 3
        for rows in tiles:
            n, inverse = norm_parts(h2_ref[rows, :])
            out_ref[rows, :] = (n * g2_ref[...] + s2_ref[...]).astype(LOW)
            cot = cot_ref[rows, :].astype(F32)
            dh2 = norm_back(cot, g2_ref[...], n, inverse)
            dh2_ref[rows, :] = dh2
            db = dh2.astype(LOW)
            db_ref[rows, :] = db
            new = (column_sum(cot * n), column_sum(cot), column_sum(db.astype(F32)))
            sums = [a + b for a, b in zip(sums, new)]
        gg2_ref[...], gs2_ref[...], gbo_ref[...] = sums


def ffn_forward(h1, cot, wi, wo, bi, bo, g1, s1, g2, s2):
    rows = h1.shape[0]
    all_rows = pl.BlockSpec((rows, D), lambda c: (0, 0))
    vector = pl.BlockSpec((1, D), lambda c: (0, 0))
    chunk = pl.BlockSpec((rows, CHUNK), lambda c: (0, c))
    return pl.pallas_call(
        ffn_forward_kernel,
        grid=(FF // CHUNK,),
        in_specs=[
            all_rows,
            all_rows,
            pl.BlockSpec((D, CHUNK), lambda c: (0, c)),
            pl.BlockSpec((CHUNK, D), lambda c: (c, 0)),
            pl.BlockSpec((1, CHUNK), lambda c: (0, c)),
            vector, vector, vector, vector, vector,
        ],
        out_specs=[all_rows, all_rows, chunk, chunk, all_rows, all_rows, vector, vector, vector],
        out_shape=[
            jax.ShapeDtypeStruct((rows, D), LOW),
            jax.ShapeDtypeStruct((rows, D), LOW),
            jax.ShapeDtypeStruct((rows, FF), LOW),
            jax.ShapeDtypeStruct((rows, FF), LOW),
            jax.ShapeDtypeStruct((rows, D), LOW),
            jax.ShapeDtypeStruct((rows, D), F32),
        ]
        + [jax.ShapeDtypeStruct((1, D), F32)] * 3,
        scratch_shapes=[pltpu.VMEM((rows, D), F32)],
        compiler_params=pltpu.CompilerParams(vmem_limit_bytes=56 * MIB),
        cost_estimate=pl.CostEstimate(flops=4 * rows * D * FF, bytes_accessed=34 * MIB, transcendentals=rows * FF),
        name="ffn_forward",
    )(h1, cot, wi, wo, bi, bo, g1, s1, g2, s2)


def ffn_backward_kernel(
    h1_ref, n1_ref, act_ref, slope_ref, db_ref, dh2_ref, ctx_ref, wi_ref, wo_ref, wout_ref, g1_ref,
    gwi_ref, gwo_ref, gbi_ref, gwout_ref, dctx_ref, dh1_ref, gg1_ref, gs1_ref, gbout_ref,
    n1t_ref, dn1_ref, dpre_ref, da_ref,
):
    step = pl.program_id(0)
    tiles = [slice(i, i + ROWS) for i in range(0, h1_ref.shape[0], ROWS)]

    @pl.when(step == 0)
    def _():
        n1t_ref[...] = jnp.transpose(n1_ref[...])
        dn1_ref[...] = dh2_ref[...]

    bias = jnp.zeros((1, CHUNK), F32)
    for rows in tiles:
        dpre = (mm_t(db_ref[rows, :], wo_ref[...]) * slope_ref[rows, :].astype(F32)).astype(LOW)
        dpre_ref[rows, :] = dpre
        bias += column_sum(dpre.astype(F32))
        dn1_ref[rows, :] += mm_t(dpre, wi_ref[...])
    gbi_ref[...] = bias
    gwo_ref[...] = t_mm(act_ref[...], db_ref[...]).astype(LOW)
    gwi_ref[...] = mm(n1t_ref[...], dpre_ref[...]).astype(LOW)

    @pl.when(step == pl.num_programs(0) - 1)
    def _():
        sums = [jnp.zeros((1, D), F32)] * 3
        for rows in tiles:
            n, inverse = norm_parts(h1_ref[rows, :])
            dn1 = dn1_ref[rows, :]
            dh1 = norm_back(dn1, g1_ref[...], n, inverse)
            dh1_ref[rows, :] = dh1
            da = dh1.astype(LOW)
            da_ref[rows, :] = da
            dctx_ref[rows, :] = mm_t(da, wout_ref[...]).astype(LOW)
            new = (column_sum(dn1 * n), column_sum(dn1), column_sum(da.astype(F32)))
            sums = [a + b for a, b in zip(sums, new)]
        gg1_ref[...], gs1_ref[...], gbout_ref[...] = sums
        gwout_ref[...] = t_mm(ctx_ref[...], da_ref[...]).astype(LOW)


def ffn_backward(h1, n1, act, slope, db, dh2, ctx, wi, wo, wout, g1):
    rows = h1.shape[0]
    all_rows = pl.BlockSpec((rows, D), lambda c: (0, 0))
    once = pl.BlockSpec((rows, D), lambda c: (0, 0), pipeline_mode=pl.Buffered(1))
    vector = pl.BlockSpec((1, D), lambda c: (0, 0))
    chunk = pl.BlockSpec((rows, CHUNK), lambda c: (0, c))
    inner = pl.BlockSpec((D, CHUNK), lambda c: (0, c))
    outer = pl.BlockSpec((CHUNK, D), lambda c: (c, 0))
    square = pl.BlockSpec((D, D), lambda c: (0, 0))
    return pl.pallas_call(
        ffn_backward_kernel,
        grid=(FF // CHUNK,),
        in_specs=[once, once, chunk, chunk, once, once, once, inner, outer, square, vector],
        out_specs=[inner, outer, pl.BlockSpec((1, CHUNK), lambda c: (0, c)), square, all_rows, all_rows]
        + [vector] * 3,
        out_shape=[
            jax.ShapeDtypeStruct((D, FF), LOW),
            jax.ShapeDtypeStruct((FF, D), LOW),
            jax.ShapeDtypeStruct((1, FF), F32),
            jax.ShapeDtypeStruct((D, D), LOW),
            jax.ShapeDtypeStruct((rows, D), LOW),
            jax.ShapeDtypeStruct((rows, D), F32),
        ]
        + [jax.ShapeDtypeStruct((1, D), F32)] * 3,
        scratch_shapes=[
            pltpu.VMEM((D, rows), LOW),
            pltpu.VMEM((rows, D), F32),
            pltpu.VMEM((rows, CHUNK), LOW),
            pltpu.VMEM((rows, D), LOW),
        ],
        compiler_params=pltpu.CompilerParams(vmem_limit_bytes=60 * MIB),
        cost_estimate=pl.CostEstimate(
            flops=8 * rows * D * FF + 4 * rows * D * D, bytes_accessed=46 * MIB, transcendentals=0
        ),
        name="ffn_backward",
    )(h1, n1, act, slope, db, dh2, ctx, wi, wo, wout, g1)


AXES = ("dp", "fsdp")
MATRICES = (0, 2, 3, 5, 9, 11)
VECTORS = (1, 4, 6, 7, 8, 10, 12, 13, 14)


def to_rows(array, lead):
    columns = array.shape[-1]
    if columns == D:
        return array
    return jnp.concatenate([array[..., i : i + D] for i in range(0, columns, D)], axis=lead)


def gather_params(params):
    pieces = [to_rows(params[i], 0) for i in MATRICES]
    vector = jnp.concatenate([params[i] for i in VECTORS])
    pieces.append(jnp.pad(vector, (0, -vector.size % D)).reshape(-1, D))
    packed = jnp.concatenate(pieces, axis=0)
    whole = lax.all_gather(packed, AXES, axis=0, tiled=False)
    count = whole.shape[0]
    full = [None] * len(params)
    start = 0
    for i in MATRICES:
        rows, columns = params[i].shape
        blocks = []
        for _ in range(columns // D):
            blocks.append(whole[:, start : start + rows].reshape(count * rows, D))
            start += rows
        full[i] = jnp.concatenate(blocks, axis=1)
    vectors = whole[:, start:].reshape(count, -1).astype(F32)
    start = 0
    for i in VECTORS:
        size = params[i].size
        full[i] = vectors[:, start : start + size].reshape(1, -1)
        start += size
    return tuple(full)


def scatter_grads(grads):
    count = lax.axis_size(AXES)
    low = [grad.astype(LOW) for grad in grads]
    pieces = [to_rows(low[i].reshape(count, -1, low[i].shape[1]), 1) for i in MATRICES]
    vector = jnp.concatenate([low[i].reshape(count, -1) for i in VECTORS], axis=1)
    vector = jnp.pad(vector, ((0, 0), (0, -vector.shape[1] % D)))
    pieces.append(vector.reshape(count, -1, D))
    packed = jnp.concatenate(pieces, axis=1)
    mine = lax.psum_scatter(packed, AXES, scatter_dimension=0, tiled=False)
    mine = mine.astype(F32)
    shards = [None] * len(grads)
    start = 0
    for i in MATRICES:
        rows, columns = grads[i].shape[0] // count, grads[i].shape[1]
        blocks = []
        for _ in range(columns // D):
            blocks.append(mine[start : start + rows])
            start += rows
        shards[i] = jnp.concatenate(blocks, axis=1)
    vectors = mine[start:].reshape(-1)
    start = 0
    for i in VECTORS:
        size = grads[i].size // count
        shards[i] = vectors[start : start + size]
        start += size
    return shards


def on_device(block_input, segment_ids, cotangent, *params):
    (
        w_query, b_query, w_key, w_value, b_value, w_out, b_out, gain_one, shift_one,
        w_inner, b_inner, w_outer, b_outer, gain_two, shift_two,
    ) = gather_params(params)
    x = block_input.reshape(-1, D)
    cot = cotangent.reshape(-1, D)
    q, k, v, ctx, lse, h1 = attention_forward(
        x, segment_ids, w_query, b_query, w_key, w_value, b_value, w_out, b_out
    )
    result, n1, act, slope, db, dh2, g_gain_two, g_shift_two, g_b_outer = ffn_forward(
        h1, cot, w_inner, w_outer, b_inner, b_outer, gain_one, shift_one, gain_two, shift_two
    )
    g_inner, g_outer, g_b_inner, g_out, dctx, dh1, g_gain_one, g_shift_one, g_b_out = ffn_backward(
        h1, n1, act, slope, db, dh2, ctx, w_inner, w_outer, w_out, gain_one
    )
    g_query, g_key, g_value, g_b_query, g_b_value, dx = attention_backward(
        x, segment_ids, q, k, v, ctx, dctx, lse, w_query, w_key, w_value, dh1
    )
    shards = scatter_grads(
        (g_query, g_b_query, g_key, g_value, g_b_value, g_out, g_b_out, g_gain_one, g_shift_one)
        + (g_inner, g_b_inner, g_outer, g_b_outer, g_gain_two, g_shift_two)
    )
    return (result.reshape(block_input.shape), dx.reshape(block_input.shape), *shards)


def solution(mesh):
    vector, matrix, rows = P(AXES), P(AXES, None), P(AXES, None, None)
    params = tuple(vector if i in VECTORS else matrix for i in range(15))
    return jax.shard_map(
        on_device,
        mesh=mesh,
        in_specs=(rows, matrix, rows) + params,
        out_specs=(rows, rows) + params,
        check_vma=False,
    )
```

```python
import jax
import jax.numpy as jnp
import numpy as np
from jax import lax
from jax.experimental import pallas as pl
from jax.experimental.pallas import tpu as pltpu
from jax.sharding import Mesh, PartitionSpec as P

D = 768
FF = 3072
HEADS = 12
HEAD_DIM = 64
SEQ = 512
MOST = 192
GROUP = 256
GROUPS = D // GROUP
TRIO = 3 * GROUP
PAIR = 128
QKV = 3 * D + PAIR
LATE = D + QKV
QT = 512
KT = 256
CHUNK = 768
CHUNKS = FF // CHUNK
ROWS = 256
EPS = 1e-05
SHARE = 1.0
ROOT = 0.7978845608028654
CUBE = 0.044715
LOW = jnp.bfloat16
F32 = jnp.float32
MIB = 1 << 20
MATRICES = (0, 2, 3, 5, 9, 11)
VECTORS = (1, 4, 6, 7, 8, 12, 13, 14, 10)
AXES = ("dp", "line", "side", "core")


def mm(a, b):
    return lax.dot_general(a, b, (((1,), (0,)), ((), ())), preferred_element_type=F32)


def mm_t(a, b):
    return lax.dot_general(a, b, (((1,), (1,)), ((), ())), preferred_element_type=F32)


def t_mm(a, b):
    return lax.dot_general(a, b, (((0,), (0,)), ((), ())), preferred_element_type=F32)


def cost(flops, moved, transcendentals):
    return pl.CostEstimate(
        flops=int(SHARE * flops),
        bytes_accessed=int(SHARE * moved),
        transcendentals=int(SHARE * transcendentals),
    )


def like(shape, kind):
    return jax.ShapeDtypeStruct(shape, kind)


def near(i, tile):
    lo, hi = i * tile - MOST + 1, (i + 1) * tile + MOST - 1
    lo = max(0, lo // PAIR * PAIR)
    hi = min(SEQ, -(-hi // PAIR) * PAIR)
    return slice(lo, hi)


def attention_forward_kernel(
    x_ref, w_ref, vec_ref, seg_col_ref, seg_row_ref,
    qkv_ref, ctx_ref, lse_ref, xt_ref, mask_ref,
):
    group = pl.program_id(1)
    x = x_ref[...]
    column = pl.ds(pl.multiple_of(group * GROUP, GROUP), GROUP)
    qkv_ref[:, :GROUP] = (mm(x, w_ref[:, :GROUP]) + vec_ref[0:1, column]).astype(LOW)
    qkv_ref[:, GROUP : 2 * GROUP] = mm(x, w_ref[:, GROUP : 2 * GROUP]).astype(LOW)
    qkv_ref[:, 2 * GROUP :] = (mm(x, w_ref[:, 2 * GROUP :]) + vec_ref[1:2, column]).astype(LOW)

    @pl.when(group == 0)
    def _():
        mask_ref[...] = jnp.where(seg_col_ref[...] == seg_row_ref[0], 0.0, -1e30)
        xt_ref[0] = jnp.transpose(x)

    lane = lax.broadcasted_iota(jnp.int32, (1, PAIR), 1)
    scale = jnp.asarray(HEAD_DIM**-0.5, LOW)
    for pair in range(GROUP // PAIR):
        q_lanes, k_lanes, v_lanes = (
            slice(part * GROUP + pair * PAIR, part * GROUP + (pair + 1) * PAIR) for part in range(3)
        )
        for i in range(SEQ // QT):
            rows = slice(i * QT, (i + 1) * QT)
            keys = near(i, QT)
            q_pair = qkv_ref[rows, q_lanes] * scale
            v_pair = qkv_ref[keys, v_lanes]
            halves = []
            for half in range(2):
                head = 2 * pair + half
                mine = (lane // HEAD_DIM) == half
                scores = mm_t(jnp.where(mine, qkv_ref[keys, k_lanes], 0), q_pair)
                scores = scores + mask_ref[keys, rows]
                top = jnp.max(scores, axis=0, keepdims=True)
                weight = jnp.exp(scores - top)
                total = jnp.sum(weight, axis=0, keepdims=True)
                halves.append(t_mm((weight * (1.0 / total)).astype(LOW), v_pair))
                lse_ref[0, 0, head : head + 1, rows] = top + jnp.log(total)
            ctx_ref[rows, q_lanes] = jnp.where(lane < HEAD_DIM, halves[0], halves[1]).astype(LOW)


def attention_forward(x, seg, w_qkv, table):
    rows = x.shape[0]
    seqs = rows // SEQ
    return pl.pallas_call(
        attention_forward_kernel,
        grid=(seqs, GROUPS),
        in_specs=[
            pl.BlockSpec((SEQ, D), lambda b, g: (b, 0)),
            pl.BlockSpec((D, TRIO), lambda b, g: (0, g)),
            pl.BlockSpec((8, D), lambda b, g: (0, 0)),
            pl.BlockSpec((SEQ, 1), lambda b, g: (b, 0)),
            pl.BlockSpec((1, 1, SEQ), lambda b, g: (b, 0, 0)),
        ],
        out_specs=[
            pl.BlockSpec((SEQ, TRIO), lambda b, g: (b, g)),
            pl.BlockSpec((SEQ, GROUP), lambda b, g: (b, g)),
            pl.BlockSpec((1, 1, 8, SEQ), lambda b, g: (b, g, 0, 0)),
            pl.BlockSpec((1, D, SEQ), lambda b, g: (b, 0, 0)),
        ],
        out_shape=[
            like((rows, 3 * D), LOW),
            like((rows, D), LOW),
            like((seqs, GROUPS, 8, SEQ), F32),
            like((seqs, D, SEQ), LOW),
        ],
        scratch_shapes=[pltpu.VMEM((SEQ, SEQ), F32)],
        compiler_params=pltpu.CompilerParams(vmem_limit_bytes=48 * MIB),
        cost_estimate=cost(rows * (6 * D * D + 4 * D * SEQ), 16 * MIB, rows * SEQ * HEADS),
        name="attention_forward",
    )(x, w_qkv, table, seg.reshape(rows, 1), seg.reshape(seqs, 1, SEQ))


def attention_backward_kernel(
    xt_ref, qkv_ref, ctx_ref, dctx_ref, lse_ref, seg_col_ref, seg_row_ref, vec_in_ref, gw_in_ref, dqkv_in_ref,
    gw_ref, dqkv_ref, vec_ref,
    ds_ref, acc_ref, mask_ref,
):
    row, seqs = pl.program_id(1), pl.num_programs(1)

    @pl.when(pl.program_id(0) == 0)
    def _():
        mask_ref[row] = jnp.where(seg_col_ref[...] == seg_row_ref[0], 0.0, -1e30)

    head_of = lax.broadcasted_iota(jnp.int32, (8, GROUP), 1) // HEAD_DIM
    picks = (head_of == lax.broadcasted_iota(jnp.int32, (8, GROUP), 0)).astype(F32)
    product = ctx_ref[...].astype(F32) * dctx_ref[...].astype(F32)
    inner = lax.dot_general(
        picks, product, (((1,), (1,)), ((), ())),
        preferred_element_type=F32, precision=lax.Precision.HIGHEST,
    )
    lane = lax.broadcasted_iota(jnp.int32, (1, PAIR), 1)
    first = lane < HEAD_DIM
    scale = jnp.asarray(HEAD_DIM**-0.5, LOW)
    for pair in range(GROUP // PAIR):
        q_lanes, k_lanes, v_lanes = (
            slice(part * GROUP + pair * PAIR, part * GROUP + (pair + 1) * PAIR) for part in range(3)
        )
        dq_halves = []
        dk_halves = []
        dv_halves = []
        for half in range(2):
            mine = (lane // HEAD_DIM) == half
            head = 2 * pair + half
            dk_tiles = []
            dv_tiles = []
            for j in range(SEQ // KT):
                keys = slice(j * KT, (j + 1) * KT)
                span = near(j, KT)
                q_pair = qkv_ref[span, q_lanes] * scale
                dctx_pair = dctx_ref[span, q_lanes]
                scores = mm_t(jnp.where(mine, qkv_ref[keys, k_lanes], 0), q_pair)
                probs = jnp.exp(scores + mask_ref[row, keys, span] - lse_ref[0, 0, head : head + 1, span])
                d_probs = mm_t(jnp.where(mine, qkv_ref[keys, v_lanes], 0), dctx_pair)
                d_scores = (probs * (d_probs - inner[head : head + 1, span])).astype(LOW)
                ds_ref[keys, span] = d_scores
                dv_tiles.append(mm(probs.astype(LOW), dctx_pair))
                dk_tiles.append(mm(d_scores, q_pair))
            dk_halves.append(dk_tiles)
            dv_halves.append(dv_tiles)
            dq_tiles = []
            for i in range(SEQ // KT):
                span = near(i, KT)
                rows = slice(i * KT, (i + 1) * KT)
                dq_tiles.append(t_mm(ds_ref[span, rows], qkv_ref[span, k_lanes] * scale))
            dq_halves.append(dq_tiles)
        for i in range(SEQ // KT):
            rows = slice(i * KT, (i + 1) * KT)
            dqkv_ref[rows, q_lanes] = jnp.where(first, dq_halves[0][i], dq_halves[1][i]).astype(LOW)
            dqkv_ref[rows, k_lanes] = jnp.where(first, dk_halves[0][i], dk_halves[1][i]).astype(LOW)
            dqkv_ref[rows, v_lanes] = jnp.where(first, dv_halves[0][i], dv_halves[1][i]).astype(LOW)
    dqkv = dqkv_ref[...]
    product = mm(xt_ref[0], dqkv)
    bias_q = jnp.sum(dqkv[:, :GROUP].astype(F32), axis=0, keepdims=True)
    bias_v = jnp.sum(dqkv[:, 2 * GROUP :].astype(F32), axis=0, keepdims=True)

    @pl.when(row == 0)
    def _():
        acc_ref[...] = product
        vec_ref[...] = vec_in_ref[...]
        vec_ref[0:1, :] = bias_q
        vec_ref[1:2, :] = bias_v

    @pl.when(row > 0)
    def _():
        acc_ref[...] += product
        vec_ref[0:1, :] += bias_q
        vec_ref[1:2, :] += bias_v

    @pl.when(row == seqs - 1)
    def _():
        gw_ref[...] = acc_ref[...].astype(LOW)


def attention_backward(group, seg, xt, qkv, ctx, dctx, lse, table, gw, dqkv=None):
    rows = ctx.shape[0]
    seqs = rows // SEQ
    mine = lambda g, b: (b, group)
    ours = lambda g, b: (0, group)
    anywhere = pl.BlockSpec(memory_space=pl.ANY)
    return pl.pallas_call(
        attention_backward_kernel,
        grid=(1, seqs),
        in_specs=[
            pl.BlockSpec((1, D, SEQ), lambda g, b: (b, 0, 0)),
            pl.BlockSpec((SEQ, TRIO), mine),
            pl.BlockSpec((SEQ, GROUP), mine),
            pl.BlockSpec((SEQ, GROUP), mine),
            pl.BlockSpec((1, 1, 8, SEQ), lambda g, b: (b, group, 0, 0)),
            pl.BlockSpec((SEQ, 1), lambda g, b: (b, 0)),
            pl.BlockSpec((1, 1, SEQ), lambda g, b: (b, 0, 0)),
            pl.BlockSpec((8, GROUP), ours),
            anywhere,
            anywhere,
        ],
        out_specs=[
            pl.BlockSpec((D, TRIO), lambda g, b: (0, 1 + group)),
            pl.BlockSpec((SEQ, TRIO), mine),
            pl.BlockSpec((8, GROUP), ours),
        ],
        out_shape=[like((D, LATE), LOW), like((rows, 3 * D), LOW), like((8, D), F32)],
        input_output_aliases={7: 2, 8: 0} if dqkv is None else {7: 2, 8: 0, 9: 1},
        scratch_shapes=[
            pltpu.VMEM((SEQ, SEQ), LOW),
            pltpu.VMEM((D, TRIO), F32),
            pltpu.VMEM((seqs, SEQ, SEQ), F32),
        ],
        compiler_params=pltpu.CompilerParams(vmem_limit_bytes=48 * MIB),
        cost_estimate=cost(
            rows * (6 * D * GROUP + 10 * GROUP * SEQ), 8 * MIB, rows * SEQ * HEADS // GROUPS
        ),
        name="attention_backward",
    )(
        xt, qkv, ctx, dctx, lse, seg.reshape(rows, 1), seg.reshape(seqs, 1, SEQ), table, gw,
        table if dqkv is None else dqkv,
    )


def input_grad_kernel(dh1_ref, dqkv_ref, w_ref, dx_ref):
    dx_ref[...] = (dh1_ref[...] + mm_t(dqkv_ref[...], w_ref[...])).astype(LOW)


def input_grad(dh1, dqkv, w_qkv):
    rows = dh1.shape[0]
    return pl.pallas_call(
        input_grad_kernel,
        grid=(rows // ROWS,),
        in_specs=[
            pl.BlockSpec((ROWS, D), lambda i: (i, 0)),
            pl.BlockSpec((ROWS, 3 * D), lambda i: (i, 0)),
            pl.BlockSpec((D, 3 * D), lambda i: (0, 0)),
        ],
        out_specs=pl.BlockSpec((ROWS, D), lambda i: (i, 0)),
        out_shape=like((rows, D), LOW),
        compiler_params=pltpu.CompilerParams(vmem_limit_bytes=40 * MIB),
        cost_estimate=cost(6 * rows * D * D, 13 * MIB, 0),
        name="input_grad",
    )(dh1, dqkv, w_qkv)


def norm_parts(hidden):
    mean = jnp.mean(hidden, axis=1, keepdims=True)
    centred = hidden - mean
    inverse = lax.rsqrt(jnp.mean(centred * centred, axis=1, keepdims=True) + EPS)
    return centred * inverse, inverse


def norm_back(grad, gain, normed, inverse):
    scaled = grad * gain
    mean = jnp.mean(scaled, axis=1, keepdims=True)
    along = jnp.mean(scaled * normed, axis=1, keepdims=True)
    return inverse * (scaled - mean - normed * along)


def column_sum(array):
    return jnp.sum(array, axis=0, keepdims=True)


def gelu_and_slope(v):
    square = v * v
    bent = jnp.tanh(v * (ROOT + ROOT * CUBE * square))
    half = 0.5 + 0.5 * bent
    slope = half + (0.5 * v) * (1.0 - bent * bent) * (ROOT + 3.0 * ROOT * CUBE * square)
    return v * half, slope


def order_outer(block_ref, out_ref, unit):
    for o in range(block_ref.shape[0] // unit):
        for j in range(CHUNKS):
            to = (o * CHUNKS + j) * unit
            out_ref[to : to + unit, :] = block_ref[o * unit : (o + 1) * unit, j * D : (j + 1) * D]


def ffn_forward_kernel(
    unit, x_ref, ctx_ref, cot_ref, outer_ref, wi_ref, wout_ref, bi_ref, vec_ref,
    out_ref, h1_ref, n1_ref, act_ref, slope_ref, db_ref, dh2_ref, sums_ref,
    h2_ref, wo_ref,
):
    step = pl.program_id(0)
    tiles = [slice(i, i + ROWS) for i in range(0, h1_ref.shape[0], ROWS)]
    order_outer(outer_ref, wo_ref, unit)

    @pl.when(step == 0)
    def _():
        for rows in tiles:
            h1 = x_ref[rows, :].astype(F32) + mm(ctx_ref[rows, :], wout_ref[...]) + vec_ref[2:3, :]
            h1_ref[rows, :] = h1
            n, _ = norm_parts(h1)
            n1 = n * vec_ref[3:4, :] + vec_ref[4:5, :]
            n1_ref[rows, :] = n1.astype(LOW)
            h2_ref[rows, :] = n1 + vec_ref[5:6, :]

    for rows in tiles:
        pre = mm(n1_ref[rows, :], wi_ref[...]) + bi_ref[...]
        act, slope = gelu_and_slope(pre)
        act = act.astype(LOW)
        act_ref[rows, :] = act
        slope_ref[rows, :] = slope.astype(LOW)
        h2_ref[rows, :] += mm(act, wo_ref[...])

    @pl.when(step == CHUNKS - 1)
    def _():
        gain, shift = vec_ref[6:7, :], vec_ref[7:8, :]
        sums = [jnp.zeros((1, D), F32)] * 3
        for rows in tiles:
            n, inverse = norm_parts(h2_ref[rows, :])
            out_ref[rows, :] = (n * gain + shift).astype(LOW)
            cot = cot_ref[rows, :].astype(F32)
            dh2 = norm_back(cot, gain, n, inverse)
            dh2_ref[rows, :] = dh2
            db = dh2.astype(LOW)
            db_ref[rows, :] = db
            new = (column_sum(db.astype(F32)), column_sum(cot * n), column_sum(cot))
            sums = [a + b for a, b in zip(sums, new)]
        sums_ref[...] = jnp.zeros_like(sums_ref)
        for i in range(3):
            sums_ref[5 + i : 6 + i, :] = sums[i]


def ffn_forward(unit, x, ctx, cot, rest, b_inner, table):
    rows = x.shape[0]
    all_rows = pl.BlockSpec((rows, D), lambda c: (0, 0))
    once = pl.BlockSpec((rows, D), lambda c: (0, 0), pipeline_mode=pl.Buffered(1))
    eight = pl.BlockSpec((8, D), lambda c: (0, 0))
    chunk = pl.BlockSpec((rows, CHUNK), lambda c: (0, c))
    return pl.pallas_call(
        lambda *refs: ffn_forward_kernel(unit, *refs),
        grid=(CHUNKS,),
        in_specs=[
            once,
            once,
            once,
            pl.BlockSpec((D // CHUNKS, FF), lambda c: (c, 0)),
            pl.BlockSpec((D, CHUNK), lambda c: (0, CHUNKS + c)),
            pl.BlockSpec((D, D), lambda c: (0, 2 * CHUNKS), pipeline_mode=pl.Buffered(1)),
            pl.BlockSpec((1, CHUNK), lambda c: (0, c)),
            eight,
        ],
        out_specs=[all_rows, all_rows, all_rows, chunk, chunk, all_rows, all_rows, eight],
        out_shape=[
            like((rows, D), LOW),
            like((rows, D), F32),
            like((rows, D), LOW),
            like((rows, FF), LOW),
            like((rows, FF), LOW),
            like((rows, D), LOW),
            like((rows, D), F32),
            like((8, D), F32),
        ],
        scratch_shapes=[pltpu.VMEM((rows, D), F32), pltpu.VMEM((CHUNK, D), LOW)],
        compiler_params=pltpu.CompilerParams(vmem_limit_bytes=60 * MIB),
        cost_estimate=cost(rows * D * (4 * FF + 2 * D), 40 * MIB, rows * FF),
        name="ffn_forward",
    )(x, ctx, cot, rest, rest, rest, b_inner, table)


def outer_grad_kernel(act_ref, db_ref, gwo_ref):
    gwo_ref[...] = t_mm(act_ref[...], db_ref[...]).astype(LOW)


def outer_grad(act, db):
    rows = db.shape[0]
    return pl.pallas_call(
        outer_grad_kernel,
        grid=(CHUNKS,),
        in_specs=[
            pl.BlockSpec((rows, CHUNK), lambda c: (0, c)),
            pl.BlockSpec((rows, D), lambda c: (0, 0)),
        ],
        out_specs=pl.BlockSpec((CHUNK, D), lambda c: (c, 0)),
        out_shape=like((FF, D), LOW),
        compiler_params=pltpu.CompilerParams(vmem_limit_bytes=40 * MIB),
        cost_estimate=cost(2 * rows * D * FF, 13 * MIB, 0),
        name="outer_grad",
    )(act, db)


def ffn_backward_kernel(
    unit, n1_ref, slope_ref, db_ref, dh2_ref, outer_ref, wi_ref,
    gwi_ref, gbi_ref, dn1_ref,
    n1t_ref, dpre_ref, wo_ref,
):
    step = pl.program_id(0)
    tiles = [slice(i, i + ROWS) for i in range(0, n1_ref.shape[0], ROWS)]

    @pl.when(step == 0)
    def _():
        n1t_ref[...] = jnp.transpose(n1_ref[...])
        dn1_ref[...] = dh2_ref[...]

    order_outer(outer_ref, wo_ref, unit)
    bias = jnp.zeros((1, CHUNK), F32)
    for rows in tiles:
        dpre = (mm_t(db_ref[rows, :], wo_ref[...]) * slope_ref[rows, :].astype(F32)).astype(LOW)
        dpre_ref[rows, :] = dpre
        bias += column_sum(dpre.astype(F32))
        dn1_ref[rows, :] += mm_t(dpre, wi_ref[...])
    gbi_ref[...] = bias
    gwi_ref[...] = mm(n1t_ref[...], dpre_ref[...]).astype(LOW)


def ffn_backward(unit, n1, slope, db, dh2, rest):
    rows = n1.shape[0]
    all_rows = pl.BlockSpec((rows, D), lambda c: (0, 0))
    once = pl.BlockSpec((rows, D), lambda c: (0, 0), pipeline_mode=pl.Buffered(1))
    return pl.pallas_call(
        lambda *refs: ffn_backward_kernel(unit, *refs),
        grid=(CHUNKS,),
        in_specs=[
            once,
            pl.BlockSpec((rows, CHUNK), lambda c: (0, c)),
            once,
            once,
            pl.BlockSpec((D // CHUNKS, FF), lambda c: (c, 0)),
            pl.BlockSpec((D, CHUNK), lambda c: (0, CHUNKS + c)),
        ],
        out_specs=[
            pl.BlockSpec((D, CHUNK), lambda c: (0, c)),
            pl.BlockSpec((1, CHUNK), lambda c: (0, c)),
            all_rows,
        ],
        out_shape=[like((D, FF), LOW), like((1, FF), F32), like((rows, D), F32)],
        scratch_shapes=[
            pltpu.VMEM((D, rows), LOW),
            pltpu.VMEM((rows, CHUNK), LOW),
            pltpu.VMEM((CHUNK, D), LOW),
        ],
        compiler_params=pltpu.CompilerParams(vmem_limit_bytes=56 * MIB),
        cost_estimate=cost(6 * rows * D * FF, 32 * MIB, 0),
        name="ffn_backward",
    )(n1, slope, db, dh2, rest, rest)


def norm_backward_kernel(
    h1_ref, dn1_ref, ctx_ref, wout_ref, vec_ref, sums_in_ref,
    gw_ref, dctx_ref, dh1_ref, sums_ref,
    da_ref,
):
    tiles = [slice(i, i + ROWS) for i in range(0, h1_ref.shape[0], ROWS)]
    sums = [jnp.zeros((1, D), F32)] * 3
    for rows in tiles:
        n, inverse = norm_parts(h1_ref[rows, :])
        dn1 = dn1_ref[rows, :]
        dh1 = norm_back(dn1, vec_ref[3:4, :], n, inverse)
        dh1_ref[rows, :] = dh1
        da = dh1.astype(LOW)
        da_ref[rows, :] = da
        dctx_ref[rows, :] = mm_t(da, wout_ref[...]).astype(LOW)
        new = (column_sum(da.astype(F32)), column_sum(dn1 * n), column_sum(dn1))
        sums = [a + b for a, b in zip(sums, new)]
    sums_ref[...] = sums_in_ref[...]
    for i in range(3):
        sums_ref[2 + i : 3 + i, :] = sums[i]
    gw_ref[...] = t_mm(ctx_ref[...], da_ref[...]).astype(LOW)


def norm_backward(h1, dn1, ctx, rest, table, sums):
    rows = h1.shape[0]
    all_rows = pl.BlockSpec((rows, D), lambda i: (0, 0))
    eight = pl.BlockSpec((8, D), lambda i: (0, 0))
    return pl.pallas_call(
        norm_backward_kernel,
        grid=(1,),
        in_specs=[
            all_rows,
            all_rows,
            all_rows,
            pl.BlockSpec((D, D), lambda i: (0, 2 * CHUNKS)),
            eight,
            eight,
        ],
        out_specs=[pl.BlockSpec((D, D), lambda i: (0, 0)), all_rows, all_rows, eight],
        out_shape=[like((D, LATE), LOW), like((rows, D), LOW), like((rows, D), F32), like((8, D), F32)],
        scratch_shapes=[pltpu.VMEM((rows, D), LOW)],
        compiler_params=pltpu.CompilerParams(vmem_limit_bytes=56 * MIB),
        cost_estimate=cost(4 * rows * D * D, 14 * MIB, 0),
        name="norm_backward",
    )(h1, dn1, ctx, rest, table, sums)


def after(values, *others):
    return lax.optimization_barrier((values, others))[0]


def whole(array):
    return pl.BlockSpec(array.shape, lambda *_: (0,) * len(array.shape))


def pack_kernel(wq_ref, wk_ref, wv_ref, wout_ref, wi_ref, wo_ref, *refs):
    vectors, (qkv_ref, rest_ref) = refs[:9], refs[9:]
    unit = wq_ref.shape[0]
    for g in range(GROUPS):
        for part, ref in enumerate((wq_ref, wk_ref, wv_ref)):
            to = g * TRIO + part * GROUP
            qkv_ref[:, to : to + GROUP] = ref[:, g * GROUP : (g + 1) * GROUP]
    qkv_ref[:, 3 * D :] = jnp.zeros((unit, PAIR), LOW)
    table = jnp.zeros((unit, PAIR), F32)
    row = lax.broadcasted_iota(jnp.int32, (unit, PAIR), 0)
    for i, ref in enumerate(vectors):
        size = ref.shape[1]
        line = jnp.concatenate([ref[...].astype(F32), jnp.zeros((1, PAIR - size), F32)], axis=1)
        table = jnp.where(row == i, line, table)
    qkv_ref[:, 3 * D :] = table.astype(LOW)
    for j in range(CHUNKS):
        rest_ref[:, j * D : (j + 1) * D] = wo_ref[j * unit : (j + 1) * unit, :]
    rest_ref[:, FF : 2 * FF] = wi_ref[...]
    rest_ref[:, 2 * FF :] = wout_ref[...]


def pack(wq, wk, wv, wout, wi, wo, vectors):
    unit = wq.shape[0]
    args = (wq, wk, wv, wout, wi, wo, *(v.reshape(1, -1) for v in vectors))
    shapes = [like((unit, QKV), LOW), like((unit, 2 * FF + D), LOW)]
    return pl.pallas_call(
        pack_kernel,
        in_specs=[whole(a) for a in args],
        out_specs=[whole(a) for a in shapes],
        out_shape=shapes,
        name="pack",
    )(*args)


def stack_kernel(*refs):
    for i, ref in enumerate(refs[:-1]):
        refs[-1][i] = ref[...]


def stack(pieces):
    shape = like((len(pieces), *pieces[0].shape), pieces[0].dtype)
    return pl.pallas_call(
        stack_kernel,
        in_specs=[whole(a) for a in pieces],
        out_specs=whole(shape),
        out_shape=shape,
        name="stack",
    )(*pieces)


class Slice:
    def __init__(self):
        self.sizes = tuple(lax.axis_size(name) for name in AXES)
        self.dp, self.line, self.side, self.core = (lax.axis_index(name) for name in AXES)
        self.offsets = [(a, b) for a in range(self.sizes[0]) for b in range(self.sizes[2])]

    def to_core(self, array):
        return lax.ppermute(array, "core", [(0, 1), (1, 0)])

    def to_plane(self, array, offset):
        dps, _, sides, _ = self.sizes
        pairs = [
            (i * sides + j, (i + offset[0]) % dps * sides + (j + offset[1]) % sides)
            for i in range(dps)
            for j in range(sides)
        ]
        return lax.ppermute(array, ("dp", "side"), pairs)

    def to_line(self, array, shift):
        count = self.sizes[1]
        return lax.ppermute(array, "line", [(i, (i + shift) % count) for i in range(count)])

    def gather(self, mine):
        dps, lines, sides, _ = self.sizes
        unit, columns = mine.shape
        line = stack([mine] + [self.to_line(mine, s) for s in range(1, lines)])
        here = [line if o == (0, 0) else self.to_plane(line, o) for o in self.offsets]
        there = [self.to_core(a) for a in here]
        place = jnp.stack([self.dp, self.line, self.side, self.core]).astype(jnp.int32)
        pieces = here + there

        def kernel(place_ref, *refs):
            out_ref = refs[-1]
            for i in range(len(pieces)):
                a, b = self.offsets[i % len(here)]
                dp = lax.rem(place_ref[0] + dps - a, dps)
                side = lax.rem(place_ref[2] + sides - b, sides)
                core = place_ref[3] if i < len(here) else 1 - place_ref[3]
                for s in range(lines):
                    along = lax.rem(place_ref[1] + lines - s, lines)
                    out_ref[((dp * lines + along) * sides + side) * 2 + core] = refs[i][s]

        shape = like((dps * lines * sides * 2, unit, columns), mine.dtype)
        return pl.pallas_call(
            kernel,
            in_specs=[pl.BlockSpec(memory_space=pltpu.SMEM)] + [whole(a) for a in pieces],
            out_specs=whole(shape),
            out_shape=shape,
            compiler_params=pltpu.CompilerParams(vmem_limit_bytes=40 * MIB),
            name="place",
        )(place, *pieces).reshape(-1, columns)


    def block(self, grad, got, dp, side, columns):
        dps, lines, sides, _ = self.sizes
        parts = grad.reshape(*self.sizes, -1, grad.shape[1])
        unit, (first, last) = parts.shape[4], columns
        start = (0 if dp is None else dp, 0, 0 if side is None else side)
        size = (dps if dp is None else 1, lines, sides if side is None else 1)
        mine = lax.dynamic_slice(parts, (*start, self.core, 0, first), (*size, 1, unit, last - first))
        other = lax.dynamic_slice(got, (*start, 0, first), (*size, unit, last - first))
        return mine[:, :, :, 0].astype(F32) + other.astype(F32)

    def halves(self, grad):
        columns = grad.shape[1]
        middle = -(-columns // (2 * PAIR)) * PAIR
        return (0, middle), (middle, columns)

    def core_message(self, grad):
        parts = grad.reshape(*self.sizes, -1, grad.shape[1])
        return lax.dynamic_index_in_dim(parts, 1 - self.core, 3, keepdims=False)

    def first_messages(self, grad, got):
        one, two = self.halves(grad)
        return (
            self.block(grad, got, None, 1 - self.side, one).astype(LOW),
            self.block(grad, got, 1 - self.dp, None, two).astype(LOW),
        )

    def first_exchange(self, messages):
        return self.to_plane(messages[0], (0, 1)), self.to_plane(messages[1], (1, 0))

    def second_messages(self, grad, got, more):
        one, two = self.halves(grad)
        a = self.block(grad, got, 1 - self.dp, self.side, one)
        b = self.block(grad, got, self.dp, 1 - self.side, two)
        a += lax.dynamic_slice_in_dim(more[0], 1 - self.dp, 1, 0).astype(F32)
        b += lax.dynamic_slice_in_dim(more[1], 1 - self.side, 1, 2).astype(F32)
        return a.astype(LOW), b.astype(LOW)

    def second_exchange(self, messages):
        return self.to_plane(messages[0], (1, 0)), self.to_plane(messages[1], (0, 1))

    def line_messages(self, grad, got, more, most):
        one, two = self.halves(grad)
        a = self.block(grad, got, self.dp, self.side, one) + most[0].astype(F32)
        b = self.block(grad, got, self.dp, self.side, two) + most[1].astype(F32)
        a += lax.dynamic_slice_in_dim(more[0], self.dp, 1, 0).astype(F32)
        b += lax.dynamic_slice_in_dim(more[1], self.side, 1, 2).astype(F32)
        total = jnp.concatenate([a[0, :, 0], b[0, :, 0]], axis=2).astype(LOW)
        lines = self.sizes[1]
        at = [lax.rem(self.line + s, lines) for s in range(lines)]
        return [lax.dynamic_index_in_dim(total, i, 0, keepdims=False) for i in at]

    def line_exchange(self, messages):
        return messages[:1] + [self.to_line(m, s) for s, m in enumerate(messages) if s]


def finish_kernel(count, *refs):
    parts, (wout_ref, wq_ref, wk_ref, wv_ref), vectors = refs[:count], refs[count : count + 4], refs[count + 4 :]
    total = sum(ref[...].astype(F32) for ref in parts)
    wout_ref[...] = total[:, :D]
    for g in range(GROUPS):
        for part, ref in enumerate((wq_ref, wk_ref, wv_ref)):
            at = D + g * TRIO + part * GROUP
            ref[:, g * GROUP : (g + 1) * GROUP] = total[:, at : at + GROUP]
    for i, ref in enumerate(vectors):
        ref[...] = total[i : i + 1, 4 * D : 4 * D + ref.shape[1]]


def finish(parts):
    unit = parts[0].shape[0]
    shapes = [like((unit, D), F32)] * 4 + [like((1, unit), F32)] * 8 + [like((1, CHUNKS * unit), F32)]
    outs = pl.pallas_call(
        lambda *refs: finish_kernel(len(parts), *refs),
        in_specs=[whole(a) for a in parts],
        out_specs=[whole(a) for a in shapes],
        out_shape=shapes,
        name="finish",
    )(*parts)
    return outs[:4], [v.reshape(-1) for v in outs[4:]]


def vector_rows(table, b_inner, count):
    unit = D // count
    eight = table.reshape(8, count, unit).transpose(1, 0, 2)
    inner = b_inner.reshape(count, 1, CHUNKS * unit)
    eight = jnp.pad(eight, ((0, 0), (0, 0), (0, PAIR - unit)))
    inner = jnp.pad(inner, ((0, 0), (0, unit - 9), (0, PAIR - CHUNKS * unit)))
    return jnp.concatenate([eight, inner], axis=1).reshape(D, PAIR).astype(LOW)


def on_device(block_input, segment_ids, cotangent, *params):
    w_query, w_key, w_value, w_out, w_inner, w_outer = (params[i] for i in MATRICES)
    vectors = [params[i] for i in VECTORS]
    unit = w_query.shape[0]
    count = D // unit
    mesh = Slice()
    quick = mesh.sizes[0] == 2 and unit % 8 == 0 and unit > 8 and CHUNKS * unit <= PAIR
    x = block_input.reshape(-1, D)
    cot = cotangent.reshape(-1, D)

    if quick:
        mine, rest_mine = pack(w_query, w_key, w_value, w_out, w_inner, w_outer, vectors)
        rest = lax.all_gather(rest_mine, AXES, axis=0, tiled=True)
        w_qkv = mesh.gather(mine)
        side = w_qkv[:, 3 * D :].reshape(count, unit, PAIR)
        table = side[:, :8, :unit].transpose(1, 0, 2).reshape(8, D).astype(F32)
        b_inner = side[:, 8, : CHUNKS * unit].reshape(1, FF).astype(F32)
    else:
        trios = [w[:, g : g + GROUP] for g in range(0, D, GROUP) for w in (w_query, w_key, w_value)]
        full = lax.all_gather(jnp.concatenate([*trios, w_inner, w_out], axis=1), AXES, axis=0, tiled=True)
        outer = lax.all_gather(w_outer, AXES, axis=0, tiled=True)
        vector = lax.all_gather(jnp.concatenate(vectors), AXES, axis=0).astype(F32)
        w_qkv = full[:, : 3 * D]
        table = jnp.concatenate([vector[:, i * unit : (i + 1) * unit].reshape(1, D) for i in range(8)])
        b_inner = vector[:, 8 * unit :].reshape(1, FF)
        unit = 24
        outer = outer.reshape(-1, CHUNKS, unit, D).transpose(0, 2, 1, 3).reshape(D, FF)
        rest = jnp.concatenate([outer, full[:, 3 * D :]], axis=1)

    qkv, ctx, lse, xt = attention_forward(x, segment_ids, w_qkv, table)
    result, h1, n1, act, slope, db, dh2, sums = ffn_forward(unit, x, ctx, cot, rest, b_inner, table)
    g_outer = outer_grad(act, db)
    if quick:
        db = after(db, g_outer)
        g_outer = lax.psum_scatter(g_outer, AXES, scatter_dimension=0, tiled=True)
    g_inner, g_b_inner, dn1 = ffn_backward(unit, n1, slope, db, dh2, rest)
    fixed = (segment_ids, xt, qkv, ctx)
    back = attention_backward
    if not quick:
        late, dctx, dh1, sums = norm_backward(h1, dn1, ctx, rest, table, sums)
        late, dqkv, sums = back(0, *fixed, dctx, lse, sums, late)
        for g in range(1, GROUPS):
            late, dqkv, sums = back(g, *fixed, dctx, lse, sums, late, dqkv)
        dx = input_grad(dh1, dqkv, w_qkv)
        wide = jnp.concatenate([late[:, : 4 * D], g_inner], axis=1)
        wide = lax.psum_scatter(wide, AXES, scatter_dimension=0, tiled=True).astype(F32)
        g_outer = lax.psum_scatter(g_outer, AXES, scatter_dimension=0, tiled=True).astype(F32)
        vector = jnp.concatenate([*sums.reshape(8, count, -1), g_b_inner.reshape(count, -1)], axis=1)
        vector = lax.psum_scatter(vector.reshape(-1), AXES, scatter_dimension=0, tiled=True)
        size = D // count
        vectors = [vector[i * size : (i + 1) * size] for i in range(8)] + [vector[8 * size :]]
        matrices = [wide[:, :D]] + [
            jnp.concatenate([wide[:, g + part : g + part + GROUP] for g in range(D, 4 * D, TRIO)], axis=1)
            for part in range(0, TRIO, GROUP)
        ]
        g_inner = wide[:, 4 * D :]
    else:
        message = mesh.core_message(g_inner)
        dn1 = after(dn1, message)
        got = mesh.to_core(message)
        late, dctx, dh1, sums = norm_backward(h1, dn1, ctx, rest, table, sums)
        got, lse = after((got, lse), dctx)
        message = mesh.first_messages(g_inner, got)
        lse = after(lse, message)
        more = mesh.first_exchange(message)
        late, dqkv, sums = back(0, *fixed, dctx, lse, sums, late)
        more, lse = after((more, lse), dqkv)
        message = mesh.second_messages(g_inner, got, more)
        lse = after(lse, message)
        most = mesh.second_exchange(message)
        late, dqkv, sums = back(1, *fixed, dctx, lse, sums, late, dqkv)
        most, lse = after((most, lse), dqkv)
        message = mesh.line_messages(g_inner, got, more, most)
        lse = after(lse, message)
        lines = mesh.line_exchange(message)
        late, dqkv, sums = back(2, *fixed, dctx, lse, sums, late, dqkv)
        late, lines = after((late, lines), dqkv)
        late = lax.dynamic_update_slice(late, vector_rows(sums, g_b_inner, count), (0, 4 * D))
        message = mesh.core_message(late)
        dqkv = after(dqkv, message)
        g_inner = sum(p.astype(F32) for p in lines)
        got = mesh.to_core(message)
        more = mesh.first_exchange(mesh.first_messages(late, got))
        most = mesh.second_exchange(mesh.second_messages(late, got, more))
        dx = input_grad(dh1, dqkv, w_qkv)
        matrices, vectors = finish(mesh.line_exchange(mesh.line_messages(late, got, more, most)))
        g_outer = g_outer.astype(F32)
    g_out, *matrices = matrices

    shards = [None] * len(params)
    for i, value in zip(MATRICES, (*matrices, g_out, g_inner, g_outer)):
        shards[i] = value
    for i, value in zip(VECTORS, vectors):
        shards[i] = value
    return (result.reshape(block_input.shape), dx.reshape(block_input.shape), *shards)


def solution(mesh):
    sizes = (mesh.shape["dp"], mesh.shape["fsdp"] // 4, 2, 2)
    parts = Mesh(np.asarray(mesh.devices).reshape(sizes), AXES)
    vector, matrix, rows = P(AXES), P(AXES, None), P(AXES, None, None)
    params = tuple(vector if i in VECTORS else matrix for i in range(15))
    return jax.shard_map(
        on_device,
        mesh=parts,
        in_specs=(rows, matrix, rows) + params,
        out_specs=(rows, rows) + params,
        check_vma=False,
    )
```

```python
import jax
import jax.numpy as jnp
import numpy as np
from jax import lax
from jax.experimental import pallas as pl
from jax.experimental.pallas import tpu as pltpu
from jax.sharding import Mesh, PartitionSpec as P

D = 768
FF = 3072
HEADS = 12
HEAD_DIM = 64
SEQ = 512
GROUP = 256
GROUPS = D // GROUP
TRIO = 3 * GROUP
PAIR = 128
SET = 4 * D + PAIR
KT = 256
CHUNK = 768
CHUNKS = FF // CHUNK
ROWS = 256
EPS = 1e-05
SHARE = 1.0
ROOT = 0.7978845608028654
CUBE = 0.044715
LOW = jnp.bfloat16
F32 = jnp.float32
MIB = 1 << 20
VMEM = 63 * MIB
MATRICES = (0, 2, 3, 5, 9, 11)
VECTORS = (1, 4, 6, 7, 8, 12, 13, 14, 10)
AXES = ("dp", "line", "side", "core")


def mm(a, b):
    return lax.dot_general(a, b, (((1,), (0,)), ((), ())), preferred_element_type=F32)


def mm_t(a, b):
    return lax.dot_general(a, b, (((1,), (1,)), ((), ())), preferred_element_type=F32)


def t_mm(a, b):
    return lax.dot_general(a, b, (((0,), (0,)), ((), ())), preferred_element_type=F32)


def cost(flops, moved, transcendentals):
    return pl.CostEstimate(
        flops=int(SHARE * flops),
        bytes_accessed=int(SHARE * moved),
        transcendentals=int(SHARE * transcendentals),
    )


def like(shape, kind):
    return jax.ShapeDtypeStruct(shape, kind)


def attention_forward_kernel(
    x_ref, w_ref, wout_ref, vec_ref, seg_ref,
    qkv_ref, ctx_ref, probs_ref, xt_ref, h1_ref, n1_ref, n1low_ref, n1t_ref, mask_ref,
):
    group = pl.program_id(1)
    x = x_ref[...]
    column = pl.ds(pl.multiple_of(group * GROUP, GROUP), GROUP)
    qkv_ref[:, :GROUP] = (mm(x, w_ref[:, :GROUP]) + vec_ref[0:1, column]).astype(LOW)
    qkv_ref[:, GROUP : 2 * GROUP] = mm(x, w_ref[:, GROUP : 2 * GROUP]).astype(LOW)
    qkv_ref[:, 2 * GROUP :] = (mm(x, w_ref[:, 2 * GROUP :]) + vec_ref[1:2, column]).astype(LOW)

    @pl.when(group == 0)
    def _():
        number = seg_ref[pl.ds(pl.program_id(0), 1), :].astype(F32)
        column = jnp.transpose(jnp.broadcast_to(number, (PAIR, SEQ)))[:, :1]
        mask_ref[...] = jnp.where(column == number, 0.0, -1e30)
        xt_ref[0] = jnp.transpose(x)
        h1_ref[...] = x.astype(F32) + vec_ref[2:3, :]

    lane = lax.broadcasted_iota(jnp.int32, (1, PAIR), 1)
    scale = jnp.asarray(HEAD_DIM**-0.5, LOW)
    for pair in range(GROUP // PAIR):
        q_lanes, k_lanes, v_lanes = (
            slice(part * GROUP + pair * PAIR, part * GROUP + (pair + 1) * PAIR) for part in range(3)
        )
        q_pair = qkv_ref[:, q_lanes] * scale
        v_pair = qkv_ref[:, v_lanes]
        halves = []
        for half in range(2):
            mine = (lane // HEAD_DIM) == half
            scores = mm_t(jnp.where(mine, qkv_ref[:, k_lanes], 0), q_pair) + mask_ref[...]
            weight = jnp.exp(scores - jnp.max(scores, axis=0, keepdims=True))
            total = jnp.sum(weight, axis=0, keepdims=True)
            probs = (weight * (1.0 / total)).astype(LOW)
            probs_ref[0, 0, 2 * pair + half] = probs
            halves.append(t_mm(probs, v_pair))
        ctx_ref[:, q_lanes] = jnp.where(lane < HEAD_DIM, halves[0], halves[1]).astype(LOW)
    h1_ref[...] += mm(ctx_ref[...], wout_ref[...])

    @pl.when(group == GROUPS - 1)
    def _():
        @pl.loop(0, SEQ // ROWS)
        def _(i):
            rows = pl.ds(pl.multiple_of(i * ROWS, ROWS), ROWS)
            n, _ = norm_parts(h1_ref[rows, :])
            n1 = n * vec_ref[3:4, :] + vec_ref[4:5, :]
            n1_ref[rows, :] = n1
            n1low_ref[rows, :] = n1.astype(LOW)

        n1t_ref[...] = jnp.transpose(n1low_ref[...])


def attention_forward(x, seg, weights, table):
    rows = x.shape[0]
    seqs = rows // SEQ
    row = pl.BlockSpec((SEQ, D), lambda b, g: (b, 0))
    return pl.pallas_call(
        attention_forward_kernel,
        grid=(seqs, GROUPS),
        in_specs=[
            row,
            pl.BlockSpec((D, TRIO), lambda b, g: (0, 1 + g)),
            pl.BlockSpec((GROUP, D), lambda b, g: (g, 0)),
            pl.BlockSpec((8, D), lambda b, g: (0, 0)),
            pl.BlockSpec((seqs, SEQ), lambda b, g: (0, 0)),
        ],
        out_specs=[
            pl.BlockSpec((SEQ, TRIO), lambda b, g: (b, g)),
            pl.BlockSpec((SEQ, GROUP), lambda b, g: (b, g)),
            pl.BlockSpec((1, 1, GROUP // HEAD_DIM, SEQ, SEQ), lambda b, g: (b, g, 0, 0, 0)),
            pl.BlockSpec((1, D, SEQ), lambda b, g: (b, 0, 0)),
            row,
            row,
            row,
            pl.BlockSpec((D, SEQ), lambda b, g: (0, b)),
        ],
        out_shape=[
            like((rows, 3 * D), LOW),
            like((rows, D), LOW),
            like((seqs, GROUPS, GROUP // HEAD_DIM, SEQ, SEQ), LOW),
            like((seqs, D, SEQ), LOW),
            like((rows, D), F32),
            like((rows, D), F32),
            like((rows, D), LOW),
            like((D, rows), LOW),
        ],
        scratch_shapes=[pltpu.VMEM((SEQ, SEQ), F32)],
        compiler_params=pltpu.CompilerParams(vmem_limit_bytes=VMEM),
        cost_estimate=cost(rows * (8 * D * D + 4 * D * SEQ), 36 * MIB, rows * SEQ * HEADS),
        name="attention_forward",
    )(x, weights, weights, table, seg)


def attention_backward_kernel(
    xt_ref, qkv_ref, ctx_ref, dctx_ref, probs_ref, vec_in_ref, gw_in_ref,
    gw_ref, dqkv_ref, vec_ref,
    ds_ref, acc_ref,
):
    row, seqs = pl.program_id(1), pl.num_programs(1)
    head_of = lax.broadcasted_iota(jnp.int32, (8, GROUP), 1) // HEAD_DIM
    picks = (head_of == lax.broadcasted_iota(jnp.int32, (8, GROUP), 0)).astype(F32)
    product = ctx_ref[...].astype(F32) * dctx_ref[...].astype(F32)
    inner = lax.dot_general(
        picks, product, (((1,), (1,)), ((), ())),
        preferred_element_type=F32, precision=lax.Precision.HIGHEST,
    )
    lane = lax.broadcasted_iota(jnp.int32, (1, PAIR), 1)
    first = lane < HEAD_DIM
    scale = jnp.asarray(HEAD_DIM**-0.5, LOW)
    tiles = [slice(i, i + KT) for i in range(0, SEQ, KT)]
    for pair in range(GROUP // PAIR):
        q_lanes, k_lanes, v_lanes = (
            slice(part * GROUP + pair * PAIR, part * GROUP + (pair + 1) * PAIR) for part in range(3)
        )
        q_pair = qkv_ref[:, q_lanes] * scale
        k_pair = qkv_ref[:, k_lanes] * scale
        dctx_pair = dctx_ref[:, q_lanes]
        dq, dk, dv = [], [], []
        for half in range(2):
            mine = (lane // HEAD_DIM) == half
            head = 2 * pair + half
            dk_tiles, dv_tiles = [], []
            for keys in tiles:
                probs = probs_ref[0, 0, head, keys, :]
                d_probs = mm_t(jnp.where(mine, qkv_ref[keys, v_lanes], 0), dctx_pair)
                d_scores = (probs.astype(F32) * (d_probs - inner[head : head + 1, :])).astype(LOW)
                ds_ref[half, keys, :] = d_scores
                dv_tiles.append(mm(probs, dctx_pair))
                dk_tiles.append(mm(d_scores, q_pair))
            dk.append(dk_tiles)
            dv.append(dv_tiles)
            dq.append([t_mm(ds_ref[half, :, rows], k_pair) for rows in tiles])
        for i, rows in enumerate(tiles):
            dqkv_ref[rows, q_lanes] = jnp.where(first, dq[0][i], dq[1][i]).astype(LOW)
            dqkv_ref[rows, k_lanes] = jnp.where(first, dk[0][i], dk[1][i]).astype(LOW)
            dqkv_ref[rows, v_lanes] = jnp.where(first, dv[0][i], dv[1][i]).astype(LOW)
    dqkv = dqkv_ref[...]
    product = mm(xt_ref[0], dqkv)
    bias_q = column_sum(dqkv[:, :GROUP].astype(F32))
    bias_v = column_sum(dqkv[:, 2 * GROUP :].astype(F32))

    @pl.when(row == 0)
    def _():
        acc_ref[...] = product
        vec_ref[...] = vec_in_ref[...]
        vec_ref[0:1, :] = bias_q
        vec_ref[1:2, :] = bias_v

    @pl.when(row > 0)
    def _():
        acc_ref[...] += product
        vec_ref[0:1, :] += bias_q
        vec_ref[1:2, :] += bias_v

    @pl.when(row == seqs - 1)
    def _():
        gw_ref[...] = acc_ref[...].astype(LOW)


def attention_backward(xt, qkv, ctx, probs, dctx, table, gw):
    rows = ctx.shape[0]
    seqs = rows // SEQ
    mine = lambda g, b: (b, g)
    return pl.pallas_call(
        attention_backward_kernel,
        grid=(GROUPS, seqs),
        in_specs=[
            pl.BlockSpec((1, D, SEQ), lambda g, b: (b, 0, 0)),
            pl.BlockSpec((SEQ, TRIO), mine),
            pl.BlockSpec((SEQ, GROUP), mine),
            pl.BlockSpec((SEQ, GROUP), mine),
            pl.BlockSpec((1, 1, GROUP // HEAD_DIM, SEQ, SEQ), lambda g, b: (b, g, 0, 0, 0)),
            pl.BlockSpec((8, GROUP), lambda g, b: (0, g)),
            pl.BlockSpec(memory_space=pl.ANY),
        ],
        out_specs=[
            pl.BlockSpec((D, TRIO), lambda g, b: (0, 1 + g)),
            pl.BlockSpec((SEQ, TRIO), mine),
            pl.BlockSpec((8, GROUP), lambda g, b: (0, g)),
        ],
        out_shape=[like((D, SET), LOW), like((rows, 3 * D), LOW), like((8, D), F32)],
        input_output_aliases={5: 2, 6: 0},
        scratch_shapes=[pltpu.VMEM((2, SEQ, SEQ), LOW), pltpu.VMEM((D, TRIO), F32)],
        compiler_params=pltpu.CompilerParams(vmem_limit_bytes=VMEM),
        cost_estimate=cost(rows * (6 * D * D + 8 * D * SEQ), 36 * MIB, 0),
        name="attention_backward",
    )(xt, qkv, ctx, dctx, probs, table, gw)


def input_grad_kernel(dh1_ref, dqkv_ref, *refs):
    total = dh1_ref[...]
    for g in range(GROUPS):
        total += mm_t(dqkv_ref[:, g * TRIO : (g + 1) * TRIO], refs[g][...])
    refs[GROUPS][...] = total.astype(LOW)


def input_grad(dh1, dqkv, weights):
    rows = dh1.shape[0]
    return pl.pallas_call(
        input_grad_kernel,
        grid=(rows // ROWS,),
        in_specs=[
            pl.BlockSpec((ROWS, D), lambda i: (i, 0)),
            pl.BlockSpec((ROWS, 3 * D), lambda i: (i, 0)),
            *(pl.BlockSpec((D, TRIO), lambda i, g=g: (0, 1 + g)) for g in range(GROUPS)),
        ],
        out_specs=pl.BlockSpec((ROWS, D), lambda i: (i, 0)),
        out_shape=like((rows, D), LOW),
        compiler_params=pltpu.CompilerParams(vmem_limit_bytes=VMEM),
        cost_estimate=cost(6 * rows * D * D, 13 * MIB, 0),
        name="input_grad",
    )(dh1, dqkv, *[weights] * GROUPS)


def norm_parts(hidden):
    mean = jnp.mean(hidden, axis=1, keepdims=True)
    centred = hidden - mean
    inverse = lax.rsqrt(jnp.mean(centred * centred, axis=1, keepdims=True) + EPS)
    return centred * inverse, inverse


def norm_back(grad, gain, normed, inverse):
    scaled = grad * gain
    mean = jnp.mean(scaled, axis=1, keepdims=True)
    along = jnp.mean(scaled * normed, axis=1, keepdims=True)
    return inverse * (scaled - mean - normed * along)


def column_sum(array):
    return jnp.sum(array, axis=0, keepdims=True)


def gelu_and_slope(v):
    square = v * v
    bent = jnp.tanh(v * (ROOT + ROOT * CUBE * square))
    half = 0.5 + 0.5 * bent
    act = v * half
    slope = half + act * (1.0 - half) * (2.0 * ROOT + 6.0 * ROOT * CUBE * square)
    return act, slope


def order_outer(block_ref, out_ref, unit):
    for o in range(block_ref.shape[0] // unit):
        for j in range(CHUNKS):
            to = (o * CHUNKS + j) * unit
            out_ref[to : to + unit, :] = block_ref[o * unit : (o + 1) * unit, j * D : (j + 1) * D]


def ffn_forward_kernel(
    unit, n1low_ref, outer_ref, wi_ref, bi_ref, vec_ref, n1_hbm, cot_hbm,
    slope_ref, gwo_ref, sums_ref, out_hbm, db_hbm, dh2_hbm,
    n1_ref, cot_ref, h2_ref, wo_ref, act_ref, out_ref, db_ref, dh2_ref, sem,
):
    step = pl.program_id(0)
    tiles = [slice(i, i + ROWS) for i in range(0, h2_ref.shape[0], ROWS)]
    loads = [
        pltpu.make_async_copy(n1_hbm, n1_ref, sem.at[0]),
        pltpu.make_async_copy(cot_hbm, cot_ref, sem.at[1]),
    ]
    stores = [
        pltpu.make_async_copy(out_ref, out_hbm, sem.at[2]),
        pltpu.make_async_copy(db_ref, db_hbm, sem.at[3]),
        pltpu.make_async_copy(dh2_ref, dh2_hbm, sem.at[4]),
    ]

    @pl.when(step == 0)
    def _():
        for copy in loads:
            copy.start()
        h2_ref[...] = jnp.zeros_like(h2_ref)

    @pl.when(step < CHUNKS)
    def _():
        order_outer(outer_ref, wo_ref, unit)
        for rows in tiles:
            pre = mm(n1low_ref[rows, :], wi_ref[...]) + bi_ref[...]
            act, slope = gelu_and_slope(pre)
            act = act.astype(LOW)
            act_ref[step, rows, :] = act
            slope_ref[rows, :] = slope.astype(LOW)
            h2_ref[rows, :] += mm(act, wo_ref[...])

    @pl.when(step == CHUNKS - 1)
    def _():
        for copy in loads:
            copy.wait()
        gain, shift = vec_ref[6:7, :], vec_ref[7:8, :]
        sums_ref[...] = jnp.zeros_like(sums_ref)

        @pl.loop(0, h2_ref.shape[0] // ROWS, unroll=2)
        def _(i):
            rows = pl.ds(pl.multiple_of(i * ROWS, ROWS), ROWS)
            n, inverse = norm_parts(h2_ref[rows, :] + (n1_ref[rows, :] + vec_ref[5:6, :]))
            out_ref[rows, :] = (n * gain + shift).astype(LOW)
            cot = cot_ref[rows, :].astype(F32)
            dh2 = norm_back(cot, gain, n, inverse)
            dh2_ref[rows, :] = dh2
            db = dh2.astype(LOW)
            db_ref[rows, :] = db
            for j, new in enumerate((column_sum(db.astype(F32)), column_sum(cot * n), column_sum(cot))):
                sums_ref[5 + j : 6 + j, :] += new

        for copy in stores:
            copy.start()

    @pl.when(step >= CHUNKS)
    def _():
        grad = t_mm(act_ref[step - CHUNKS], db_ref[...]).astype(LOW)
        if len(gwo_ref.shape) == 2:
            gwo_ref[...] = grad
        else:
            _, _, sides, lines, deep, _ = gwo_ref.shape
            for i in range(CHUNK // deep):
                core, side, line = i % 2, i // 2 % sides, i // 2 // sides
                gwo_ref[core, 0, side, line] = grad[i * deep : (i + 1) * deep, :]

    @pl.when(step == 2 * CHUNKS - 1)
    def _():
        for copy in stores:
            copy.wait()


def ffn_forward(unit, n1, n1low, cot, rest, b_inner, table, sizes=None):
    rows = n1.shape[0]
    last = CHUNKS - 1
    now = lambda c: jnp.minimum(c, last)
    then = lambda c: jnp.maximum(c - CHUNKS, 0)
    eight = pl.BlockSpec((8, D), lambda c: (0, 0))
    if sizes is None:
        outer_shape = (FF, D)
        outer_block = pl.BlockSpec((CHUNK, D), lambda c: (then(c), 0))
    else:
        dps, lines, sides, cores = sizes
        deep = CHUNKS * unit
        held = CHUNK // (deep * sides * cores)
        outer_shape = (cores, dps, sides, lines, deep, D)
        outer_block = pl.BlockSpec(
            (cores, 1, sides, held, deep, D),
            lambda c: (0, then(c) * held // lines, 0, then(c) % (lines // held), 0, 0),
        )
    anywhere = pl.BlockSpec(memory_space=pl.ANY)
    return pl.pallas_call(
        lambda *refs: ffn_forward_kernel(unit, *refs),
        grid=(2 * CHUNKS,),
        in_specs=[
            pl.BlockSpec((rows, D), lambda c: (0, 0), pipeline_mode=pl.Buffered(1)),
            pl.BlockSpec((D // CHUNKS, FF), lambda c: (now(c), 0)),
            pl.BlockSpec((D, CHUNK), lambda c: (0, CHUNKS + now(c))),
            pl.BlockSpec((1, CHUNK), lambda c: (0, now(c))),
            eight,
            anywhere,
            anywhere,
        ],
        out_specs=[
            pl.BlockSpec((rows, CHUNK), lambda c: (0, now(c))),
            outer_block,
            eight,
            anywhere,
            anywhere,
            anywhere,
        ],
        out_shape=[
            like((rows, FF), LOW),
            like(outer_shape, LOW),
            like((8, D), F32),
            like((rows, D), LOW),
            like((rows, D), LOW),
            like((rows, D), F32),
        ],
        scratch_shapes=[
            pltpu.VMEM((rows, D), F32),
            pltpu.VMEM((rows, D), LOW),
            pltpu.VMEM((rows, D), F32),
            pltpu.VMEM((CHUNK, D), LOW),
            pltpu.VMEM((CHUNKS, rows, CHUNK), LOW),
            pltpu.VMEM((rows, D), LOW),
            pltpu.VMEM((rows, D), LOW),
            pltpu.VMEM((rows, D), F32),
            pltpu.SemaphoreType.DMA((5,)),
        ],
        compiler_params=pltpu.CompilerParams(vmem_limit_bytes=VMEM),
        cost_estimate=cost(6 * rows * D * FF, 34 * MIB, rows * FF),
        name="ffn_forward",
    )(n1low, rest, rest, b_inner, table, n1, cot)


def ffn_backward_kernel(
    unit, n1t_ref, slope_ref, db_ref, outer_ref, wi_ref,
    gwi_ref, gbi_ref, dn1_ref,
    dpre_ref, wo_ref,
):
    step = pl.program_id(0)
    tiles = [slice(i, i + ROWS) for i in range(0, db_ref.shape[0], ROWS)]
    order_outer(outer_ref, wo_ref, unit)

    @pl.when(step == 0)
    def _():
        dn1_ref[...] = jnp.zeros_like(dn1_ref)

    bias = jnp.zeros((1, CHUNK), F32)
    for rows in tiles:
        dpre = (mm_t(db_ref[rows, :], wo_ref[...]) * slope_ref[rows, :].astype(F32)).astype(LOW)
        dpre_ref[rows, :] = dpre
        bias += column_sum(dpre.astype(F32))
        dn1_ref[rows, :] += mm_t(dpre, wi_ref[...])
    gbi_ref[...] = bias
    gwi_ref[...] = mm(n1t_ref[...], dpre_ref[...]).astype(LOW)


def ffn_backward(unit, n1t, slope, db, rest):
    rows = db.shape[0]
    once = pl.BlockSpec((rows, D), lambda c: (0, 0), pipeline_mode=pl.Buffered(1))
    return pl.pallas_call(
        lambda *refs: ffn_backward_kernel(unit, *refs),
        grid=(CHUNKS,),
        in_specs=[
            pl.BlockSpec((D, rows), lambda c: (0, 0), pipeline_mode=pl.Buffered(1)),
            pl.BlockSpec((rows, CHUNK), lambda c: (0, c)),
            once,
            pl.BlockSpec((D // CHUNKS, FF), lambda c: (c, 0)),
            pl.BlockSpec((D, CHUNK), lambda c: (0, CHUNKS + c)),
        ],
        out_specs=[
            pl.BlockSpec((D, CHUNK), lambda c: (0, c)),
            pl.BlockSpec((1, CHUNK), lambda c: (0, c)),
            pl.BlockSpec((rows, D), lambda c: (0, 0)),
        ],
        out_shape=[like((D, FF), LOW), like((1, FF), F32), like((rows, D), F32)],
        scratch_shapes=[pltpu.VMEM((rows, CHUNK), LOW), pltpu.VMEM((CHUNK, D), LOW)],
        compiler_params=pltpu.CompilerParams(vmem_limit_bytes=VMEM),
        cost_estimate=cost(6 * rows * D * FF, 30 * MIB, 0),
        name="ffn_backward",
    )(n1t, slope, db, rest, rest)


def norm_backward_kernel(
    wout_ref, vec_ref, sums_in_ref, h1_hbm, dn1_hbm, dh2_hbm, ctx_hbm,
    gw_ref, sums_ref, dctx_hbm, dh1_hbm,
    h1_ref, dn1_ref, dh2_ref, ctx_ref, da_ref, dctx_ref, dh1_ref, load_sem, store_sem,
):
    tiles = [slice(i, i + ROWS) for i in range(0, h1_ref.shape[0], ROWS)]
    pairs = ((h1_hbm, h1_ref), (dn1_hbm, dn1_ref), (dh2_hbm, dh2_ref), (ctx_hbm, ctx_ref))
    loads = [
        [pltpu.make_async_copy(a.at[rows, :], b.at[rows, :], load_sem.at[i, j]) for j, (a, b) in enumerate(pairs)]
        for i, rows in enumerate(tiles)
    ]
    stores = [
        [
            pltpu.make_async_copy(dh1_ref.at[rows, :], dh1_hbm.at[rows, :], store_sem.at[i, 0]),
            pltpu.make_async_copy(dctx_ref.at[rows, :], dctx_hbm.at[rows, :], store_sem.at[i, 1]),
        ]
        for i, rows in enumerate(tiles)
    ]
    for group in loads:
        for copy in group:
            copy.start()
    sums = [jnp.zeros((1, D), F32)] * 3
    for i, rows in enumerate([*tiles, None]):
        if rows is not None:
            for copy in loads[i]:
                copy.wait()
        if i > 0:
            dctx_ref[tiles[i - 1], :] = mm_t(da_ref[tiles[i - 1], :], wout_ref[...]).astype(LOW)
        if rows is not None:
            n, inverse = norm_parts(h1_ref[rows, :])
            dn1 = dn1_ref[rows, :] + dh2_ref[rows, :]
            dh1 = norm_back(dn1, vec_ref[3:4, :], n, inverse)
            dh1_ref[rows, :] = dh1
            da = dh1.astype(LOW)
            da_ref[rows, :] = da
            new = (column_sum(da.astype(F32)), column_sum(dn1 * n), column_sum(dn1))
            sums = [a + b for a, b in zip(sums, new)]
            stores[i][0].start()
        if i > 0:
            stores[i - 1][1].start()
    gw_ref[...] = t_mm(ctx_ref[...], da_ref[...]).astype(LOW)
    sums_ref[...] = sums_in_ref[...]
    for i in range(3):
        sums_ref[2 + i : 3 + i, :] = sums[i]
    for group in stores:
        for copy in group:
            copy.wait()


def norm_backward(h1, dn1, dh2, ctx, weights, table, sums):
    rows = h1.shape[0]
    eight = pl.BlockSpec((8, D), lambda i: (0, 0))
    square = pl.BlockSpec((D, D), lambda i: (0, 0))
    anywhere = pl.BlockSpec(memory_space=pl.ANY)
    return pl.pallas_call(
        norm_backward_kernel,
        grid=(1,),
        in_specs=[square, eight, eight] + [anywhere] * 4,
        out_specs=[square, eight, anywhere, anywhere],
        out_shape=[like((D, SET), LOW), like((8, D), F32), like((rows, D), LOW), like((rows, D), F32)],
        scratch_shapes=[
            pltpu.VMEM((rows, D), F32),
            pltpu.VMEM((rows, D), F32),
            pltpu.VMEM((rows, D), F32),
            pltpu.VMEM((rows, D), LOW),
            pltpu.VMEM((rows, D), LOW),
            pltpu.VMEM((rows, D), LOW),
            pltpu.VMEM((rows, D), F32),
            pltpu.SemaphoreType.DMA((rows // ROWS, 4)),
            pltpu.SemaphoreType.DMA((rows // ROWS, 2)),
        ],
        compiler_params=pltpu.CompilerParams(vmem_limit_bytes=VMEM),
        cost_estimate=cost(4 * rows * D * D, 17 * MIB, 0),
        name="norm_backward",
    )(weights, table, sums, h1, dn1, dh2, ctx)


def after(values, *others):
    return lax.optimization_barrier((values, others))[0]


def whole(array):
    return pl.BlockSpec(array.shape, lambda *_: (0,) * len(array.shape))


def pack_kernel(wq_ref, wk_ref, wv_ref, wout_ref, wi_ref, wo_ref, *refs):
    vectors, (set_ref, rest_ref) = refs[:9], refs[9:]
    unit = wq_ref.shape[0]
    set_ref[:, :D] = wout_ref[...]
    for g in range(GROUPS):
        for part, ref in enumerate((wq_ref, wk_ref, wv_ref)):
            to = D + g * TRIO + part * GROUP
            set_ref[:, to : to + GROUP] = ref[:, g * GROUP : (g + 1) * GROUP]
    table = jnp.zeros((unit, PAIR), F32)
    row = lax.broadcasted_iota(jnp.int32, (unit, PAIR), 0)
    for i, ref in enumerate(vectors):
        size = ref.shape[1]
        line = jnp.concatenate([ref[...].astype(F32), jnp.zeros((1, PAIR - size), F32)], axis=1)
        table = jnp.where(row == i, line, table)
    set_ref[:, 4 * D :] = table.astype(LOW)
    for j in range(CHUNKS):
        rest_ref[:, j * D : (j + 1) * D] = wo_ref[j * unit : (j + 1) * unit, :]
    rest_ref[:, FF:] = wi_ref[...]


def pack(wq, wk, wv, wout, wi, wo, vectors):
    unit = wq.shape[0]
    args = (wq, wk, wv, wout, wi, wo, *(v.reshape(1, -1) for v in vectors))
    shapes = [like((unit, SET), LOW), like((unit, 2 * FF), LOW)]
    return pl.pallas_call(
        pack_kernel,
        in_specs=[whole(a) for a in args],
        out_specs=[whole(a) for a in shapes],
        out_shape=shapes,
        name="pack",
    )(*args)


def stack_kernel(*refs):
    for i, ref in enumerate(refs[:-1]):
        refs[-1][i] = ref[...]


def stack(pieces):
    shape = like((len(pieces), *pieces[0].shape), pieces[0].dtype)
    return pl.pallas_call(
        stack_kernel,
        in_specs=[whole(a) for a in pieces],
        out_specs=whole(shape),
        out_shape=shape,
        name="stack",
    )(*pieces)


class Slice:
    def __init__(self):
        self.sizes = tuple(lax.axis_size(name) for name in AXES)
        self.dp, self.line, self.side, self.core = (lax.axis_index(name) for name in AXES)
        self.offsets = [(a, b) for a in range(self.sizes[0]) for b in range(self.sizes[2])]

    def to_core(self, array):
        return lax.ppermute(array, "core", [(0, 1), (1, 0)])

    def to_plane(self, array, offset):
        dps, _, sides, _ = self.sizes
        pairs = [
            (i * sides + j, (i + offset[0]) % dps * sides + (j + offset[1]) % sides)
            for i in range(dps)
            for j in range(sides)
        ]
        return lax.ppermute(array, ("dp", "side"), pairs)

    def to_line(self, array, shift):
        count = self.sizes[1]
        return lax.ppermute(array, "line", [(i, (i + shift) % count) for i in range(count)])

    def gather(self, mine):
        dps, lines, sides, _ = self.sizes
        unit, columns = mine.shape
        line = stack([mine] + [self.to_line(mine, s) for s in range(1, lines)])
        here = [line if o == (0, 0) else self.to_plane(line, o) for o in self.offsets]
        there = [self.to_core(a) for a in here]
        place = jnp.stack([self.dp, self.line, self.side, self.core]).astype(jnp.int32)
        pieces = here + there

        def kernel(place_ref, *refs):
            out_ref = refs[-1]
            for i in range(len(pieces)):
                a, b = self.offsets[i % len(here)]
                dp = lax.rem(place_ref[0] + dps - a, dps)
                side = lax.rem(place_ref[2] + sides - b, sides)
                core = place_ref[3] if i < len(here) else 1 - place_ref[3]
                for s in range(lines):
                    along = lax.rem(place_ref[1] + lines - s, lines)
                    out_ref[((dp * lines + along) * sides + side) * 2 + core] = refs[i][s]

        wide = 5 * PAIR
        count = dps * lines * sides * 2
        return pl.pallas_call(
            kernel,
            grid=(columns // wide,),
            in_specs=[pl.BlockSpec(memory_space=pltpu.SMEM)]
            + [pl.BlockSpec((lines, unit, wide), lambda i: (0, 0, i))] * len(pieces),
            out_specs=pl.BlockSpec((count, unit, wide), lambda i: (0, 0, i)),
            out_shape=like((count, unit, columns), mine.dtype),
            compiler_params=pltpu.CompilerParams(vmem_limit_bytes=VMEM),
            name="place",
        )(place, *pieces).reshape(-1, columns)


    def core_sum(self, grad):
        return lax.psum_scatter(grad, "core", scatter_dimension=0)

    def plane_sum(self, grad):
        return lax.psum_scatter(grad.reshape(-1, *grad.shape[2:]), ("dp", "side"), scatter_dimension=0)

    def line_sum(self, grad):
        return lax.psum_scatter(grad, "line", scatter_dimension=0)


    def plane_messages(self, grad, got):
        dps, _, sides, _ = self.sizes
        return [
            self.block(
                grad, got, lax.rem(self.dp + a, dps), lax.rem(self.side + b, sides), (0, grad.shape[1])
            )[0, :, 0].astype(LOW)
            for a, b in self.offsets
        ]

    def plane_exchange(self, messages):
        return messages[:1] + [self.to_plane(m, o) for m, o in zip(messages[1:], self.offsets[1:])]

    def plane_done(self, parts):
        return self.along_line(sum(p.astype(F32) for p in parts).astype(LOW))

    def block(self, grad, got, dp, side, columns):
        dps, lines, sides, _ = self.sizes
        parts = grad.reshape(*self.sizes, -1, grad.shape[1])
        unit, (first, last) = parts.shape[4], columns
        start = (0 if dp is None else dp, 0, 0 if side is None else side)
        size = (dps if dp is None else 1, lines, sides if side is None else 1)
        mine = lax.dynamic_slice(parts, (*start, self.core, 0, first), (*size, 1, unit, last - first))
        other = lax.dynamic_slice(got, (*start, 0, first), (*size, unit, last - first))
        return mine[:, :, :, 0].astype(F32) + other.astype(F32)

    def halves(self, grad):
        columns = grad.shape[1]
        middle = -(-columns // (2 * PAIR)) * PAIR
        return (0, middle), (middle, columns)

    def core_message(self, grad):
        parts = grad.reshape(*self.sizes, -1, grad.shape[1])
        return lax.dynamic_index_in_dim(parts, 1 - self.core, 3, keepdims=False)

    def first_messages(self, grad, got):
        one, two = self.halves(grad)
        return (
            self.block(grad, got, None, 1 - self.side, one).astype(LOW),
            self.block(grad, got, 1 - self.dp, None, two).astype(LOW),
        )

    def first_exchange(self, messages):
        return self.to_plane(messages[0], (0, 1)), self.to_plane(messages[1], (1, 0))

    def second_messages(self, grad, got, more):
        one, two = self.halves(grad)
        a = self.block(grad, got, 1 - self.dp, self.side, one)
        b = self.block(grad, got, self.dp, 1 - self.side, two)
        a += lax.dynamic_slice_in_dim(more[0], 1 - self.dp, 1, 0).astype(F32)
        b += lax.dynamic_slice_in_dim(more[1], 1 - self.side, 1, 2).astype(F32)
        return a.astype(LOW), b.astype(LOW)

    def second_exchange(self, messages):
        return self.to_plane(messages[0], (1, 0)), self.to_plane(messages[1], (0, 1))

    def line_messages(self, grad, got, more, most):
        one, two = self.halves(grad)
        a = self.block(grad, got, self.dp, self.side, one) + most[0].astype(F32)
        b = self.block(grad, got, self.dp, self.side, two) + most[1].astype(F32)
        a += lax.dynamic_slice_in_dim(more[0], self.dp, 1, 0).astype(F32)
        b += lax.dynamic_slice_in_dim(more[1], self.side, 1, 2).astype(F32)
        total = jnp.concatenate([a[0, :, 0], b[0, :, 0]], axis=2).astype(LOW)
        return self.along_line(total)

    def along_line(self, total):
        lines = self.sizes[1]
        at = [lax.rem(self.line + s, lines) for s in range(lines)]
        return [lax.dynamic_index_in_dim(total, i, 0, keepdims=False) for i in at]

    def line_exchange(self, messages):
        return messages[:1] + [self.to_line(m, s) for s, m in enumerate(messages) if s]


def finish_kernel(count, *refs):
    parts, (wout_ref, wq_ref, wk_ref, wv_ref), vectors = refs[:count], refs[count : count + 4], refs[count + 4 :]
    total = sum(ref[...].astype(F32) for ref in parts)
    wout_ref[...] = total[:, :D]
    for g in range(GROUPS):
        for part, ref in enumerate((wq_ref, wk_ref, wv_ref)):
            at = D + g * TRIO + part * GROUP
            ref[:, g * GROUP : (g + 1) * GROUP] = total[:, at : at + GROUP]
    for i, ref in enumerate(vectors):
        ref[...] = total[i : i + 1, 4 * D : 4 * D + ref.shape[1]]


def finish(parts):
    unit = parts[0].shape[0]
    shapes = [like((unit, D), F32)] * 4 + [like((1, unit), F32)] * 8 + [like((1, CHUNKS * unit), F32)]
    outs = pl.pallas_call(
        lambda *refs: finish_kernel(len(parts), *refs),
        in_specs=[whole(a) for a in parts],
        out_specs=[whole(a) for a in shapes],
        out_shape=shapes,
        name="finish",
    )(*parts)
    return outs[:4], [v.reshape(-1) for v in outs[4:]]


def vector_rows(table, b_inner, count):
    unit = D // count
    eight = table.reshape(8, count, unit).transpose(1, 0, 2)
    inner = b_inner.reshape(count, 1, CHUNKS * unit)
    eight = jnp.pad(eight, ((0, 0), (0, 0), (0, PAIR - unit)))
    inner = jnp.pad(inner, ((0, 0), (0, unit - 9), (0, PAIR - CHUNKS * unit)))
    return jnp.concatenate([eight, inner], axis=1).reshape(D, PAIR).astype(LOW)


def on_device(block_input, segment_ids, cotangent, *params):
    w_query, w_key, w_value, w_out, w_inner, w_outer = (params[i] for i in MATRICES)
    vectors = [params[i] for i in VECTORS]
    unit = w_query.shape[0]
    count = D // unit
    mesh = Slice()
    quick = mesh.sizes == (2, 4, 2, 2) and unit == 24
    x = block_input.reshape(-1, D)
    cot = cotangent.reshape(-1, D)

    if quick:
        mine, rest_mine = pack(w_query, w_key, w_value, w_out, w_inner, w_outer, vectors)
        rest = lax.all_gather(rest_mine, AXES, axis=0, tiled=True)
        weights = mesh.gather(mine)
        side = weights[:, 4 * D :].reshape(count, unit, PAIR)
        table = side[:, :8, :unit].transpose(1, 0, 2).reshape(8, D).astype(F32)
        b_inner = side[:, 8, : CHUNKS * unit].reshape(1, FF).astype(F32)
    else:
        trios = [w[:, g : g + GROUP] for g in range(0, D, GROUP) for w in (w_query, w_key, w_value)]
        full = lax.all_gather(jnp.concatenate([w_out, *trios, w_inner], axis=1), AXES, axis=0, tiled=True)
        outer = lax.all_gather(w_outer, AXES, axis=0, tiled=True)
        vector = lax.all_gather(jnp.concatenate(vectors), AXES, axis=0).astype(F32)
        weights = full[:, : 4 * D]
        table = jnp.concatenate([vector[:, i * unit : (i + 1) * unit].reshape(1, D) for i in range(8)])
        b_inner = vector[:, 8 * unit :].reshape(1, FF)
        unit = 24
        outer = outer.reshape(-1, CHUNKS, unit, D).transpose(0, 2, 1, 3).reshape(D, FF)
        rest = jnp.concatenate([outer, full[:, 4 * D :]], axis=1)

    qkv, ctx, probs, xt, h1, n1, n1low, n1t = attention_forward(x, segment_ids, weights, table)
    slope, g_outer, sums, result, db, dh2 = ffn_forward(
        unit, n1, n1low, cot, rest, b_inner, table, mesh.sizes if quick else None
    )
    if quick:
        db = after(db, g_outer)
        g_outer = mesh.core_sum(g_outer)
    g_inner, g_b_inner, dn1 = ffn_backward(unit, n1t, slope, db, rest)
    if not quick:
        late, sums, dctx, dh1 = norm_backward(h1, dn1, dh2, ctx, weights, table, sums)
        late, dqkv, sums = attention_backward(xt, qkv, ctx, probs, dctx, sums, late)
        dx = input_grad(dh1, dqkv, weights)
        wide = jnp.concatenate([late[:, : 4 * D], g_inner], axis=1)
        wide = lax.psum_scatter(wide, AXES, scatter_dimension=0, tiled=True).astype(F32)
        g_outer = lax.psum_scatter(g_outer, AXES, scatter_dimension=0, tiled=True).astype(F32)
        vector = jnp.concatenate([*sums.reshape(8, count, -1), g_b_inner.reshape(count, -1)], axis=1)
        vector = lax.psum_scatter(vector.reshape(-1), AXES, scatter_dimension=0, tiled=True)
        size = D // count
        vectors = [vector[i * size : (i + 1) * size] for i in range(8)] + [vector[8 * size :]]
        matrices = [wide[:, :D]] + [
            jnp.concatenate([wide[:, g + part : g + part + GROUP] for g in range(D, 4 * D, TRIO)], axis=1)
            for part in range(0, TRIO, GROUP)
        ]
        g_inner = wide[:, 4 * D :]
    else:
        message = mesh.core_message(g_inner)
        dn1, g_outer = after((dn1, g_outer), message)
        g_outer = mesh.plane_sum(g_outer)
        got = mesh.to_core(message)
        late, sums, dctx, dh1 = norm_backward(h1, dn1, dh2, ctx, weights, table, sums)
        got, sums = after((got, sums), dctx)
        message = mesh.plane_messages(g_inner, got)
        sums = after(sums, message)
        parts = mesh.plane_exchange(message)
        late, dqkv, sums = attention_backward(xt, qkv, ctx, probs, dctx, sums, late)
        late, parts, g_outer = after((late, parts, g_outer), dqkv)
        g_outer = mesh.line_sum(g_outer)
        late = lax.dynamic_update_slice(late, vector_rows(sums, g_b_inner, count), (0, 4 * D))
        message = mesh.core_message(late)
        dqkv, parts = after((dqkv, parts), message)
        lines = mesh.line_exchange(mesh.plane_done(parts))
        got = mesh.to_core(message)
        more = mesh.first_exchange(mesh.first_messages(late, got))
        dx = input_grad(dh1, dqkv, weights)
        more, g_inner = after((more, lines), dx)
        most = mesh.second_exchange(mesh.second_messages(late, got, more))
        most, g_outer = after((most, g_outer), dx)
        message = mesh.line_messages(late, got, more, most)
        g_outer, g_inner = after((g_outer, g_inner), message)
        matrices, vectors = finish(mesh.line_exchange(message))
        g_outer = g_outer.astype(F32)
        g_inner = sum(p.astype(F32) for p in g_inner)
    g_out, *matrices = matrices

    shards = [None] * len(params)
    for i, value in zip(MATRICES, (*matrices, g_out, g_inner, g_outer)):
        shards[i] = value
    for i, value in zip(VECTORS, vectors):
        shards[i] = value
    return (result.reshape(block_input.shape), dx.reshape(block_input.shape), *shards)


def solution(mesh):
    sizes = (mesh.shape["dp"], mesh.shape["fsdp"] // 4, 2, 2)
    parts = Mesh(np.asarray(mesh.devices).reshape(sizes), AXES)
    vector, matrix, rows = P(AXES), P(AXES, None), P(AXES, None, None)
    params = tuple(vector if i in VECTORS else matrix for i in range(15))
    return jax.shard_map(
        on_device,
        mesh=parts,
        in_specs=(rows, matrix, rows) + params,
        out_specs=(rows, rows) + params,
        check_vma=False,
    )
```

```python
import jax
import jax.numpy as jnp
import numpy as np
from jax import lax
from jax.experimental import pallas as pl
from jax.experimental.pallas import tpu as pltpu
from jax.sharding import Mesh, PartitionSpec as P

D = 768
FF = 3072
HEADS = 12
HEAD_DIM = 64
SEQ = 512
GROUP = 256
GROUPS = D // GROUP
TRIO = 3 * GROUP
PAIR = 128
SET = 4 * D + PAIR
KT = 256
CHUNK = 768
CHUNKS = FF // CHUNK
ROWS = 256
EPS = 1e-05
SHARE = 1.0
ROOT = 0.7978845608028654
CUBE = 0.044715
LOW = jnp.bfloat16
F32 = jnp.float32
MIB = 1 << 20
VMEM = 63 * MIB
MATRICES = (0, 2, 3, 5, 9, 11)
VECTORS = (1, 4, 6, 7, 8, 12, 13, 14, 10)
AXES = ("dp", "line", "side", "core")


def mm(a, b):
    return lax.dot_general(a, b, (((1,), (0,)), ((), ())), preferred_element_type=F32)


def mm_t(a, b):
    return lax.dot_general(a, b, (((1,), (1,)), ((), ())), preferred_element_type=F32)


def t_mm(a, b):
    return lax.dot_general(a, b, (((0,), (0,)), ((), ())), preferred_element_type=F32)


def cost(flops, moved, transcendentals):
    return pl.CostEstimate(
        flops=int(SHARE * flops),
        bytes_accessed=int(SHARE * moved),
        transcendentals=int(SHARE * transcendentals),
    )


def like(shape, kind):
    return jax.ShapeDtypeStruct(shape, kind)


def attention_forward_kernel(
    x_ref, w_ref, wout_ref, vec_ref, seg_ref,
    qkv_ref, ctx_ref, probs_ref, xt_ref, n_ref, inverse_ref, n1low_ref, n1t_ref, mask_ref, h1_ref,
):
    group = pl.program_id(1)
    x = x_ref[...]
    column = pl.ds(pl.multiple_of(group * GROUP, GROUP), GROUP)
    qkv_ref[:, :GROUP] = (mm(x, w_ref[:, :GROUP]) + vec_ref[0:1, column]).astype(LOW)
    qkv_ref[:, GROUP : 2 * GROUP] = mm(x, w_ref[:, GROUP : 2 * GROUP]).astype(LOW)
    qkv_ref[:, 2 * GROUP :] = (mm(x, w_ref[:, 2 * GROUP :]) + vec_ref[1:2, column]).astype(LOW)

    @pl.when(group == 0)
    def _():
        number = seg_ref[pl.ds(pl.program_id(0), 1), :].astype(F32)
        column = jnp.transpose(jnp.broadcast_to(number, (PAIR, SEQ)))[:, :1]
        mask_ref[...] = jnp.where(column == number, 0.0, -1e30)
        xt_ref[0] = jnp.transpose(x)
        h1_ref[...] = x.astype(F32) + vec_ref[2:3, :]

    lane = lax.broadcasted_iota(jnp.int32, (1, PAIR), 1)
    scale = jnp.asarray(HEAD_DIM**-0.5, LOW)
    for pair in range(GROUP // PAIR):
        q_lanes, k_lanes, v_lanes = (
            slice(part * GROUP + pair * PAIR, part * GROUP + (pair + 1) * PAIR) for part in range(3)
        )
        q_pair = qkv_ref[:, q_lanes] * scale
        v_pair = qkv_ref[:, v_lanes]
        halves = []
        for half in range(2):
            mine = (lane // HEAD_DIM) == half
            scores = mm_t(jnp.where(mine, qkv_ref[:, k_lanes], 0), q_pair) + mask_ref[...]
            weight = jnp.exp(scores - jnp.max(scores, axis=0, keepdims=True))
            total = jnp.sum(weight, axis=0, keepdims=True)
            probs = (weight * (1.0 / total)).astype(LOW)
            probs_ref[0, 0, 2 * pair + half] = probs
            halves.append(t_mm(probs, v_pair))
        ctx_ref[:, q_lanes] = jnp.where(lane < HEAD_DIM, halves[0], halves[1]).astype(LOW)
    h1_ref[...] += mm(ctx_ref[...], wout_ref[...])

    @pl.when(group == GROUPS - 1)
    def _():
        @pl.loop(0, SEQ // ROWS)
        def _(i):
            rows = pl.ds(pl.multiple_of(i * ROWS, ROWS), ROWS)
            n, inverse = norm_parts(h1_ref[rows, :])
            n_ref[rows, :] = n
            inverse_ref[rows, :] = jnp.broadcast_to(inverse, (ROWS, PAIR))
            n1low_ref[rows, :] = (n * vec_ref[3:4, :] + vec_ref[4:5, :]).astype(LOW)

        n1t_ref[...] = jnp.transpose(n1low_ref[...])


def attention_forward(x, seg, weights, table):
    rows = x.shape[0]
    seqs = rows // SEQ
    row = pl.BlockSpec((SEQ, D), lambda b, g: (b, 0))
    return pl.pallas_call(
        attention_forward_kernel,
        grid=(seqs, GROUPS),
        in_specs=[
            row,
            pl.BlockSpec((D, TRIO), lambda b, g: (0, 1 + g)),
            pl.BlockSpec((GROUP, D), lambda b, g: (g, 0)),
            pl.BlockSpec((8, D), lambda b, g: (0, 0)),
            pl.BlockSpec((seqs, SEQ), lambda b, g: (0, 0)),
        ],
        out_specs=[
            pl.BlockSpec((SEQ, TRIO), lambda b, g: (b, g)),
            pl.BlockSpec((SEQ, GROUP), lambda b, g: (b, g)),
            pl.BlockSpec((1, 1, GROUP // HEAD_DIM, SEQ, SEQ), lambda b, g: (b, g, 0, 0, 0)),
            pl.BlockSpec((1, D, SEQ), lambda b, g: (b, 0, 0)),
            row,
            pl.BlockSpec((SEQ, PAIR), lambda b, g: (b, 0)),
            row,
            pl.BlockSpec((D, SEQ), lambda b, g: (0, b)),
        ],
        out_shape=[
            like((rows, 3 * D), LOW),
            like((rows, D), LOW),
            like((seqs, GROUPS, GROUP // HEAD_DIM, SEQ, SEQ), LOW),
            like((seqs, D, SEQ), LOW),
            like((rows, D), F32),
            like((rows, PAIR), F32),
            like((rows, D), LOW),
            like((D, rows), LOW),
        ],
        scratch_shapes=[pltpu.VMEM((SEQ, SEQ), F32), pltpu.VMEM((SEQ, D), F32)],
        compiler_params=pltpu.CompilerParams(vmem_limit_bytes=VMEM),
        cost_estimate=cost(rows * (8 * D * D + 4 * D * SEQ), 36 * MIB, rows * SEQ * HEADS),
        name="attention_forward",
    )(x, weights, weights, table, seg)


def attention_backward_kernel(
    unit, core_ref, xt_ref, qkv_ref, ctx_ref, dctx_ref, probs_ref, vec_in_ref, keep_in_ref, send_in_ref,
    keep_ref, send_ref, dqkv_ref, vec_ref,
    ds_ref, acc_ref,
):
    row, seqs = pl.program_id(1), pl.num_programs(1)
    head_of = lax.broadcasted_iota(jnp.int32, (8, GROUP), 1) // HEAD_DIM
    picks = (head_of == lax.broadcasted_iota(jnp.int32, (8, GROUP), 0)).astype(F32)
    product = ctx_ref[...].astype(F32) * dctx_ref[...].astype(F32)
    inner = lax.dot_general(
        picks, product, (((1,), (1,)), ((), ())),
        preferred_element_type=F32, precision=lax.Precision.HIGHEST,
    )
    lane = lax.broadcasted_iota(jnp.int32, (1, PAIR), 1)
    first = lane < HEAD_DIM
    scale = jnp.asarray(HEAD_DIM**-0.5, LOW)
    tiles = [slice(i, i + KT) for i in range(0, SEQ, KT)]
    for pair in range(GROUP // PAIR):
        q_lanes, k_lanes, v_lanes = (
            slice(part * GROUP + pair * PAIR, part * GROUP + (pair + 1) * PAIR) for part in range(3)
        )
        q_pair = qkv_ref[:, q_lanes] * scale
        k_pair = qkv_ref[:, k_lanes] * scale
        dctx_pair = dctx_ref[:, q_lanes]
        dq, dk, dv = [], [], []
        for half in range(2):
            mine = (lane // HEAD_DIM) == half
            head = 2 * pair + half
            dk_tiles, dv_tiles = [], []
            for keys in tiles:
                probs = probs_ref[0, 0, head, keys, :]
                d_probs = mm_t(jnp.where(mine, qkv_ref[keys, v_lanes], 0), dctx_pair)
                d_scores = (probs.astype(F32) * (d_probs - inner[head : head + 1, :])).astype(LOW)
                ds_ref[half, keys, :] = d_scores
                dv_tiles.append(mm(probs, dctx_pair))
                dk_tiles.append(mm(d_scores, q_pair))
            dk.append(dk_tiles)
            dv.append(dv_tiles)
            dq.append([t_mm(ds_ref[half, :, rows], k_pair) for rows in tiles])
        for i, rows in enumerate(tiles):
            dqkv_ref[rows, q_lanes] = jnp.where(first, dq[0][i], dq[1][i]).astype(LOW)
            dqkv_ref[rows, k_lanes] = jnp.where(first, dk[0][i], dk[1][i]).astype(LOW)
            dqkv_ref[rows, v_lanes] = jnp.where(first, dv[0][i], dv[1][i]).astype(LOW)
    dqkv = dqkv_ref[...]
    product = mm(xt_ref[0], dqkv)
    bias_q = column_sum(dqkv[:, :GROUP].astype(F32))
    bias_v = column_sum(dqkv[:, 2 * GROUP :].astype(F32))

    @pl.when(row == 0)
    def _():
        acc_ref[...] = product
        vec_ref[...] = vec_in_ref[...]
        vec_ref[0:1, :] = bias_q
        vec_ref[1:2, :] = bias_v

    @pl.when(row > 0)
    def _():
        acc_ref[...] += product
        vec_ref[0:1, :] += bias_q
        vec_ref[1:2, :] += bias_v

    @pl.when(row == seqs - 1)
    def _():
        keep_ref[...], send_ref[...] = split_cores(acc_ref[...], core_ref[0], unit)


def attention_backward(unit, core, xt, qkv, ctx, probs, dctx, table, keep, send):
    rows = ctx.shape[0]
    seqs = rows // SEQ
    mine = lambda g, b: (b, g)
    return pl.pallas_call(
        lambda *refs: attention_backward_kernel(unit, *refs),
        grid=(GROUPS, seqs),
        in_specs=[
            pl.BlockSpec(memory_space=pltpu.SMEM),
            pl.BlockSpec((1, D, SEQ), lambda g, b: (b, 0, 0)),
            pl.BlockSpec((SEQ, TRIO), mine),
            pl.BlockSpec((SEQ, GROUP), mine),
            pl.BlockSpec((SEQ, GROUP), mine),
            pl.BlockSpec((1, 1, GROUP // HEAD_DIM, SEQ, SEQ), lambda g, b: (b, g, 0, 0, 0)),
            pl.BlockSpec((8, GROUP), lambda g, b: (0, g)),
            pl.BlockSpec(memory_space=pl.ANY),
            pl.BlockSpec(memory_space=pl.ANY),
        ],
        out_specs=[
            pl.BlockSpec((D // 2, TRIO), lambda g, b: (0, 1 + g)),
            pl.BlockSpec((D // 2, TRIO), lambda g, b: (0, 1 + g)),
            pl.BlockSpec((SEQ, TRIO), mine),
            pl.BlockSpec((8, GROUP), lambda g, b: (0, g)),
        ],
        out_shape=[like((D // 2, SET), LOW)] * 2 + [like((rows, 3 * D), LOW), like((8, D), F32)],
        input_output_aliases={6: 3, 7: 0, 8: 1},
        scratch_shapes=[pltpu.VMEM((2, SEQ, SEQ), LOW), pltpu.VMEM((D, TRIO), F32)],
        compiler_params=pltpu.CompilerParams(vmem_limit_bytes=VMEM),
        cost_estimate=cost(rows * (6 * D * D + 8 * D * SEQ), 36 * MIB, 0),
        name="attention_backward",
    )(core, xt, qkv, ctx, dctx, probs, table, keep, send)


def input_grad_kernel(da_ref, dqkv_ref, *refs):
    total = da_ref[...].astype(F32)
    for g in range(GROUPS):
        total += mm_t(dqkv_ref[:, g * TRIO : (g + 1) * TRIO], refs[g][...])
    refs[GROUPS][...] = total.astype(LOW)


def input_grad(da, dqkv, weights):
    rows = da.shape[0]
    return pl.pallas_call(
        input_grad_kernel,
        grid=(rows // ROWS,),
        in_specs=[
            pl.BlockSpec((ROWS, D), lambda i: (i, 0)),
            pl.BlockSpec((ROWS, 3 * D), lambda i: (i, 0)),
            *(pl.BlockSpec((D, TRIO), lambda i, g=g: (0, 1 + g)) for g in range(GROUPS)),
        ],
        out_specs=pl.BlockSpec((ROWS, D), lambda i: (i, 0)),
        out_shape=like((rows, D), LOW),
        compiler_params=pltpu.CompilerParams(vmem_limit_bytes=VMEM),
        cost_estimate=cost(6 * rows * D * D, 13 * MIB, 0),
        name="input_grad",
    )(da, dqkv, *[weights] * GROUPS)


def norm_parts(hidden):
    mean = jnp.mean(hidden, axis=1, keepdims=True)
    centred = hidden - mean
    inverse = lax.rsqrt(jnp.mean(centred * centred, axis=1, keepdims=True) + EPS)
    return centred * inverse, inverse


def norm_back(grad, gain, normed, inverse):
    scaled = grad * gain
    mean = jnp.mean(scaled, axis=1, keepdims=True)
    along = jnp.mean(scaled * normed, axis=1, keepdims=True)
    return inverse * (scaled - mean - normed * along)


def column_sum(array):
    return jnp.sum(array, axis=0, keepdims=True)


def gelu_and_slope(v):
    square = v * v
    bent = jnp.tanh(v * (ROOT + ROOT * CUBE * square))
    half = 0.5 + 0.5 * bent
    act = v * half
    slope = half + act * (1.0 - half) * (2.0 * ROOT + 6.0 * ROOT * CUBE * square)
    return act, slope


def order_outer(block_ref, out_ref, unit):
    for o in range(block_ref.shape[0] // unit):
        for j in range(CHUNKS):
            to = (o * CHUNKS + j) * unit
            out_ref[to : to + unit, :] = block_ref[o * unit : (o + 1) * unit, j * D : (j + 1) * D]


def ffn_forward_kernel(
    unit, n1low_ref, outer_ref, wi_ref, bi_ref, vec_ref, n_hbm, cot_hbm,
    slope_ref, gwo_ref, sums_ref, out_hbm, db_hbm, dh2_hbm,
    n_ref, cot_ref, h2_ref, wo_ref, act_ref, out_ref, db_ref, dh2_ref, sem,
):
    step = pl.program_id(0)
    tiles = [slice(i, i + ROWS) for i in range(0, h2_ref.shape[0], ROWS)]
    loads = [
        pltpu.make_async_copy(n_hbm, n_ref, sem.at[0]),
        pltpu.make_async_copy(cot_hbm, cot_ref, sem.at[1]),
    ]
    stores = [
        pltpu.make_async_copy(out_ref, out_hbm, sem.at[2]),
        pltpu.make_async_copy(db_ref, db_hbm, sem.at[3]),
        pltpu.make_async_copy(dh2_ref, dh2_hbm, sem.at[4]),
    ]

    @pl.when(step == 0)
    def _():
        for copy in loads:
            copy.start()
        h2_ref[...] = jnp.zeros_like(h2_ref)

    @pl.when(step < CHUNKS)
    def _():
        order_outer(outer_ref, wo_ref, unit)
        for rows in tiles:
            pre = mm(n1low_ref[rows, :], wi_ref[...]) + bi_ref[...]
            act, slope = gelu_and_slope(pre)
            act = act.astype(LOW)
            act_ref[step, rows, :] = act
            slope_ref[rows, :] = slope.astype(LOW)
            h2_ref[rows, :] += mm(act, wo_ref[...])

    @pl.when(step == CHUNKS - 1)
    def _():
        for copy in loads:
            copy.wait()
        gain, shift = vec_ref[6:7, :], vec_ref[7:8, :]
        sums_ref[...] = jnp.zeros_like(sums_ref)

        @pl.loop(0, h2_ref.shape[0] // ROWS, unroll=2)
        def _(i):
            rows = pl.ds(pl.multiple_of(i * ROWS, ROWS), ROWS)
            n, inverse = norm_parts(
                h2_ref[rows, :] + (n_ref[rows, :] * vec_ref[3:4, :] + vec_ref[4:5, :] + vec_ref[5:6, :])
            )
            out_ref[rows, :] = (n * gain + shift).astype(LOW)
            cot = cot_ref[rows, :].astype(F32)
            dh2 = norm_back(cot, gain, n, inverse)
            dh2_ref[rows, :] = dh2
            db = dh2.astype(LOW)
            db_ref[rows, :] = db
            for j, new in enumerate((column_sum(db.astype(F32)), column_sum(cot * n), column_sum(cot))):
                sums_ref[5 + j : 6 + j, :] += new

        for copy in stores:
            copy.start()

    @pl.when(step >= CHUNKS)
    def _():
        grad = t_mm(act_ref[step - CHUNKS], db_ref[...]).astype(LOW)
        if len(gwo_ref.shape) == 2:
            gwo_ref[...] = grad
        else:
            _, _, sides, lines, deep, _ = gwo_ref.shape
            for i in range(CHUNK // deep):
                core, side, line = i % 2, i // 2 % sides, i // 2 // sides
                gwo_ref[core, 0, side, line] = grad[i * deep : (i + 1) * deep, :]

    @pl.when(step == 2 * CHUNKS - 1)
    def _():
        for copy in stores:
            copy.wait()


def ffn_forward(unit, normed, n1low, cot, rest, b_inner, table, sizes=None):
    rows = normed.shape[0]
    last = CHUNKS - 1
    now = lambda c: jnp.minimum(c, last)
    then = lambda c: jnp.maximum(c - CHUNKS, 0)
    eight = pl.BlockSpec((8, D), lambda c: (0, 0))
    if sizes is None:
        outer_shape = (FF, D)
        outer_block = pl.BlockSpec((CHUNK, D), lambda c: (then(c), 0))
    else:
        dps, lines, sides, cores = sizes
        deep = CHUNKS * unit
        held = CHUNK // (deep * sides * cores)
        outer_shape = (cores, dps, sides, lines, deep, D)
        outer_block = pl.BlockSpec(
            (cores, 1, sides, held, deep, D),
            lambda c: (0, then(c) * held // lines, 0, then(c) % (lines // held), 0, 0),
        )
    anywhere = pl.BlockSpec(memory_space=pl.ANY)
    return pl.pallas_call(
        lambda *refs: ffn_forward_kernel(unit, *refs),
        grid=(2 * CHUNKS,),
        in_specs=[
            pl.BlockSpec((rows, D), lambda c: (0, 0), pipeline_mode=pl.Buffered(1)),
            pl.BlockSpec((D // CHUNKS, FF), lambda c: (now(c), 0)),
            pl.BlockSpec((D, CHUNK), lambda c: (0, CHUNKS + now(c))),
            pl.BlockSpec((1, CHUNK), lambda c: (0, now(c))),
            eight,
            anywhere,
            anywhere,
        ],
        out_specs=[
            pl.BlockSpec((rows, CHUNK), lambda c: (0, now(c))),
            outer_block,
            eight,
            anywhere,
            anywhere,
            anywhere,
        ],
        out_shape=[
            like((rows, FF), LOW),
            like(outer_shape, LOW),
            like((8, D), F32),
            like((rows, D), LOW),
            like((rows, D), LOW),
            like((rows, D), F32),
        ],
        scratch_shapes=[
            pltpu.VMEM((rows, D), F32),
            pltpu.VMEM((rows, D), LOW),
            pltpu.VMEM((rows, D), F32),
            pltpu.VMEM((CHUNK, D), LOW),
            pltpu.VMEM((CHUNKS, rows, CHUNK), LOW),
            pltpu.VMEM((rows, D), LOW),
            pltpu.VMEM((rows, D), LOW),
            pltpu.VMEM((rows, D), F32),
            pltpu.SemaphoreType.DMA((5,)),
        ],
        compiler_params=pltpu.CompilerParams(vmem_limit_bytes=VMEM),
        cost_estimate=cost(6 * rows * D * FF, 34 * MIB, rows * FF),
        name="ffn_forward",
    )(n1low, rest, rest, b_inner, table, normed, cot)


def split_cores(grad, core, unit):
    rows = range(0, grad.shape[0], 2 * unit)
    even = jnp.concatenate([grad[i : i + unit] for i in rows], axis=0)
    odd = jnp.concatenate([grad[i + unit : i + 2 * unit] for i in rows], axis=0)
    return jnp.where(core == 0, even, odd).astype(LOW), jnp.where(core == 0, odd, even).astype(LOW)


def ffn_backward_kernel(
    unit, core_ref, n1t_ref, slope_ref, db_ref, outer_ref, wi_ref, dh2_hbm,
    keep_ref, send_ref, gbi_ref, dn1_ref,
    dpre_ref, wo_ref, dh2_ref, sem,
):
    step = pl.program_id(0)
    tiles = [slice(i, i + ROWS) for i in range(0, db_ref.shape[0], ROWS)]
    order_outer(outer_ref, wo_ref, unit)

    load = pltpu.make_async_copy(dh2_hbm, dh2_ref, sem)

    @pl.when(step == 0)
    def _():
        load.start()
        dn1_ref[...] = jnp.zeros_like(dn1_ref)

    @pl.when(step == CHUNKS - 1)
    def _():
        load.wait()
        dn1_ref[...] += dh2_ref[...]

    bias = jnp.zeros((1, CHUNK), F32)
    for rows in tiles:
        dpre = (mm_t(db_ref[rows, :], wo_ref[...]) * slope_ref[rows, :].astype(F32)).astype(LOW)
        dpre_ref[rows, :] = dpre
        bias += column_sum(dpre.astype(F32))
        dn1_ref[rows, :] += mm_t(dpre, wi_ref[...])
    gbi_ref[...] = bias
    keep_ref[...], send_ref[...] = split_cores(mm(n1t_ref[...], dpre_ref[...]), core_ref[0], unit)


def ffn_backward(unit, core, n1t, slope, db, dh2, rest):
    rows = db.shape[0]
    once = pl.BlockSpec((rows, D), lambda c: (0, 0), pipeline_mode=pl.Buffered(1))
    return pl.pallas_call(
        lambda *refs: ffn_backward_kernel(unit, *refs),
        grid=(CHUNKS,),
        in_specs=[
            pl.BlockSpec(memory_space=pltpu.SMEM),
            pl.BlockSpec((D, rows), lambda c: (0, 0), pipeline_mode=pl.Buffered(1)),
            pl.BlockSpec((rows, CHUNK), lambda c: (0, c)),
            once,
            pl.BlockSpec((D // CHUNKS, FF), lambda c: (c, 0)),
            pl.BlockSpec((D, CHUNK), lambda c: (0, CHUNKS + c)),
            pl.BlockSpec(memory_space=pl.ANY),
        ],
        out_specs=[
            pl.BlockSpec((D // 2, CHUNK), lambda c: (0, c)),
            pl.BlockSpec((D // 2, CHUNK), lambda c: (0, c)),
            pl.BlockSpec((1, CHUNK), lambda c: (0, c)),
            pl.BlockSpec((rows, D), lambda c: (0, 0)),
        ],
        out_shape=[like((D // 2, FF), LOW)] * 2 + [like((1, FF), F32), like((rows, D), F32)],
        scratch_shapes=[
            pltpu.VMEM((rows, CHUNK), LOW),
            pltpu.VMEM((CHUNK, D), LOW),
            pltpu.VMEM((rows, D), F32),
            pltpu.SemaphoreType.DMA,
        ],
        compiler_params=pltpu.CompilerParams(vmem_limit_bytes=VMEM),
        cost_estimate=cost(6 * rows * D * FF, 30 * MIB, 0),
        name="ffn_backward",
    )(core, n1t, slope, db, rest, rest, dh2)


def norm_backward_kernel(
    unit, core_ref, wout_ref, vec_ref, sums_in_ref, n_hbm, inverse_hbm, dn1_hbm, ctx_hbm,
    keep_ref, send_ref, sums_ref, dctx_hbm, da_hbm,
    n_ref, inverse_ref, dn1_ref, ctx_ref, da_ref, dctx_ref, load_sem, store_sem,
):
    tiles = [slice(i, i + ROWS) for i in range(0, n_ref.shape[0], ROWS)]
    pairs = ((n_hbm, n_ref), (inverse_hbm, inverse_ref), (dn1_hbm, dn1_ref), (ctx_hbm, ctx_ref))
    loads = [
        [pltpu.make_async_copy(a.at[rows, :], b.at[rows, :], load_sem.at[i, j]) for j, (a, b) in enumerate(pairs)]
        for i, rows in enumerate(tiles)
    ]
    stores = [
        [
            pltpu.make_async_copy(da_ref.at[rows, :], da_hbm.at[rows, :], store_sem.at[i, 0]),
            pltpu.make_async_copy(dctx_ref.at[rows, :], dctx_hbm.at[rows, :], store_sem.at[i, 1]),
        ]
        for i, rows in enumerate(tiles)
    ]
    for group in loads:
        for copy in group:
            copy.start()
    sums = [jnp.zeros((1, D), F32)] * 3
    for i, rows in enumerate([*tiles, None]):
        if rows is not None:
            for copy in loads[i]:
                copy.wait()
        if i > 0:
            dctx_ref[tiles[i - 1], :] = mm_t(da_ref[tiles[i - 1], :], wout_ref[...]).astype(LOW)
        if rows is not None:
            n = n_ref[rows, :]
            dn1 = dn1_ref[rows, :]
            da = norm_back(dn1, vec_ref[3:4, :], n, inverse_ref[rows, 0:1]).astype(LOW)
            da_ref[rows, :] = da
            new = (column_sum(da.astype(F32)), column_sum(dn1 * n), column_sum(dn1))
            sums = [a + b for a, b in zip(sums, new)]
            stores[i][0].start()
        if i > 0:
            stores[i - 1][1].start()
    keep_ref[...], send_ref[...] = split_cores(t_mm(ctx_ref[...], da_ref[...]), core_ref[0], unit)
    sums_ref[...] = sums_in_ref[...]
    for i in range(3):
        sums_ref[2 + i : 3 + i, :] = sums[i]
    for group in stores:
        for copy in group:
            copy.wait()


def norm_backward(unit, core, normed, inverse, dn1, ctx, weights, table, sums):
    rows = normed.shape[0]
    eight = pl.BlockSpec((8, D), lambda i: (0, 0))
    half = pl.BlockSpec((D // 2, D), lambda i: (0, 0))
    anywhere = pl.BlockSpec(memory_space=pl.ANY)
    return pl.pallas_call(
        lambda *refs: norm_backward_kernel(unit, *refs),
        grid=(1,),
        in_specs=[
            pl.BlockSpec(memory_space=pltpu.SMEM),
            pl.BlockSpec((D, D), lambda i: (0, 0)),
            eight,
            eight,
        ]
        + [anywhere] * 4,
        out_specs=[half, half, eight, anywhere, anywhere],
        out_shape=[like((D // 2, SET), LOW)] * 2
        + [like((8, D), F32), like((rows, D), LOW), like((rows, D), LOW)],
        scratch_shapes=[
            pltpu.VMEM((rows, D), F32),
            pltpu.VMEM((rows, PAIR), F32),
            pltpu.VMEM((rows, D), F32),
            pltpu.VMEM((rows, D), LOW),
            pltpu.VMEM((rows, D), LOW),
            pltpu.VMEM((rows, D), LOW),
            pltpu.SemaphoreType.DMA((rows // ROWS, 4)),
            pltpu.SemaphoreType.DMA((rows // ROWS, 2)),
        ],
        compiler_params=pltpu.CompilerParams(vmem_limit_bytes=VMEM),
        cost_estimate=cost(4 * rows * D * D, 17 * MIB, 0),
        name="norm_backward",
    )(core, weights, table, sums, normed, inverse, dn1, ctx)


def after(values, *others):
    return lax.optimization_barrier((values, others))[0]


def whole(array):
    return pl.BlockSpec(array.shape, lambda *_: (0,) * len(array.shape))


def pack_kernel(wq_ref, wk_ref, wv_ref, wout_ref, wi_ref, wo_ref, *refs):
    vectors, (set_ref, rest_ref) = refs[:9], refs[9:]
    unit = wq_ref.shape[0]
    set_ref[:, :D] = wout_ref[...]
    for g in range(GROUPS):
        for part, ref in enumerate((wq_ref, wk_ref, wv_ref)):
            to = D + g * TRIO + part * GROUP
            set_ref[:, to : to + GROUP] = ref[:, g * GROUP : (g + 1) * GROUP]
    table = jnp.zeros((unit, PAIR), F32)
    row = lax.broadcasted_iota(jnp.int32, (unit, PAIR), 0)
    for i, ref in enumerate(vectors):
        size = ref.shape[1]
        line = jnp.concatenate([ref[...].astype(F32), jnp.zeros((1, PAIR - size), F32)], axis=1)
        table = jnp.where(row == i, line, table)
    set_ref[:, 4 * D :] = table.astype(LOW)
    for j in range(CHUNKS):
        rest_ref[:, j * D : (j + 1) * D] = wo_ref[j * unit : (j + 1) * unit, :]
    rest_ref[:, FF:] = wi_ref[...]


def pack(wq, wk, wv, wout, wi, wo, vectors):
    unit = wq.shape[0]
    args = (wq, wk, wv, wout, wi, wo, *(v.reshape(1, -1) for v in vectors))
    shapes = [like((unit, SET), LOW), like((unit, 2 * FF), LOW)]
    return pl.pallas_call(
        pack_kernel,
        grid=(1,),
        in_specs=[whole(a) for a in args],
        out_specs=[whole(a) for a in shapes],
        out_shape=shapes,
        compiler_params=pltpu.CompilerParams(vmem_limit_bytes=VMEM),
        name="pack",
    )(*args)


def stack_kernel(*refs):
    for i, ref in enumerate(refs[:-1]):
        refs[-1][i] = ref[...]


def stack(pieces):
    shape = like((len(pieces), *pieces[0].shape), pieces[0].dtype)
    return pl.pallas_call(
        stack_kernel,
        grid=(1,),
        in_specs=[pl.BlockSpec(memory_space=pltpu.VMEM)] * len(pieces),
        out_specs=whole(shape),
        out_shape=shape,
        compiler_params=pltpu.CompilerParams(vmem_limit_bytes=8 * MIB),
        name="stack",
    )(*pieces)


class Slice:
    def __init__(self):
        self.sizes = tuple(lax.axis_size(name) for name in AXES)
        self.dp, self.line, self.side, self.core = (lax.axis_index(name) for name in AXES)
        self.offsets = [(a, b) for a in range(self.sizes[0]) for b in range(self.sizes[2])]

    def to_core(self, array):
        return lax.ppermute(array, "core", [(0, 1), (1, 0)])

    def to_plane(self, array, offset):
        dps, _, sides, _ = self.sizes
        pairs = [
            (i * sides + j, (i + offset[0]) % dps * sides + (j + offset[1]) % sides)
            for i in range(dps)
            for j in range(sides)
        ]
        return lax.ppermute(array, ("dp", "side"), pairs)

    def to_line(self, array, shift):
        count = self.sizes[1]
        return lax.ppermute(array, "line", [(i, (i + shift) % count) for i in range(count)])

    def gather(self, mine):
        dps, lines, sides, _ = self.sizes
        unit, columns = mine.shape
        line = stack([mine] + [self.to_line(mine, s) for s in range(1, lines)])
        here = [line if o == (0, 0) else self.to_plane(line, o) for o in self.offsets]
        there = [self.to_core(a) for a in here]
        place = jnp.stack([self.dp, self.line, self.side, self.core]).astype(jnp.int32)
        pieces = here + there

        wide = 5 * PAIR

        def kernel(place_ref, *refs):
            out_ref = refs[-1]
            for i in range(len(pieces)):
                a, b = self.offsets[i % len(here)]
                dp = lax.rem(place_ref[0] + dps - a, dps)
                side = lax.rem(place_ref[2] + sides - b, sides)
                core = place_ref[3] if i < len(here) else 1 - place_ref[3]
                for s in range(lines):
                    along = lax.rem(place_ref[1] + lines - s, lines)
                    out_ref[((dp * lines + along) * sides + side) * 2 + core] = refs[i][s]

        count = dps * lines * sides * 2
        return pl.pallas_call(
            kernel,
            grid=(columns // wide,),
            in_specs=[pl.BlockSpec(memory_space=pltpu.SMEM)]
            + [pl.BlockSpec((lines, unit, wide), lambda i: (0, 0, i))] * len(pieces),
            out_specs=pl.BlockSpec((count, unit, wide), lambda i: (0, 0, i)),
            out_shape=like((count, unit, columns), mine.dtype),
            compiler_params=pltpu.CompilerParams(vmem_limit_bytes=VMEM),
            name="place",
        )(place, *pieces).reshape(-1, columns)


    def chips_sum(self, grad):
        return lax.psum_scatter(grad.reshape(-1, *grad.shape[3:]), ("core", "dp", "side"), scatter_dimension=0)

    def line_sum(self, grad):
        return lax.psum_scatter(grad, "line", scatter_dimension=0)

    def join_cores(self, keep, send, unit):
        keep, send = (part.reshape(-1, 1, unit, part.shape[1]) for part in (keep, send))
        mine = self.core == 0
        pair = [jnp.where(mine, keep, send), jnp.where(mine, send, keep)]
        return jnp.concatenate(pair, axis=1).reshape(-1, keep.shape[3])


    def plane_messages(self, grad, got):
        dps, _, sides, _ = self.sizes
        return [
            self.block(grad, got, lax.rem(self.dp + a, dps), lax.rem(self.side + b, sides)).astype(LOW)
            for a, b in self.offsets[1:]
        ]

    def plane_exchange(self, messages):
        return [self.to_plane(m, o) for m, o in zip(messages, self.offsets[1:])]

    def plane_done(self, grad, got, parts):
        total = self.block(grad, got, self.dp, self.side)
        return self.along_line((total + sum(p.astype(F32) for p in parts)).astype(LOW))

    def block(self, grad, got, dp, side):
        dps, lines, sides, _ = self.sizes
        total = 0.0
        for part in (grad, got):
            part = part.reshape(dps, lines, sides, -1, grad.shape[1])
            size = (1, lines, 1, *part.shape[3:])
            total += lax.dynamic_slice(part, (dp, 0, side, 0, 0), size)[0, :, 0].astype(F32)
        return total

    def along_line(self, total):
        lines = self.sizes[1]
        at = [lax.rem(self.line + s, lines) for s in range(lines)]
        return [lax.dynamic_index_in_dim(total, i, 0, keepdims=False) for i in at]

    def line_exchange(self, messages):
        return messages[:1] + [self.to_line(m, s) for s, m in enumerate(messages) if s]


def finish_kernel(count, *refs):
    parts, (wout_ref, wq_ref, wk_ref, wv_ref), vectors = refs[:count], refs[count : count + 4], refs[count + 4 :]
    total = sum(ref[...].astype(F32) for ref in parts)
    wout_ref[...] = total[:, :D]
    for g in range(GROUPS):
        for part, ref in enumerate((wq_ref, wk_ref, wv_ref)):
            at = D + g * TRIO + part * GROUP
            ref[:, g * GROUP : (g + 1) * GROUP] = total[:, at : at + GROUP]
    for i, ref in enumerate(vectors):
        ref[...] = total[i : i + 1, 4 * D : 4 * D + ref.shape[1]]


def finish(parts):
    unit = parts[0].shape[0]
    shapes = [like((unit, D), F32)] * 4 + [like((1, unit), F32)] * 8 + [like((1, CHUNKS * unit), F32)]
    outs = pl.pallas_call(
        lambda *refs: finish_kernel(len(parts), *refs),
        grid=(1,),
        in_specs=[pl.BlockSpec(memory_space=pltpu.VMEM)] * len(parts),
        out_specs=[whole(a) for a in shapes],
        out_shape=shapes,
        compiler_params=pltpu.CompilerParams(vmem_limit_bytes=8 * MIB),
        name="finish",
    )(*parts)
    return outs[:4], [v.reshape(-1) for v in outs[4:]]


def vector_rows(table, b_inner, count):
    unit = D // count
    eight = table.reshape(8, count, unit).transpose(1, 0, 2)
    inner = b_inner.reshape(count, 1, CHUNKS * unit)
    eight = jnp.pad(eight, ((0, 0), (0, 0), (0, PAIR - unit)))
    inner = jnp.pad(inner, ((0, 0), (0, unit - 9), (0, PAIR - CHUNKS * unit)))
    return jnp.concatenate([eight, inner], axis=1).astype(LOW)


def on_device(block_input, segment_ids, cotangent, *params):
    w_query, w_key, w_value, w_out, w_inner, w_outer = (params[i] for i in MATRICES)
    vectors = [params[i] for i in VECTORS]
    unit = w_query.shape[0]
    count = D // unit
    mesh = Slice()
    quick = mesh.sizes == (2, 4, 2, 2) and unit == 24
    x = block_input.reshape(-1, D)
    cot = cotangent.reshape(-1, D)

    if quick:
        mine, rest_mine = pack(w_query, w_key, w_value, w_out, w_inner, w_outer, vectors)
        rest = lax.all_gather(rest_mine, AXES, axis=0, tiled=True)
        weights = mesh.gather(mine)
        side = weights[:, 4 * D :].reshape(count, unit, PAIR)
        table = side[:, :8, :unit].transpose(1, 0, 2).reshape(8, D).astype(F32)
        b_inner = side[:, 8, : CHUNKS * unit].reshape(1, FF).astype(F32)
    else:
        trios = [w[:, g : g + GROUP] for g in range(0, D, GROUP) for w in (w_query, w_key, w_value)]
        full = lax.all_gather(jnp.concatenate([w_out, *trios, w_inner], axis=1), AXES, axis=0, tiled=True)
        outer = lax.all_gather(w_outer, AXES, axis=0, tiled=True)
        vector = lax.all_gather(jnp.concatenate(vectors), AXES, axis=0).astype(F32)
        weights = full[:, : 4 * D]
        table = jnp.concatenate([vector[:, i * unit : (i + 1) * unit].reshape(1, D) for i in range(8)])
        b_inner = vector[:, 8 * unit :].reshape(1, FF)
        unit = 24
        outer = outer.reshape(-1, CHUNKS, unit, D).transpose(0, 2, 1, 3).reshape(D, FF)
        rest = jnp.concatenate([outer, full[:, 4 * D :]], axis=1)

    core = mesh.core[None].astype(jnp.int32)
    qkv, ctx, probs, xt, normed, inverse, n1low, n1t = attention_forward(x, segment_ids, weights, table)
    slope, g_outer, sums, result, db, dh2 = ffn_forward(
        unit, normed, n1low, cot, rest, b_inner, table, mesh.sizes if quick else None
    )
    if quick:
        db = after(db, g_outer)
        g_outer = mesh.chips_sum(g_outer)
    keep, send, g_b_inner, dn1 = ffn_backward(unit, core, n1t, slope, db, dh2, rest)
    if not quick:
        g_inner = mesh.join_cores(keep, send, unit)
        keep, send, sums, dctx, da = norm_backward(unit, core, normed, inverse, dn1, ctx, weights, table, sums)
        keep, send, dqkv, sums = attention_backward(unit, core, xt, qkv, ctx, probs, dctx, sums, keep, send)
        late = mesh.join_cores(keep, send, unit)
        dx = input_grad(da, dqkv, weights)
        wide = jnp.concatenate([late[:, : 4 * D], g_inner], axis=1)
        wide = lax.psum_scatter(wide, AXES, scatter_dimension=0, tiled=True).astype(F32)
        g_outer = lax.psum_scatter(g_outer, AXES, scatter_dimension=0, tiled=True).astype(F32)
        vector = jnp.concatenate([*sums.reshape(8, count, -1), g_b_inner.reshape(count, -1)], axis=1)
        vector = lax.psum_scatter(vector.reshape(-1), AXES, scatter_dimension=0, tiled=True)
        size = D // count
        vectors = [vector[i * size : (i + 1) * size] for i in range(8)] + [vector[8 * size :]]
        matrices = [wide[:, :D]] + [
            jnp.concatenate([wide[:, g + part : g + part + GROUP] for g in range(D, 4 * D, TRIO)], axis=1)
            for part in range(0, TRIO, GROUP)
        ]
        g_inner = wide[:, 4 * D :]
    else:
        g_inner = keep
        dn1 = after(dn1, send)
        got = mesh.to_core(send)
        keep, send, sums, dctx, da = norm_backward(unit, core, normed, inverse, dn1, ctx, weights, table, sums)
        inner_got, sums = after((got, sums), dctx)
        message = mesh.plane_messages(g_inner, inner_got)
        sums = after(sums, message)
        parts = mesh.plane_exchange(message)
        late, send, dqkv, sums = attention_backward(unit, core, xt, qkv, ctx, probs, dctx, sums, keep, send)
        late, send, parts, g_outer = after((late, send, parts, g_outer), dqkv)
        g_outer = mesh.line_sum(g_outer)
        vector = vector_rows(sums, g_b_inner, count).reshape(-1, 2, unit, PAIR)
        at = (mesh.core, 1 - mesh.core)
        vector = [lax.dynamic_index_in_dim(vector, i, 1, keepdims=False).reshape(-1, PAIR) for i in at]
        late = lax.dynamic_update_slice(late, vector[0], (0, 4 * D))
        send = lax.dynamic_update_slice(send, vector[1], (0, 4 * D))
        dqkv, parts = after((dqkv, parts), (late, send))
        lines = mesh.line_exchange(mesh.plane_done(g_inner, inner_got, parts))
        got = mesh.to_core(send)
        parts = mesh.plane_exchange(mesh.plane_messages(late, got))
        dx = input_grad(da, dqkv, weights)
        parts, g_inner, g_outer = after((parts, lines, g_outer), dx)
        message = mesh.plane_done(late, got, parts)
        g_outer, g_inner = after((g_outer, g_inner), message)
        matrices, vectors = finish(mesh.line_exchange(message))
        g_outer = g_outer.astype(F32)
        g_inner = sum(p.astype(F32) for p in g_inner)
    g_out, *matrices = matrices

    shards = [None] * len(params)
    for i, value in zip(MATRICES, (*matrices, g_out, g_inner, g_outer)):
        shards[i] = value
    for i, value in zip(VECTORS, vectors):
        shards[i] = value
    return (result.reshape(block_input.shape), dx.reshape(block_input.shape), *shards)


def solution(mesh):
    sizes = (mesh.shape["dp"], mesh.shape["fsdp"] // 4, 2, 2)
    parts = Mesh(np.asarray(mesh.devices).reshape(sizes), AXES)
    vector, matrix, rows = P(AXES), P(AXES, None), P(AXES, None, None)
    params = tuple(vector if i in VECTORS else matrix for i in range(15))
    return jax.shard_map(
        on_device,
        mesh=parts,
        in_specs=(rows, matrix, rows) + params,
        out_specs=(rows, rows) + params,
        check_vma=False,
    )
```

```python
import jax
import jax.numpy as jnp
import numpy as np
from jax import lax
from jax.experimental import pallas as pl
from jax.experimental.pallas import tpu as pltpu
from jax.sharding import Mesh, PartitionSpec as P

D = 768
FF = 3072
HEADS = 12
HEAD_DIM = 64
SEQ = 512
GROUP = 256
GROUPS = D // GROUP
TRIO = 3 * GROUP
PAIR = 128
SET = 4 * D + PAIR
KT = 256
CHUNK = 768
CHUNKS = FF // CHUNK
ROWS = 256
EPS = 1e-05
SHARE = 1.0
ROOT = 0.7978845608028654
CUBE = 0.044715
LOW = jnp.bfloat16
F32 = jnp.float32
MIB = 1 << 20
VMEM = 63 * MIB
MATRICES = (0, 2, 3, 5, 9, 11)
VECTORS = (1, 4, 6, 7, 8, 12, 13, 14, 10)
AXES = ("dp", "line", "side", "core")


def mm(a, b):
    return lax.dot_general(a, b, (((1,), (0,)), ((), ())), preferred_element_type=F32)


def mm_t(a, b):
    return lax.dot_general(a, b, (((1,), (1,)), ((), ())), preferred_element_type=F32)


def t_mm(a, b):
    return lax.dot_general(a, b, (((0,), (0,)), ((), ())), preferred_element_type=F32)


def cost(flops, moved, transcendentals):
    return pl.CostEstimate(
        flops=int(SHARE * flops),
        bytes_accessed=int(SHARE * moved),
        transcendentals=int(SHARE * transcendentals),
    )


def like(shape, kind):
    return jax.ShapeDtypeStruct(shape, kind)


def attention_forward_kernel(
    x_ref, w_ref, wout_ref, vec_ref, seg_ref,
    qkv_ref, ctx_ref, probs_ref, xt_ref, n_ref, inverse_ref, n1low_ref, n1t_ref, mask_ref, h1_ref,
):
    group = pl.program_id(1)
    x = x_ref[...]
    column = pl.ds(pl.multiple_of(group * GROUP, GROUP), GROUP)
    qkv_ref[:, :GROUP] = (mm(x, w_ref[:, :GROUP]) + vec_ref[0:1, column]).astype(LOW)
    qkv_ref[:, GROUP : 2 * GROUP] = mm(x, w_ref[:, GROUP : 2 * GROUP]).astype(LOW)
    qkv_ref[:, 2 * GROUP :] = (mm(x, w_ref[:, 2 * GROUP :]) + vec_ref[1:2, column]).astype(LOW)

    @pl.when(group == 0)
    def _():
        number = seg_ref[pl.ds(pl.program_id(0), 1), :].astype(F32)
        column = jnp.transpose(jnp.broadcast_to(number, (PAIR, SEQ)))[:, :1]
        mask_ref[...] = jnp.where(column == number, 0.0, -1e30)
        xt_ref[0] = jnp.transpose(x)
        h1_ref[...] = x.astype(F32) + vec_ref[2:3, :]

    lane = lax.broadcasted_iota(jnp.int32, (1, PAIR), 1)
    scale = jnp.asarray(HEAD_DIM**-0.5, LOW)
    for pair in range(GROUP // PAIR):
        q_lanes, k_lanes, v_lanes = (
            slice(part * GROUP + pair * PAIR, part * GROUP + (pair + 1) * PAIR) for part in range(3)
        )
        q_pair = qkv_ref[:, q_lanes] * scale
        v_pair = qkv_ref[:, v_lanes]
        halves = []
        for half in range(2):
            mine = (lane // HEAD_DIM) == half
            scores = mm_t(jnp.where(mine, qkv_ref[:, k_lanes], 0), q_pair) + mask_ref[...]
            weight = jnp.exp(scores - jnp.max(scores, axis=0, keepdims=True))
            total = jnp.sum(weight, axis=0, keepdims=True)
            probs = (weight * (1.0 / total)).astype(LOW)
            probs_ref[0, 0, 2 * pair + half] = probs
            halves.append(t_mm(probs, v_pair))
        ctx_ref[:, q_lanes] = jnp.where(lane < HEAD_DIM, halves[0], halves[1]).astype(LOW)
    h1_ref[...] += mm(ctx_ref[...], wout_ref[...])

    @pl.when(group == GROUPS - 1)
    def _():
        @pl.loop(0, SEQ // ROWS)
        def _(i):
            rows = pl.ds(pl.multiple_of(i * ROWS, ROWS), ROWS)
            n, inverse = norm_parts(h1_ref[rows, :])
            n_ref[rows, :] = n
            inverse_ref[rows, :] = jnp.broadcast_to(inverse, (ROWS, PAIR))
            n1low_ref[rows, :] = (n * vec_ref[3:4, :] + vec_ref[4:5, :]).astype(LOW)

        n1t_ref[...] = jnp.transpose(n1low_ref[...])


def attention_forward(x, seg, weights, table):
    rows = x.shape[0]
    seqs = rows // SEQ
    row = pl.BlockSpec((SEQ, D), lambda b, g: (b, 0))
    return pl.pallas_call(
        attention_forward_kernel,
        grid=(seqs, GROUPS),
        in_specs=[
            row,
            pl.BlockSpec((D, TRIO), lambda b, g: (0, 1 + g)),
            pl.BlockSpec((GROUP, D), lambda b, g: (g, 0)),
            pl.BlockSpec((8, D), lambda b, g: (0, 0)),
            pl.BlockSpec((seqs, SEQ), lambda b, g: (0, 0)),
        ],
        out_specs=[
            pl.BlockSpec((SEQ, TRIO), lambda b, g: (b, g)),
            pl.BlockSpec((SEQ, GROUP), lambda b, g: (b, g)),
            pl.BlockSpec((1, 1, GROUP // HEAD_DIM, SEQ, SEQ), lambda b, g: (b, g, 0, 0, 0)),
            pl.BlockSpec((1, D, SEQ), lambda b, g: (b, 0, 0)),
            row,
            pl.BlockSpec((SEQ, PAIR), lambda b, g: (b, 0)),
            row,
            pl.BlockSpec((D, SEQ), lambda b, g: (0, b)),
        ],
        out_shape=[
            like((rows, 3 * D), LOW),
            like((rows, D), LOW),
            like((seqs, GROUPS, GROUP // HEAD_DIM, SEQ, SEQ), LOW),
            like((seqs, D, SEQ), LOW),
            like((rows, D), F32),
            like((rows, PAIR), F32),
            like((rows, D), LOW),
            like((D, rows), LOW),
        ],
        scratch_shapes=[pltpu.VMEM((SEQ, SEQ), F32), pltpu.VMEM((SEQ, D), F32)],
        compiler_params=pltpu.CompilerParams(vmem_limit_bytes=VMEM),
        cost_estimate=cost(rows * (8 * D * D + 4 * D * SEQ), 36 * MIB, rows * SEQ * HEADS),
        name="attention_forward",
    )(x, weights, weights, table, seg)


def attention_backward_kernel(
    unit, core_ref, xt_ref, qkv_ref, ctx_ref, dctx_ref, probs_ref, vec_in_ref, keep_in_ref, send_in_ref,
    keep_ref, send_ref, dqkv_ref, vec_ref,
    ds_ref, acc_ref,
):
    row, seqs = pl.program_id(1), pl.num_programs(1)
    head_of = lax.broadcasted_iota(jnp.int32, (8, GROUP), 1) // HEAD_DIM
    picks = (head_of == lax.broadcasted_iota(jnp.int32, (8, GROUP), 0)).astype(LOW)
    product = ctx_ref[...].astype(F32) * dctx_ref[...].astype(F32)
    high = product.astype(LOW)
    inner = mm_t(picks, high) + mm_t(picks, (product - high.astype(F32)).astype(LOW))
    lane = lax.broadcasted_iota(jnp.int32, (1, PAIR), 1)
    first = lane < HEAD_DIM
    scale = jnp.asarray(HEAD_DIM**-0.5, LOW)
    tiles = [slice(i, i + KT) for i in range(0, SEQ, KT)]
    for pair in range(GROUP // PAIR):
        q_lanes, k_lanes, v_lanes = (
            slice(part * GROUP + pair * PAIR, part * GROUP + (pair + 1) * PAIR) for part in range(3)
        )
        q_pair = qkv_ref[:, q_lanes] * scale
        k_pair = qkv_ref[:, k_lanes] * scale
        dctx_pair = dctx_ref[:, q_lanes]
        dq, dk, dv = [], [], []
        for half in range(2):
            mine = (lane // HEAD_DIM) == half
            head = 2 * pair + half
            dk_tiles, dv_tiles = [], []
            for keys in tiles:
                probs = probs_ref[0, 0, head, keys, :]
                d_probs = mm_t(jnp.where(mine, qkv_ref[keys, v_lanes], 0), dctx_pair)
                d_scores = (probs.astype(F32) * (d_probs - inner[head : head + 1, :])).astype(LOW)
                ds_ref[half, keys, :] = d_scores
                dv_tiles.append(mm(probs, dctx_pair))
                dk_tiles.append(mm(d_scores, q_pair))
            dk.append(dk_tiles)
            dv.append(dv_tiles)
            dq.append([t_mm(ds_ref[half, :, rows], k_pair) for rows in tiles])
        for i, rows in enumerate(tiles):
            dqkv_ref[rows, q_lanes] = jnp.where(first, dq[0][i], dq[1][i]).astype(LOW)
            dqkv_ref[rows, k_lanes] = jnp.where(first, dk[0][i], dk[1][i]).astype(LOW)
            dqkv_ref[rows, v_lanes] = jnp.where(first, dv[0][i], dv[1][i]).astype(LOW)
    dqkv = dqkv_ref[...]
    product = mm(xt_ref[0], dqkv)
    bias_q = column_sum(dqkv[:, :GROUP].astype(F32))
    bias_v = column_sum(dqkv[:, 2 * GROUP :].astype(F32))

    @pl.when(row == 0)
    def _():
        acc_ref[...] = product
        vec_ref[...] = vec_in_ref[...]
        vec_ref[0:1, :] = bias_q
        vec_ref[1:2, :] = bias_v

    @pl.when(row > 0)
    def _():
        acc_ref[...] += product
        vec_ref[0:1, :] += bias_q
        vec_ref[1:2, :] += bias_v

    @pl.when(row == seqs - 1)
    def _():
        keep_ref[...], send_ref[...] = split_cores(acc_ref[...], core_ref[0], unit)


def attention_backward(unit, core, xt, qkv, ctx, probs, dctx, table, keep, send):
    rows = ctx.shape[0]
    seqs = rows // SEQ
    mine = lambda g, b: (b, g)
    return pl.pallas_call(
        lambda *refs: attention_backward_kernel(unit, *refs),
        grid=(GROUPS, seqs),
        in_specs=[
            pl.BlockSpec(memory_space=pltpu.SMEM),
            pl.BlockSpec((1, D, SEQ), lambda g, b: (b, 0, 0)),
            pl.BlockSpec((SEQ, TRIO), mine),
            pl.BlockSpec((SEQ, GROUP), mine),
            pl.BlockSpec((SEQ, GROUP), mine),
            pl.BlockSpec((1, 1, GROUP // HEAD_DIM, SEQ, SEQ), lambda g, b: (b, g, 0, 0, 0)),
            pl.BlockSpec((8, GROUP), lambda g, b: (0, g)),
            pl.BlockSpec(memory_space=pl.ANY),
            pl.BlockSpec(memory_space=pl.ANY),
        ],
        out_specs=[
            pl.BlockSpec((D // 2, TRIO), lambda g, b: (0, 1 + g)),
            pl.BlockSpec((D // 2, TRIO), lambda g, b: (0, 1 + g)),
            pl.BlockSpec((SEQ, TRIO), mine),
            pl.BlockSpec((8, GROUP), lambda g, b: (0, g)),
        ],
        out_shape=[like((D // 2, SET), LOW)] * 2 + [like((rows, 3 * D), LOW), like((8, D), F32)],
        input_output_aliases={6: 3, 7: 0, 8: 1},
        scratch_shapes=[pltpu.VMEM((2, SEQ, SEQ), LOW), pltpu.VMEM((D, TRIO), F32)],
        compiler_params=pltpu.CompilerParams(vmem_limit_bytes=VMEM),
        cost_estimate=cost(rows * (6 * D * D + 8 * D * SEQ), 36 * MIB, 0),
        name="attention_backward",
    )(core, xt, qkv, ctx, dctx, probs, table, keep, send)


def input_grad_kernel(da_ref, dqkv_ref, *refs):
    total = da_ref[...].astype(F32)
    for g in range(GROUPS):
        total += mm_t(dqkv_ref[:, g * TRIO : (g + 1) * TRIO], refs[g][...])
    refs[GROUPS][...] = total.astype(LOW)


def input_grad(da, dqkv, weights):
    rows = da.shape[0]
    return pl.pallas_call(
        input_grad_kernel,
        grid=(rows // ROWS,),
        in_specs=[
            pl.BlockSpec((ROWS, D), lambda i: (i, 0)),
            pl.BlockSpec((ROWS, 3 * D), lambda i: (i, 0)),
            *(pl.BlockSpec((D, TRIO), lambda i, g=g: (0, 1 + g)) for g in range(GROUPS)),
        ],
        out_specs=pl.BlockSpec((ROWS, D), lambda i: (i, 0)),
        out_shape=like((rows, D), LOW),
        compiler_params=pltpu.CompilerParams(vmem_limit_bytes=VMEM),
        cost_estimate=cost(6 * rows * D * D, 13 * MIB, 0),
        name="input_grad",
    )(da, dqkv, *[weights] * GROUPS)


def norm_parts(hidden):
    mean = jnp.mean(hidden, axis=1, keepdims=True)
    centred = hidden - mean
    inverse = lax.rsqrt(jnp.mean(centred * centred, axis=1, keepdims=True) + EPS)
    return centred * inverse, inverse


def norm_back(grad, gain, normed, inverse):
    scaled = grad * gain
    mean = jnp.mean(scaled, axis=1, keepdims=True)
    along = jnp.mean(scaled * normed, axis=1, keepdims=True)
    return inverse * (scaled - mean - normed * along)


def column_sum(array):
    return jnp.sum(array, axis=0, keepdims=True)


def gelu_and_slope(v):
    square = v * v
    bent = jnp.tanh(v * (ROOT + ROOT * CUBE * square))
    half = 0.5 + 0.5 * bent
    act = v * half
    slope = half + act * (1.0 - half) * (2.0 * ROOT + 6.0 * ROOT * CUBE * square)
    return act, slope


def order_outer(block_ref, out_ref, unit):
    for o in range(block_ref.shape[0] // unit):
        for j in range(CHUNKS):
            to = (o * CHUNKS + j) * unit
            out_ref[to : to + unit, :] = block_ref[o * unit : (o + 1) * unit, j * D : (j + 1) * D]


def ffn_forward_kernel(
    unit, n1low_ref, outer_ref, wi_ref, bi_ref, vec_ref, n_hbm, cot_hbm,
    slope_ref, gwo_ref, sums_ref, out_hbm, db_hbm, dh2_hbm,
    n_ref, cot_ref, h2_ref, wo_ref, act_ref, out_ref, db_ref, dh2_ref, sem,
):
    step = pl.program_id(0)
    tiles = [slice(i, i + ROWS) for i in range(0, h2_ref.shape[0], ROWS)]
    loads = [
        pltpu.make_async_copy(n_hbm, n_ref, sem.at[0]),
        pltpu.make_async_copy(cot_hbm, cot_ref, sem.at[1]),
    ]
    stores = [
        pltpu.make_async_copy(out_ref, out_hbm, sem.at[2]),
        pltpu.make_async_copy(db_ref, db_hbm, sem.at[3]),
        pltpu.make_async_copy(dh2_ref, dh2_hbm, sem.at[4]),
    ]

    @pl.when(step == 0)
    def _():
        for copy in loads:
            copy.start()
        h2_ref[...] = jnp.zeros_like(h2_ref)

    @pl.when(step < CHUNKS)
    def _():
        order_outer(outer_ref, wo_ref, unit)
        for rows in tiles:
            pre = mm(n1low_ref[rows, :], wi_ref[...]) + bi_ref[...]
            act, slope = gelu_and_slope(pre)
            act = act.astype(LOW)
            act_ref[step, rows, :] = act
            slope_ref[rows, :] = slope.astype(LOW)
            h2_ref[rows, :] += mm(act, wo_ref[...])

    @pl.when(step == CHUNKS - 1)
    def _():
        for copy in loads:
            copy.wait()
        gain, shift = vec_ref[6:7, :], vec_ref[7:8, :]
        sums_ref[...] = jnp.zeros_like(sums_ref)

        @pl.loop(0, h2_ref.shape[0] // ROWS, unroll=2)
        def _(i):
            rows = pl.ds(pl.multiple_of(i * ROWS, ROWS), ROWS)
            n, inverse = norm_parts(
                h2_ref[rows, :] + (n_ref[rows, :] * vec_ref[3:4, :] + vec_ref[4:5, :] + vec_ref[5:6, :])
            )
            out_ref[rows, :] = (n * gain + shift).astype(LOW)
            cot = cot_ref[rows, :].astype(F32)
            dh2 = norm_back(cot, gain, n, inverse)
            dh2_ref[rows, :] = dh2
            db = dh2.astype(LOW)
            db_ref[rows, :] = db
            for j, new in enumerate((column_sum(db.astype(F32)), column_sum(cot * n), column_sum(cot))):
                sums_ref[5 + j : 6 + j, :] += new

        for copy in stores:
            copy.start()

    @pl.when(step >= CHUNKS)
    def _():
        grad = t_mm(act_ref[step - CHUNKS], db_ref[...]).astype(LOW)
        if len(gwo_ref.shape) == 2:
            gwo_ref[...] = grad
        else:
            _, _, sides, lines, deep, _ = gwo_ref.shape
            for i in range(CHUNK // deep):
                core, side, line = i % 2, i // 2 % sides, i // 2 // sides
                gwo_ref[core, 0, side, line] = grad[i * deep : (i + 1) * deep, :]

    @pl.when(step == 2 * CHUNKS - 1)
    def _():
        for copy in stores:
            copy.wait()


def ffn_forward(unit, normed, n1low, cot, rest, b_inner, table, sizes=None):
    rows = normed.shape[0]
    last = CHUNKS - 1
    now = lambda c: jnp.minimum(c, last)
    then = lambda c: jnp.maximum(c - CHUNKS, 0)
    eight = pl.BlockSpec((8, D), lambda c: (0, 0))
    if sizes is None:
        outer_shape = (FF, D)
        outer_block = pl.BlockSpec((CHUNK, D), lambda c: (then(c), 0))
    else:
        dps, lines, sides, cores = sizes
        deep = CHUNKS * unit
        held = CHUNK // (deep * sides * cores)
        outer_shape = (cores, dps, sides, lines, deep, D)
        outer_block = pl.BlockSpec(
            (cores, 1, sides, held, deep, D),
            lambda c: (0, then(c) * held // lines, 0, then(c) % (lines // held), 0, 0),
        )
    anywhere = pl.BlockSpec(memory_space=pl.ANY)
    return pl.pallas_call(
        lambda *refs: ffn_forward_kernel(unit, *refs),
        grid=(2 * CHUNKS,),
        in_specs=[
            pl.BlockSpec((rows, D), lambda c: (0, 0), pipeline_mode=pl.Buffered(1)),
            pl.BlockSpec((D // CHUNKS, FF), lambda c: (now(c), 0)),
            pl.BlockSpec((D, CHUNK), lambda c: (0, CHUNKS + now(c))),
            pl.BlockSpec((1, CHUNK), lambda c: (0, now(c))),
            eight,
            anywhere,
            anywhere,
        ],
        out_specs=[
            pl.BlockSpec((rows, CHUNK), lambda c: (0, now(c))),
            outer_block,
            eight,
            anywhere,
            anywhere,
            anywhere,
        ],
        out_shape=[
            like((rows, FF), LOW),
            like(outer_shape, LOW),
            like((8, D), F32),
            like((rows, D), LOW),
            like((rows, D), LOW),
            like((rows, D), F32),
        ],
        scratch_shapes=[
            pltpu.VMEM((rows, D), F32),
            pltpu.VMEM((rows, D), LOW),
            pltpu.VMEM((rows, D), F32),
            pltpu.VMEM((CHUNK, D), LOW),
            pltpu.VMEM((CHUNKS, rows, CHUNK), LOW),
            pltpu.VMEM((rows, D), LOW),
            pltpu.VMEM((rows, D), LOW),
            pltpu.VMEM((rows, D), F32),
            pltpu.SemaphoreType.DMA((5,)),
        ],
        compiler_params=pltpu.CompilerParams(vmem_limit_bytes=VMEM),
        cost_estimate=cost(6 * rows * D * FF, 34 * MIB, rows * FF),
        name="ffn_forward",
    )(n1low, rest, rest, b_inner, table, normed, cot)


def split_cores(grad, core, unit):
    rows = range(0, grad.shape[0], 2 * unit)
    even = jnp.concatenate([grad[i : i + unit] for i in rows], axis=0)
    odd = jnp.concatenate([grad[i + unit : i + 2 * unit] for i in rows], axis=0)
    return jnp.where(core == 0, even, odd).astype(LOW), jnp.where(core == 0, odd, even).astype(LOW)


def ffn_backward_kernel(
    unit, core_ref, n1t_ref, slope_ref, db_ref, outer_ref, wi_ref, dh2_hbm,
    keep_ref, send_ref, gbi_ref, dn1_ref,
    dpre_ref, wo_ref, dh2_ref, sem,
):
    step = pl.program_id(0)
    tiles = [slice(i, i + ROWS) for i in range(0, db_ref.shape[0], ROWS)]
    order_outer(outer_ref, wo_ref, unit)

    load = pltpu.make_async_copy(dh2_hbm, dh2_ref, sem)

    @pl.when(step == 0)
    def _():
        load.start()
        dn1_ref[...] = jnp.zeros_like(dn1_ref)

    @pl.when(step == CHUNKS - 1)
    def _():
        load.wait()
        dn1_ref[...] += dh2_ref[...]

    bias = jnp.zeros((1, CHUNK), F32)
    for rows in tiles:
        dpre = (mm_t(db_ref[rows, :], wo_ref[...]) * slope_ref[rows, :].astype(F32)).astype(LOW)
        dpre_ref[rows, :] = dpre
        bias += column_sum(dpre.astype(F32))
        dn1_ref[rows, :] += mm_t(dpre, wi_ref[...])
    gbi_ref[...] = bias
    keep_ref[...], send_ref[...] = split_cores(mm(n1t_ref[...], dpre_ref[...]), core_ref[0], unit)


def ffn_backward(unit, core, n1t, slope, db, dh2, rest):
    rows = db.shape[0]
    once = pl.BlockSpec((rows, D), lambda c: (0, 0), pipeline_mode=pl.Buffered(1))
    return pl.pallas_call(
        lambda *refs: ffn_backward_kernel(unit, *refs),
        grid=(CHUNKS,),
        in_specs=[
            pl.BlockSpec(memory_space=pltpu.SMEM),
            pl.BlockSpec((D, rows), lambda c: (0, 0), pipeline_mode=pl.Buffered(1)),
            pl.BlockSpec((rows, CHUNK), lambda c: (0, c)),
            once,
            pl.BlockSpec((D // CHUNKS, FF), lambda c: (c, 0)),
            pl.BlockSpec((D, CHUNK), lambda c: (0, CHUNKS + c)),
            pl.BlockSpec(memory_space=pl.ANY),
        ],
        out_specs=[
            pl.BlockSpec((D // 2, CHUNK), lambda c: (0, c)),
            pl.BlockSpec((D // 2, CHUNK), lambda c: (0, c)),
            pl.BlockSpec((1, CHUNK), lambda c: (0, c)),
            pl.BlockSpec((rows, D), lambda c: (0, 0)),
        ],
        out_shape=[like((D // 2, FF), LOW)] * 2 + [like((1, FF), F32), like((rows, D), F32)],
        scratch_shapes=[
            pltpu.VMEM((rows, CHUNK), LOW),
            pltpu.VMEM((CHUNK, D), LOW),
            pltpu.VMEM((rows, D), F32),
            pltpu.SemaphoreType.DMA,
        ],
        compiler_params=pltpu.CompilerParams(vmem_limit_bytes=VMEM),
        cost_estimate=cost(6 * rows * D * FF, 30 * MIB, 0),
        name="ffn_backward",
    )(core, n1t, slope, db, rest, rest, dh2)


def norm_backward_kernel(
    unit, core_ref, wout_ref, vec_ref, sums_in_ref, n_hbm, inverse_hbm, dn1_hbm, ctx_hbm,
    keep_ref, send_ref, sums_ref, dctx_hbm, da_hbm,
    n_ref, inverse_ref, dn1_ref, ctx_ref, da_ref, dctx_ref, load_sem, store_sem,
):
    tiles = [slice(i, i + ROWS) for i in range(0, n_ref.shape[0], ROWS)]
    pairs = ((n_hbm, n_ref), (inverse_hbm, inverse_ref), (dn1_hbm, dn1_ref), (ctx_hbm, ctx_ref))
    loads = [
        [pltpu.make_async_copy(a.at[rows, :], b.at[rows, :], load_sem.at[i, j]) for j, (a, b) in enumerate(pairs)]
        for i, rows in enumerate(tiles)
    ]
    stores = [
        [
            pltpu.make_async_copy(da_ref.at[rows, :], da_hbm.at[rows, :], store_sem.at[i, 0]),
            pltpu.make_async_copy(dctx_ref.at[rows, :], dctx_hbm.at[rows, :], store_sem.at[i, 1]),
        ]
        for i, rows in enumerate(tiles)
    ]
    for group in loads:
        for copy in group:
            copy.start()
    sums = [jnp.zeros((1, D), F32)] * 3
    for i, rows in enumerate([*tiles, None]):
        if rows is not None:
            for copy in loads[i]:
                copy.wait()
        if i > 0:
            dctx_ref[tiles[i - 1], :] = mm_t(da_ref[tiles[i - 1], :], wout_ref[...]).astype(LOW)
        if rows is not None:
            n = n_ref[rows, :]
            dn1 = dn1_ref[rows, :]
            da = norm_back(dn1, vec_ref[3:4, :], n, inverse_ref[rows, 0:1]).astype(LOW)
            da_ref[rows, :] = da
            new = (column_sum(da.astype(F32)), column_sum(dn1 * n), column_sum(dn1))
            sums = [a + b for a, b in zip(sums, new)]
            stores[i][0].start()
        if i > 0:
            stores[i - 1][1].start()
    keep_ref[...], send_ref[...] = split_cores(t_mm(ctx_ref[...], da_ref[...]), core_ref[0], unit)
    sums_ref[...] = sums_in_ref[...]
    for i in range(3):
        sums_ref[2 + i : 3 + i, :] = sums[i]
    for group in stores:
        for copy in group:
            copy.wait()


def norm_backward(unit, core, normed, inverse, dn1, ctx, weights, table, sums):
    rows = normed.shape[0]
    eight = pl.BlockSpec((8, D), lambda i: (0, 0))
    half = pl.BlockSpec((D // 2, D), lambda i: (0, 0))
    anywhere = pl.BlockSpec(memory_space=pl.ANY)
    return pl.pallas_call(
        lambda *refs: norm_backward_kernel(unit, *refs),
        grid=(1,),
        in_specs=[
            pl.BlockSpec(memory_space=pltpu.SMEM),
            pl.BlockSpec((D, D), lambda i: (0, 0)),
            eight,
            eight,
        ]
        + [anywhere] * 4,
        out_specs=[half, half, eight, anywhere, anywhere],
        out_shape=[like((D // 2, SET), LOW)] * 2
        + [like((8, D), F32), like((rows, D), LOW), like((rows, D), LOW)],
        scratch_shapes=[
            pltpu.VMEM((rows, D), F32),
            pltpu.VMEM((rows, PAIR), F32),
            pltpu.VMEM((rows, D), F32),
            pltpu.VMEM((rows, D), LOW),
            pltpu.VMEM((rows, D), LOW),
            pltpu.VMEM((rows, D), LOW),
            pltpu.SemaphoreType.DMA((rows // ROWS, 4)),
            pltpu.SemaphoreType.DMA((rows // ROWS, 2)),
        ],
        compiler_params=pltpu.CompilerParams(vmem_limit_bytes=VMEM),
        cost_estimate=cost(4 * rows * D * D, 17 * MIB, 0),
        name="norm_backward",
    )(core, weights, table, sums, normed, inverse, dn1, ctx)


def after(values, *others):
    return lax.optimization_barrier((values, others))[0]


def whole(array):
    return pl.BlockSpec(array.shape, lambda *_: (0,) * len(array.shape))


def pack_kernel(wq_ref, wk_ref, wv_ref, wout_ref, wi_ref, wo_ref, *refs):
    vectors, (set_ref, rest_ref) = refs[:9], refs[9:]
    unit = wq_ref.shape[0]
    set_ref[:, :D] = wout_ref[...]
    for g in range(GROUPS):
        for part, ref in enumerate((wq_ref, wk_ref, wv_ref)):
            to = D + g * TRIO + part * GROUP
            set_ref[:, to : to + GROUP] = ref[:, g * GROUP : (g + 1) * GROUP]
    table = jnp.zeros((unit, PAIR), F32)
    row = lax.broadcasted_iota(jnp.int32, (unit, PAIR), 0)
    for i, ref in enumerate(vectors):
        size = ref.shape[1]
        line = jnp.concatenate([ref[...].astype(F32), jnp.zeros((1, PAIR - size), F32)], axis=1)
        table = jnp.where(row == i, line, table)
    set_ref[:, 4 * D :] = table.astype(LOW)
    for j in range(CHUNKS):
        rest_ref[:, j * D : (j + 1) * D] = wo_ref[j * unit : (j + 1) * unit, :]
    rest_ref[:, FF:] = wi_ref[...]


def pack(wq, wk, wv, wout, wi, wo, vectors):
    unit = wq.shape[0]
    args = (wq, wk, wv, wout, wi, wo, *(v.reshape(1, -1) for v in vectors))
    shapes = [like((unit, SET), LOW), like((unit, 2 * FF), LOW)]
    return pl.pallas_call(
        pack_kernel,
        grid=(1,),
        in_specs=[whole(a) for a in args],
        out_specs=[whole(a) for a in shapes],
        out_shape=shapes,
        compiler_params=pltpu.CompilerParams(vmem_limit_bytes=VMEM),
        name="pack",
    )(*args)


def stack_kernel(*refs):
    for i, ref in enumerate(refs[:-1]):
        refs[-1][i] = ref[...]


def stack(pieces):
    shape = like((len(pieces), *pieces[0].shape), pieces[0].dtype)
    return pl.pallas_call(
        stack_kernel,
        grid=(1,),
        in_specs=[pl.BlockSpec(memory_space=pltpu.VMEM)] * len(pieces),
        out_specs=whole(shape),
        out_shape=shape,
        compiler_params=pltpu.CompilerParams(vmem_limit_bytes=8 * MIB),
        name="stack",
    )(*pieces)


class Slice:
    def __init__(self):
        self.sizes = tuple(lax.axis_size(name) for name in AXES)
        self.dp, self.line, self.side, self.core = (lax.axis_index(name) for name in AXES)
        self.offsets = [(a, b) for a in range(self.sizes[0]) for b in range(self.sizes[2])]

    def to_core(self, array):
        return lax.ppermute(array, "core", [(0, 1), (1, 0)])

    def to_plane(self, array, offset):
        dps, _, sides, _ = self.sizes
        pairs = [
            (i * sides + j, (i + offset[0]) % dps * sides + (j + offset[1]) % sides)
            for i in range(dps)
            for j in range(sides)
        ]
        return lax.ppermute(array, ("dp", "side"), pairs)

    def to_line(self, array, shift):
        count = self.sizes[1]
        return lax.ppermute(array, "line", [(i, (i + shift) % count) for i in range(count)])

    def gather(self, mine):
        dps, lines, sides, _ = self.sizes
        unit, columns = mine.shape
        line = stack([mine] + [self.to_line(mine, s) for s in range(1, lines)])
        here = [line if o == (0, 0) else self.to_plane(line, o) for o in self.offsets]
        there = [self.to_core(a) for a in here]
        place = jnp.stack([self.dp, self.line, self.side, self.core]).astype(jnp.int32)
        pieces = here + there

        wide = 5 * PAIR

        def kernel(place_ref, *refs):
            out_ref = refs[-1]
            for i in range(len(pieces)):
                a, b = self.offsets[i % len(here)]
                dp = lax.rem(place_ref[0] + dps - a, dps)
                side = lax.rem(place_ref[2] + sides - b, sides)
                core = place_ref[3] if i < len(here) else 1 - place_ref[3]
                for s in range(lines):
                    along = lax.rem(place_ref[1] + lines - s, lines)
                    out_ref[((dp * lines + along) * sides + side) * 2 + core] = refs[i][s]

        count = dps * lines * sides * 2
        return pl.pallas_call(
            kernel,
            grid=(columns // wide,),
            in_specs=[pl.BlockSpec(memory_space=pltpu.SMEM)]
            + [pl.BlockSpec((lines, unit, wide), lambda i: (0, 0, i))] * len(pieces),
            out_specs=pl.BlockSpec((count, unit, wide), lambda i: (0, 0, i)),
            out_shape=like((count, unit, columns), mine.dtype),
            compiler_params=pltpu.CompilerParams(vmem_limit_bytes=VMEM),
            name="place",
        )(place, *pieces).reshape(-1, columns)


    def chips_sum(self, grad):
        return lax.psum_scatter(grad.reshape(-1, *grad.shape[3:]), ("core", "dp", "side"), scatter_dimension=0)

    def line_sum(self, grad):
        return lax.psum_scatter(grad, "line", scatter_dimension=0)

    def join_cores(self, keep, send, unit):
        keep, send = (part.reshape(-1, 1, unit, part.shape[1]) for part in (keep, send))
        mine = self.core == 0
        pair = [jnp.where(mine, keep, send), jnp.where(mine, send, keep)]
        return jnp.concatenate(pair, axis=1).reshape(-1, keep.shape[3])


    def block(self, grad, got, dp, side, columns=None):
        dps, lines, sides, _ = self.sizes
        first, last = columns or (0, grad.shape[1])
        start = (0 if dp is None else dp, 0, 0 if side is None else side, 0, first)
        size = (dps if dp is None else 1, lines, sides if side is None else 1)
        total = 0.0
        for part in (grad, got):
            part = part.reshape(dps, lines, sides, -1, grad.shape[1])
            total += lax.dynamic_slice(part, start, (*size, part.shape[3], last - first)).astype(F32)
        return total


    def plane_messages(self, grad, got):
        dps, _, sides, _ = self.sizes
        return [
            self.block(grad, got, lax.rem(self.dp + a, dps), lax.rem(self.side + b, sides))[0, :, 0].astype(LOW)
            for a, b in self.offsets[1:]
        ]

    def plane_exchange(self, messages):
        return [self.to_plane(m, o) for m, o in zip(messages, self.offsets[1:])]

    def plane_done(self, grad, got, parts):
        total = self.block(grad, got, self.dp, self.side)[0, :, 0]
        return self.along_line((total + sum(p.astype(F32) for p in parts)).astype(LOW))


    def halves(self, grad):
        columns = grad.shape[1]
        return (0, columns // 2), (columns // 2, columns)

    def first_messages(self, grad, got):
        one, two = self.halves(grad)
        return (
            self.block(grad, got, None, 1 - self.side, one).astype(LOW),
            self.block(grad, got, 1 - self.dp, None, two).astype(LOW),
        )

    def first_exchange(self, messages):
        return self.to_plane(messages[0], (0, 1)), self.to_plane(messages[1], (1, 0))

    def second_messages(self, grad, got, more):
        one, two = self.halves(grad)
        a = self.block(grad, got, 1 - self.dp, self.side, one)
        b = self.block(grad, got, self.dp, 1 - self.side, two)
        a += lax.dynamic_slice_in_dim(more[0], 1 - self.dp, 1, 0).astype(F32)
        b += lax.dynamic_slice_in_dim(more[1], 1 - self.side, 1, 2).astype(F32)
        return a.astype(LOW), b.astype(LOW)

    def second_exchange(self, messages):
        return self.to_plane(messages[0], (1, 0)), self.to_plane(messages[1], (0, 1))

    def second_done(self, grad, got, more, most):
        one, two = self.halves(grad)
        a = self.block(grad, got, self.dp, self.side, one) + most[0].astype(F32)
        b = self.block(grad, got, self.dp, self.side, two) + most[1].astype(F32)
        a += lax.dynamic_slice_in_dim(more[0], self.dp, 1, 0).astype(F32)
        b += lax.dynamic_slice_in_dim(more[1], self.side, 1, 2).astype(F32)
        return self.along_line(jnp.concatenate([a[0, :, 0], b[0, :, 0]], axis=2).astype(LOW))

    def along_line(self, total):
        lines = self.sizes[1]
        at = [lax.rem(self.line + s, lines) for s in range(lines)]
        return [lax.dynamic_index_in_dim(total, i, 0, keepdims=False) for i in at]

    def line_exchange(self, messages):
        return messages[:1] + [self.to_line(m, s) for s, m in enumerate(messages) if s]


def finish_kernel(count, *refs):
    parts, (wout_ref, wq_ref, wk_ref, wv_ref), vectors = refs[:count], refs[count : count + 4], refs[count + 4 :]
    total = sum(ref[...].astype(F32) for ref in parts)
    wout_ref[...] = total[:, :D]
    for g in range(GROUPS):
        for part, ref in enumerate((wq_ref, wk_ref, wv_ref)):
            at = D + g * TRIO + part * GROUP
            ref[:, g * GROUP : (g + 1) * GROUP] = total[:, at : at + GROUP]
    for i, ref in enumerate(vectors):
        ref[...] = total[i : i + 1, 4 * D : 4 * D + ref.shape[1]]


def finish(parts):
    unit = parts[0].shape[0]
    shapes = [like((unit, D), F32)] * 4 + [like((1, unit), F32)] * 8 + [like((1, CHUNKS * unit), F32)]
    outs = pl.pallas_call(
        lambda *refs: finish_kernel(len(parts), *refs),
        grid=(1,),
        in_specs=[pl.BlockSpec(memory_space=pltpu.VMEM)] * len(parts),
        out_specs=[whole(a) for a in shapes],
        out_shape=shapes,
        compiler_params=pltpu.CompilerParams(vmem_limit_bytes=8 * MIB),
        name="finish",
    )(*parts)
    return outs[:4], [v.reshape(-1) for v in outs[4:]]


def vector_rows(table, b_inner, count):
    unit = D // count
    eight = table.reshape(8, count, unit).transpose(1, 0, 2)
    inner = b_inner.reshape(count, 1, CHUNKS * unit)
    eight = jnp.pad(eight, ((0, 0), (0, 0), (0, PAIR - unit)))
    inner = jnp.pad(inner, ((0, 0), (0, unit - 9), (0, PAIR - CHUNKS * unit)))
    return jnp.concatenate([eight, inner], axis=1).astype(LOW)


def on_device(block_input, segment_ids, cotangent, *params):
    w_query, w_key, w_value, w_out, w_inner, w_outer = (params[i] for i in MATRICES)
    vectors = [params[i] for i in VECTORS]
    unit = w_query.shape[0]
    count = D // unit
    mesh = Slice()
    quick = mesh.sizes == (2, 4, 2, 2) and unit == 24
    x = block_input.reshape(-1, D)
    cot = cotangent.reshape(-1, D)

    if quick:
        mine, rest_mine = pack(w_query, w_key, w_value, w_out, w_inner, w_outer, vectors)
        rest = lax.all_gather(rest_mine, AXES, axis=0, tiled=True)
        weights = mesh.gather(mine)
        side = weights[:, 4 * D :].reshape(count, unit, PAIR)
        table = side[:, :8, :unit].transpose(1, 0, 2).reshape(8, D).astype(F32)
        b_inner = side[:, 8, : CHUNKS * unit].reshape(1, FF).astype(F32)
    else:
        trios = [w[:, g : g + GROUP] for g in range(0, D, GROUP) for w in (w_query, w_key, w_value)]
        full = lax.all_gather(jnp.concatenate([w_out, *trios, w_inner], axis=1), AXES, axis=0, tiled=True)
        outer = lax.all_gather(w_outer, AXES, axis=0, tiled=True)
        vector = lax.all_gather(jnp.concatenate(vectors), AXES, axis=0).astype(F32)
        weights = full[:, : 4 * D]
        table = jnp.concatenate([vector[:, i * unit : (i + 1) * unit].reshape(1, D) for i in range(8)])
        b_inner = vector[:, 8 * unit :].reshape(1, FF)
        unit = 24
        outer = outer.reshape(-1, CHUNKS, unit, D).transpose(0, 2, 1, 3).reshape(D, FF)
        rest = jnp.concatenate([outer, full[:, 4 * D :]], axis=1)

    core = mesh.core[None].astype(jnp.int32)
    qkv, ctx, probs, xt, normed, inverse, n1low, n1t = attention_forward(x, segment_ids, weights, table)
    slope, g_outer, sums, result, db, dh2 = ffn_forward(
        unit, normed, n1low, cot, rest, b_inner, table, mesh.sizes if quick else None
    )
    if quick:
        db = after(db, g_outer)
        g_outer = mesh.chips_sum(g_outer)
    keep, send, g_b_inner, dn1 = ffn_backward(unit, core, n1t, slope, db, dh2, rest)
    if not quick:
        g_inner = mesh.join_cores(keep, send, unit)
        keep, send, sums, dctx, da = norm_backward(unit, core, normed, inverse, dn1, ctx, weights, table, sums)
        keep, send, dqkv, sums = attention_backward(unit, core, xt, qkv, ctx, probs, dctx, sums, keep, send)
        late = mesh.join_cores(keep, send, unit)
        dx = input_grad(da, dqkv, weights)
        wide = jnp.concatenate([late[:, : 4 * D], g_inner], axis=1)
        wide = lax.psum_scatter(wide, AXES, scatter_dimension=0, tiled=True).astype(F32)
        g_outer = lax.psum_scatter(g_outer, AXES, scatter_dimension=0, tiled=True).astype(F32)
        vector = jnp.concatenate([*sums.reshape(8, count, -1), g_b_inner.reshape(count, -1)], axis=1)
        vector = lax.psum_scatter(vector.reshape(-1), AXES, scatter_dimension=0, tiled=True)
        size = D // count
        vectors = [vector[i * size : (i + 1) * size] for i in range(8)] + [vector[8 * size :]]
        matrices = [wide[:, :D]] + [
            jnp.concatenate([wide[:, g + part : g + part + GROUP] for g in range(D, 4 * D, TRIO)], axis=1)
            for part in range(0, TRIO, GROUP)
        ]
        g_inner = wide[:, 4 * D :]
    else:
        g_inner = keep
        dn1 = after(dn1, send)
        got = mesh.to_core(send)
        keep, send, sums, dctx, da = norm_backward(unit, core, normed, inverse, dn1, ctx, weights, table, sums)
        inner_got, sums = after((got, sums), dctx)
        message = mesh.first_messages(g_inner, inner_got)
        sums = after(sums, message)
        more = mesh.first_exchange(message)
        late, send, dqkv, sums = attention_backward(unit, core, xt, qkv, ctx, probs, dctx, sums, keep, send)
        late, send, more, g_outer = after((late, send, more, g_outer), dqkv)
        g_outer = mesh.line_sum(g_outer)
        g_b_inner = after(g_b_inner, dqkv)
        vector = vector_rows(sums, g_b_inner, count).reshape(-1, 2, unit, PAIR)
        at = (mesh.core, 1 - mesh.core)
        vector = [lax.dynamic_index_in_dim(vector, i, 1, keepdims=False).reshape(-1, PAIR) for i in at]
        late = lax.dynamic_update_slice(late, vector[0], (0, 4 * D))
        send = lax.dynamic_update_slice(send, vector[1], (0, 4 * D))
        got = mesh.to_core(send)
        message = mesh.second_messages(g_inner, inner_got, more)
        got, dqkv = after((got, dqkv), message)
        most = mesh.second_exchange(message)
        message = mesh.plane_messages(late, got)
        most, dqkv = after((most, dqkv), message)
        parts = mesh.plane_exchange(message)
        lines = mesh.line_exchange(mesh.second_done(g_inner, inner_got, more, most))
        dx = input_grad(da, dqkv, weights)
        parts, g_inner, g_outer = after((parts, lines, g_outer), dx)
        message = mesh.plane_done(late, got, parts)
        g_outer, g_inner = after((g_outer, g_inner), message)
        matrices, vectors = finish(mesh.line_exchange(message))
        g_outer = g_outer.astype(F32)
        g_inner = sum(p.astype(F32) for p in g_inner)
    g_out, *matrices = matrices

    shards = [None] * len(params)
    for i, value in zip(MATRICES, (*matrices, g_out, g_inner, g_outer)):
        shards[i] = value
    for i, value in zip(VECTORS, vectors):
        shards[i] = value
    return (result.reshape(block_input.shape), dx.reshape(block_input.shape), *shards)


def solution(mesh):
    sizes = (mesh.shape["dp"], mesh.shape["fsdp"] // 4, 2, 2)
    parts = Mesh(np.asarray(mesh.devices).reshape(sizes), AXES)
    vector, matrix, rows = P(AXES), P(AXES, None), P(AXES, None, None)
    params = tuple(vector if i in VECTORS else matrix for i in range(15))
    return jax.shard_map(
        on_device,
        mesh=parts,
        in_specs=(rows, matrix, rows) + params,
        out_specs=(rows, rows) + params,
        check_vma=False,
    )
```

```python
import jax
import jax.numpy as jnp
import numpy as np
from jax import lax
from jax.experimental import pallas as pl
from jax.experimental.pallas import tpu as pltpu
from jax.sharding import Mesh, PartitionSpec as P

D = 768
FF = 3072
HEADS = 12
HEAD_DIM = 64
SEQ = 512
GROUP = 256
GROUPS = D // GROUP
TRIO = 3 * GROUP
PAIR = 128
SET = 4 * D + PAIR
KT = 256
CHUNK = 768
CHUNKS = FF // CHUNK
ROWS = 256
EPS = 1e-05
SHARE = 1.0
ROOT = 0.7978845608028654
CUBE = 0.044715
LOW = jnp.bfloat16
F32 = jnp.float32
MIB = 1 << 20
VMEM = 63 * MIB
MATRICES = (0, 2, 3, 5, 9, 11)
VECTORS = (1, 4, 6, 7, 8, 12, 13, 14, 10)
AXES = ("dp", "line", "side", "core")


def mm(a, b):
    return lax.dot_general(a, b, (((1,), (0,)), ((), ())), preferred_element_type=F32)


def mm_t(a, b):
    return lax.dot_general(a, b, (((1,), (1,)), ((), ())), preferred_element_type=F32)


def t_mm(a, b):
    return lax.dot_general(a, b, (((0,), (0,)), ((), ())), preferred_element_type=F32)


def cost(flops, moved, transcendentals):
    return pl.CostEstimate(
        flops=int(SHARE * flops),
        bytes_accessed=int(SHARE * moved),
        transcendentals=int(SHARE * transcendentals),
    )


def like(shape, kind):
    return jax.ShapeDtypeStruct(shape, kind)


def attention_forward_kernel(
    x_ref, w_ref, wout_ref, vec_ref, seg_ref,
    qkv_ref, ctx_ref, probs_ref, xt_ref, n_ref, inverse_ref, n1low_ref, n1t_ref, mask_ref, h1_ref,
):
    group = pl.program_id(1)
    x = x_ref[...]
    column = pl.ds(pl.multiple_of(group * GROUP, GROUP), GROUP)
    qkv_ref[:, :GROUP] = (mm(x, w_ref[:, :GROUP]) + vec_ref[0:1, column]).astype(LOW)
    qkv_ref[:, GROUP : 2 * GROUP] = mm(x, w_ref[:, GROUP : 2 * GROUP]).astype(LOW)
    qkv_ref[:, 2 * GROUP :] = (mm(x, w_ref[:, 2 * GROUP :]) + vec_ref[1:2, column]).astype(LOW)

    @pl.when(group == 0)
    def _():
        number = seg_ref[pl.ds(pl.program_id(0), 1), :].astype(F32)
        column = jnp.transpose(jnp.broadcast_to(number, (PAIR, SEQ)))[:, :1]
        mask_ref[...] = jnp.where(column == number, 0.0, -1e30)
        xt_ref[0] = jnp.transpose(x)
        h1_ref[...] = x.astype(F32) + vec_ref[2:3, :]

    lane = lax.broadcasted_iota(jnp.int32, (1, PAIR), 1)
    scale = jnp.asarray(HEAD_DIM**-0.5, LOW)
    for pair in range(GROUP // PAIR):
        q_lanes, k_lanes, v_lanes = (
            slice(part * GROUP + pair * PAIR, part * GROUP + (pair + 1) * PAIR) for part in range(3)
        )
        q_pair = qkv_ref[:, q_lanes] * scale
        v_pair = qkv_ref[:, v_lanes]
        halves = []
        for half in range(2):
            mine = (lane // HEAD_DIM) == half
            scores = mm_t(jnp.where(mine, qkv_ref[:, k_lanes], 0), q_pair) + mask_ref[...]
            weight = jnp.exp(scores - jnp.max(scores, axis=0, keepdims=True))
            total = jnp.sum(weight, axis=0, keepdims=True)
            probs = (weight * (1.0 / total)).astype(LOW)
            probs_ref[0, 0, 2 * pair + half] = probs
            halves.append(t_mm(probs, v_pair))
        ctx_ref[:, q_lanes] = jnp.where(lane < HEAD_DIM, halves[0], halves[1]).astype(LOW)
    h1_ref[...] += mm(ctx_ref[...], wout_ref[...])

    @pl.when(group == GROUPS - 1)
    def _():
        @pl.loop(0, SEQ // ROWS)
        def _(i):
            rows = pl.ds(pl.multiple_of(i * ROWS, ROWS), ROWS)
            n, inverse = norm_parts(h1_ref[rows, :])
            n_ref[rows, :] = n
            inverse_ref[rows, :] = jnp.broadcast_to(inverse, (ROWS, PAIR))
            n1low_ref[rows, :] = (n * vec_ref[3:4, :] + vec_ref[4:5, :]).astype(LOW)

        n1t_ref[...] = jnp.transpose(n1low_ref[...])


def attention_forward(x, seg, weights, table):
    rows = x.shape[0]
    seqs = rows // SEQ
    row = pl.BlockSpec((SEQ, D), lambda b, g: (b, 0))
    return pl.pallas_call(
        attention_forward_kernel,
        grid=(seqs, GROUPS),
        in_specs=[
            row,
            pl.BlockSpec((D, TRIO), lambda b, g: (0, 1 + g)),
            pl.BlockSpec((GROUP, D), lambda b, g: (g, 0)),
            pl.BlockSpec((8, D), lambda b, g: (0, 0)),
            pl.BlockSpec((seqs, SEQ), lambda b, g: (0, 0)),
        ],
        out_specs=[
            pl.BlockSpec((SEQ, TRIO), lambda b, g: (b, g)),
            pl.BlockSpec((SEQ, GROUP), lambda b, g: (b, g)),
            pl.BlockSpec((1, 1, GROUP // HEAD_DIM, SEQ, SEQ), lambda b, g: (b, g, 0, 0, 0)),
            pl.BlockSpec((1, D, SEQ), lambda b, g: (b, 0, 0)),
            row,
            pl.BlockSpec((SEQ, PAIR), lambda b, g: (b, 0)),
            row,
            pl.BlockSpec((D, SEQ), lambda b, g: (0, b)),
        ],
        out_shape=[
            like((rows, 3 * D), LOW),
            like((rows, D), LOW),
            like((seqs, GROUPS, GROUP // HEAD_DIM, SEQ, SEQ), LOW),
            like((seqs, D, SEQ), LOW),
            like((rows, D), F32),
            like((rows, PAIR), F32),
            like((rows, D), LOW),
            like((D, rows), LOW),
        ],
        scratch_shapes=[pltpu.VMEM((SEQ, SEQ), F32), pltpu.VMEM((SEQ, D), F32)],
        compiler_params=pltpu.CompilerParams(vmem_limit_bytes=VMEM),
        cost_estimate=cost(rows * (8 * D * D + 4 * D * SEQ), 36 * MIB, rows * SEQ * HEADS),
        name="attention_forward",
    )(x, weights, weights, table, seg)


def attention_backward_kernel(
    unit, core_ref, xt_ref, qkv_ref, ctx_ref, dctx_ref, probs_ref, vec_in_ref, keep_in_ref, send_in_ref,
    keep_ref, send_ref, dqkv_ref, vec_ref,
    ds_ref, acc_ref,
):
    row, seqs = pl.program_id(1), pl.num_programs(1)
    head_of = lax.broadcasted_iota(jnp.int32, (8, GROUP), 1) // HEAD_DIM
    picks = (head_of == lax.broadcasted_iota(jnp.int32, (8, GROUP), 0)).astype(LOW)
    product = ctx_ref[...].astype(F32) * dctx_ref[...].astype(F32)
    high = product.astype(LOW)
    inner = mm_t(picks, high) + mm_t(picks, (product - high.astype(F32)).astype(LOW))
    lane = lax.broadcasted_iota(jnp.int32, (1, PAIR), 1)
    first = lane < HEAD_DIM
    scale = jnp.asarray(HEAD_DIM**-0.5, LOW)
    tiles = [slice(i, i + KT) for i in range(0, SEQ, KT)]
    for pair in range(GROUP // PAIR):
        q_lanes, k_lanes, v_lanes = (
            slice(part * GROUP + pair * PAIR, part * GROUP + (pair + 1) * PAIR) for part in range(3)
        )
        q_pair = qkv_ref[:, q_lanes] * scale
        k_pair = qkv_ref[:, k_lanes] * scale
        dctx_pair = dctx_ref[:, q_lanes]
        dq, dk, dv = [], [], []
        for half in range(2):
            mine = (lane // HEAD_DIM) == half
            head = 2 * pair + half
            dk_tiles, dv_tiles = [], []
            for keys in tiles:
                probs = probs_ref[0, 0, head, keys, :]
                d_probs = mm_t(jnp.where(mine, qkv_ref[keys, v_lanes], 0), dctx_pair)
                d_scores = (probs.astype(F32) * (d_probs - inner[head : head + 1, :])).astype(LOW)
                ds_ref[half, keys, :] = d_scores
                dv_tiles.append(mm(probs, dctx_pair))
                dk_tiles.append(mm(d_scores, q_pair))
            dk.append(dk_tiles)
            dv.append(dv_tiles)
            dq.append([t_mm(ds_ref[half, :, rows], k_pair) for rows in tiles])
        for i, rows in enumerate(tiles):
            dqkv_ref[rows, q_lanes] = jnp.where(first, dq[0][i], dq[1][i]).astype(LOW)
            dqkv_ref[rows, k_lanes] = jnp.where(first, dk[0][i], dk[1][i]).astype(LOW)
            dqkv_ref[rows, v_lanes] = jnp.where(first, dv[0][i], dv[1][i]).astype(LOW)
    dqkv = dqkv_ref[...]
    product = mm(xt_ref[0], dqkv)
    bias_q = column_sum(dqkv[:, :GROUP].astype(F32))
    bias_v = column_sum(dqkv[:, 2 * GROUP :].astype(F32))

    @pl.when(row == 0)
    def _():
        acc_ref[...] = product
        vec_ref[...] = vec_in_ref[...]
        vec_ref[0:1, :] = bias_q
        vec_ref[1:2, :] = bias_v

    @pl.when(row > 0)
    def _():
        acc_ref[...] += product
        vec_ref[0:1, :] += bias_q
        vec_ref[1:2, :] += bias_v

    @pl.when(row == seqs - 1)
    def _():
        keep_ref[...], send_ref[...] = split_cores(acc_ref[...], core_ref[0], unit)


def attention_backward(unit, core, xt, qkv, ctx, probs, dctx, table, keep, send):
    rows = ctx.shape[0]
    seqs = rows // SEQ
    mine = lambda g, b: (b, g)
    return pl.pallas_call(
        lambda *refs: attention_backward_kernel(unit, *refs),
        grid=(GROUPS, seqs),
        in_specs=[
            pl.BlockSpec(memory_space=pltpu.SMEM),
            pl.BlockSpec((1, D, SEQ), lambda g, b: (b, 0, 0)),
            pl.BlockSpec((SEQ, TRIO), mine),
            pl.BlockSpec((SEQ, GROUP), mine),
            pl.BlockSpec((SEQ, GROUP), mine),
            pl.BlockSpec((1, 1, GROUP // HEAD_DIM, SEQ, SEQ), lambda g, b: (b, g, 0, 0, 0)),
            pl.BlockSpec((8, GROUP), lambda g, b: (0, g)),
            pl.BlockSpec(memory_space=pl.ANY),
            pl.BlockSpec(memory_space=pl.ANY),
        ],
        out_specs=[
            pl.BlockSpec((D // 2, TRIO), lambda g, b: (0, 1 + g)),
            pl.BlockSpec((D // 2, TRIO), lambda g, b: (0, 1 + g)),
            pl.BlockSpec((SEQ, TRIO), mine),
            pl.BlockSpec((8, GROUP), lambda g, b: (0, g)),
        ],
        out_shape=[like((D // 2, SET), LOW)] * 2 + [like((rows, 3 * D), LOW), like((8, D), F32)],
        input_output_aliases={6: 3, 7: 0, 8: 1},
        scratch_shapes=[pltpu.VMEM((2, SEQ, SEQ), LOW), pltpu.VMEM((D, TRIO), F32)],
        compiler_params=pltpu.CompilerParams(vmem_limit_bytes=VMEM),
        cost_estimate=cost(rows * (6 * D * D + 8 * D * SEQ), 36 * MIB, 0),
        name="attention_backward",
    )(core, xt, qkv, ctx, dctx, probs, table, keep, send)


def input_grad_kernel(da_ref, dqkv_ref, *refs):
    total = da_ref[...].astype(F32)
    for g in range(GROUPS):
        total += mm_t(dqkv_ref[:, g * TRIO : (g + 1) * TRIO], refs[g][...])
    refs[GROUPS][...] = total.astype(LOW)


def input_grad(da, dqkv, weights):
    rows = da.shape[0]
    return pl.pallas_call(
        input_grad_kernel,
        grid=(rows // ROWS,),
        in_specs=[
            pl.BlockSpec((ROWS, D), lambda i: (i, 0)),
            pl.BlockSpec((ROWS, 3 * D), lambda i: (i, 0)),
            *(pl.BlockSpec((D, TRIO), lambda i, g=g: (0, 1 + g)) for g in range(GROUPS)),
        ],
        out_specs=pl.BlockSpec((ROWS, D), lambda i: (i, 0)),
        out_shape=like((rows, D), LOW),
        compiler_params=pltpu.CompilerParams(vmem_limit_bytes=VMEM),
        cost_estimate=cost(6 * rows * D * D, 13 * MIB, 0),
        name="input_grad",
    )(da, dqkv, *[weights] * GROUPS)


def norm_parts(hidden):
    mean = jnp.mean(hidden, axis=1, keepdims=True)
    centred = hidden - mean
    inverse = lax.rsqrt(jnp.mean(centred * centred, axis=1, keepdims=True) + EPS)
    return centred * inverse, inverse


def norm_back(grad, gain, normed, inverse):
    scaled = grad * gain
    mean = jnp.mean(scaled, axis=1, keepdims=True)
    along = jnp.mean(scaled * normed, axis=1, keepdims=True)
    return inverse * (scaled - mean - normed * along)


def column_sum(array):
    return jnp.sum(array, axis=0, keepdims=True)


def gelu_and_slope(v):
    square = v * v
    bent = jnp.tanh(v * (ROOT + ROOT * CUBE * square))
    half = 0.5 + 0.5 * bent
    act = v * half
    slope = half + act * (1.0 - half) * (2.0 * ROOT + 6.0 * ROOT * CUBE * square)
    return act, slope


def order_outer(block_ref, out_ref, unit):
    for o in range(block_ref.shape[0] // unit):
        for j in range(CHUNKS):
            to = (o * CHUNKS + j) * unit
            out_ref[to : to + unit, :] = block_ref[o * unit : (o + 1) * unit, j * D : (j + 1) * D]


def ffn_forward_kernel(
    unit, n1low_ref, outer_ref, wi_ref, bi_ref, vec_ref, n_hbm, cot_hbm,
    slope_ref, gwo_ref, sums_ref, out_hbm, db_hbm, dh2_hbm,
    n_ref, cot_ref, h2_ref, wo_ref, act_ref, out_ref, db_ref, dh2_ref, sem,
):
    step = pl.program_id(0)
    tiles = [slice(i, i + ROWS) for i in range(0, h2_ref.shape[0], ROWS)]
    loads = [
        pltpu.make_async_copy(n_hbm, n_ref, sem.at[0]),
        pltpu.make_async_copy(cot_hbm, cot_ref, sem.at[1]),
    ]
    stores = [
        pltpu.make_async_copy(out_ref, out_hbm, sem.at[2]),
        pltpu.make_async_copy(db_ref, db_hbm, sem.at[3]),
        pltpu.make_async_copy(dh2_ref, dh2_hbm, sem.at[4]),
    ]

    @pl.when(step == 0)
    def _():
        for copy in loads:
            copy.start()
        h2_ref[...] = jnp.zeros_like(h2_ref)

    @pl.when(step < CHUNKS)
    def _():
        order_outer(outer_ref, wo_ref, unit)
        for rows in tiles:
            pre = mm(n1low_ref[rows, :], wi_ref[...]) + bi_ref[...]
            act, slope = gelu_and_slope(pre)
            act = act.astype(LOW)
            act_ref[step, rows, :] = act
            slope_ref[rows, :] = slope.astype(LOW)
            h2_ref[rows, :] += mm(act, wo_ref[...])

    @pl.when(step == CHUNKS - 1)
    def _():
        for copy in loads:
            copy.wait()
        gain, shift = vec_ref[6:7, :], vec_ref[7:8, :]
        sums_ref[...] = jnp.zeros_like(sums_ref)

        @pl.loop(0, h2_ref.shape[0] // ROWS, unroll=2)
        def _(i):
            rows = pl.ds(pl.multiple_of(i * ROWS, ROWS), ROWS)
            n, inverse = norm_parts(
                h2_ref[rows, :] + (n_ref[rows, :] * vec_ref[3:4, :] + vec_ref[4:5, :] + vec_ref[5:6, :])
            )
            out_ref[rows, :] = (n * gain + shift).astype(LOW)
            cot = cot_ref[rows, :].astype(F32)
            dh2 = norm_back(cot, gain, n, inverse)
            dh2_ref[rows, :] = dh2
            db = dh2.astype(LOW)
            db_ref[rows, :] = db
            for j, new in enumerate((column_sum(db.astype(F32)), column_sum(cot * n), column_sum(cot))):
                sums_ref[5 + j : 6 + j, :] += new

        for copy in stores:
            copy.start()

    @pl.when(step >= CHUNKS)
    def _():
        grad = t_mm(act_ref[step - CHUNKS], db_ref[...]).astype(LOW)
        if len(gwo_ref.shape) == 2:
            gwo_ref[...] = grad
        else:
            _, _, sides, lines, deep, _ = gwo_ref.shape
            for i in range(CHUNK // deep):
                core, side, line = i % 2, i // 2 % sides, i // 2 // sides
                gwo_ref[core, 0, side, line] = grad[i * deep : (i + 1) * deep, :]

    @pl.when(step == 2 * CHUNKS - 1)
    def _():
        for copy in stores:
            copy.wait()


def ffn_forward(unit, normed, n1low, cot, rest, b_inner, table, sizes=None):
    rows = normed.shape[0]
    last = CHUNKS - 1
    now = lambda c: jnp.minimum(c, last)
    then = lambda c: jnp.maximum(c - CHUNKS, 0)
    eight = pl.BlockSpec((8, D), lambda c: (0, 0))
    if sizes is None:
        outer_shape = (FF, D)
        outer_block = pl.BlockSpec((CHUNK, D), lambda c: (then(c), 0))
    else:
        dps, lines, sides, cores = sizes
        deep = CHUNKS * unit
        held = CHUNK // (deep * sides * cores)
        outer_shape = (cores, dps, sides, lines, deep, D)
        outer_block = pl.BlockSpec(
            (cores, 1, sides, held, deep, D),
            lambda c: (0, then(c) * held // lines, 0, then(c) % (lines // held), 0, 0),
        )
    anywhere = pl.BlockSpec(memory_space=pl.ANY)
    return pl.pallas_call(
        lambda *refs: ffn_forward_kernel(unit, *refs),
        grid=(2 * CHUNKS,),
        in_specs=[
            pl.BlockSpec((rows, D), lambda c: (0, 0), pipeline_mode=pl.Buffered(1)),
            pl.BlockSpec((D // CHUNKS, FF), lambda c: (now(c), 0)),
            pl.BlockSpec((D, CHUNK), lambda c: (0, CHUNKS + now(c))),
            pl.BlockSpec((1, CHUNK), lambda c: (0, now(c))),
            eight,
            anywhere,
            anywhere,
        ],
        out_specs=[
            pl.BlockSpec((rows, CHUNK), lambda c: (0, now(c))),
            outer_block,
            eight,
            anywhere,
            anywhere,
            anywhere,
        ],
        out_shape=[
            like((rows, FF), LOW),
            like(outer_shape, LOW),
            like((8, D), F32),
            like((rows, D), LOW),
            like((rows, D), LOW),
            like((rows, D), F32),
        ],
        scratch_shapes=[
            pltpu.VMEM((rows, D), F32),
            pltpu.VMEM((rows, D), LOW),
            pltpu.VMEM((rows, D), F32),
            pltpu.VMEM((CHUNK, D), LOW),
            pltpu.VMEM((CHUNKS, rows, CHUNK), LOW),
            pltpu.VMEM((rows, D), LOW),
            pltpu.VMEM((rows, D), LOW),
            pltpu.VMEM((rows, D), F32),
            pltpu.SemaphoreType.DMA((5,)),
        ],
        compiler_params=pltpu.CompilerParams(vmem_limit_bytes=VMEM),
        cost_estimate=cost(6 * rows * D * FF, 34 * MIB, rows * FF),
        name="ffn_forward",
    )(n1low, rest, rest, b_inner, table, normed, cot)


def split_cores(grad, core, unit):
    rows = range(0, grad.shape[0], 2 * unit)
    even = jnp.concatenate([grad[i : i + unit] for i in rows], axis=0)
    odd = jnp.concatenate([grad[i + unit : i + 2 * unit] for i in rows], axis=0)
    return jnp.where(core == 0, even, odd).astype(LOW), jnp.where(core == 0, odd, even).astype(LOW)


def ffn_backward_kernel(
    unit, core_ref, n1t_ref, slope_ref, db_ref, outer_ref, wi_ref, dh2_hbm,
    keep_ref, send_ref, gbi_ref, dn1_ref,
    dpre_ref, wo_ref, dh2_ref, sem,
):
    step = pl.program_id(0)
    tiles = [slice(i, i + ROWS) for i in range(0, db_ref.shape[0], ROWS)]
    order_outer(outer_ref, wo_ref, unit)

    load = pltpu.make_async_copy(dh2_hbm, dh2_ref, sem)

    @pl.when(step == 0)
    def _():
        load.start()
        dn1_ref[...] = jnp.zeros_like(dn1_ref)

    @pl.when(step == CHUNKS - 1)
    def _():
        load.wait()
        dn1_ref[...] += dh2_ref[...]

    bias = jnp.zeros((1, CHUNK), F32)
    for rows in tiles:
        dpre = (mm_t(db_ref[rows, :], wo_ref[...]) * slope_ref[rows, :].astype(F32)).astype(LOW)
        dpre_ref[rows, :] = dpre
        bias += column_sum(dpre.astype(F32))
        dn1_ref[rows, :] += mm_t(dpre, wi_ref[...])
    gbi_ref[...] = bias
    keep_ref[...], send_ref[...] = split_cores(mm(n1t_ref[...], dpre_ref[...]), core_ref[0], unit)


def ffn_backward(unit, core, n1t, slope, db, dh2, rest):
    rows = db.shape[0]
    once = pl.BlockSpec((rows, D), lambda c: (0, 0), pipeline_mode=pl.Buffered(1))
    return pl.pallas_call(
        lambda *refs: ffn_backward_kernel(unit, *refs),
        grid=(CHUNKS,),
        in_specs=[
            pl.BlockSpec(memory_space=pltpu.SMEM),
            pl.BlockSpec((D, rows), lambda c: (0, 0), pipeline_mode=pl.Buffered(1)),
            pl.BlockSpec((rows, CHUNK), lambda c: (0, c)),
            once,
            pl.BlockSpec((D // CHUNKS, FF), lambda c: (c, 0)),
            pl.BlockSpec((D, CHUNK), lambda c: (0, CHUNKS + c)),
            pl.BlockSpec(memory_space=pl.ANY),
        ],
        out_specs=[
            pl.BlockSpec((D // 2, CHUNK), lambda c: (0, c)),
            pl.BlockSpec((D // 2, CHUNK), lambda c: (0, c)),
            pl.BlockSpec((1, CHUNK), lambda c: (0, c)),
            pl.BlockSpec((rows, D), lambda c: (0, 0)),
        ],
        out_shape=[like((D // 2, FF), LOW)] * 2 + [like((1, FF), F32), like((rows, D), F32)],
        scratch_shapes=[
            pltpu.VMEM((rows, CHUNK), LOW),
            pltpu.VMEM((CHUNK, D), LOW),
            pltpu.VMEM((rows, D), F32),
            pltpu.SemaphoreType.DMA,
        ],
        compiler_params=pltpu.CompilerParams(vmem_limit_bytes=VMEM),
        cost_estimate=cost(6 * rows * D * FF, 30 * MIB, 0),
        name="ffn_backward",
    )(core, n1t, slope, db, rest, rest, dh2)


def norm_backward_kernel(
    unit, core_ref, wout_ref, vec_ref, sums_in_ref, n_hbm, inverse_hbm, dn1_hbm, ctx_hbm,
    keep_ref, send_ref, sums_ref, dctx_hbm, da_hbm,
    n_ref, inverse_ref, dn1_ref, ctx_ref, da_ref, dctx_ref, load_sem, store_sem,
):
    tiles = [slice(i, i + ROWS) for i in range(0, n_ref.shape[0], ROWS)]
    pairs = ((n_hbm, n_ref), (inverse_hbm, inverse_ref), (dn1_hbm, dn1_ref), (ctx_hbm, ctx_ref))
    loads = [
        [pltpu.make_async_copy(a.at[rows, :], b.at[rows, :], load_sem.at[i, j]) for j, (a, b) in enumerate(pairs)]
        for i, rows in enumerate(tiles)
    ]
    stores = [
        [
            pltpu.make_async_copy(da_ref.at[rows, :], da_hbm.at[rows, :], store_sem.at[i, 0]),
            pltpu.make_async_copy(dctx_ref.at[rows, :], dctx_hbm.at[rows, :], store_sem.at[i, 1]),
        ]
        for i, rows in enumerate(tiles)
    ]
    for group in loads:
        for copy in group:
            copy.start()
    sums = [jnp.zeros((1, D), F32)] * 3
    for i, rows in enumerate([*tiles, None]):
        if rows is not None:
            for copy in loads[i]:
                copy.wait()
        if i > 0:
            dctx_ref[tiles[i - 1], :] = mm_t(da_ref[tiles[i - 1], :], wout_ref[...]).astype(LOW)
        if rows is not None:
            n = n_ref[rows, :]
            dn1 = dn1_ref[rows, :]
            da = norm_back(dn1, vec_ref[3:4, :], n, inverse_ref[rows, 0:1]).astype(LOW)
            da_ref[rows, :] = da
            new = (column_sum(da.astype(F32)), column_sum(dn1 * n), column_sum(dn1))
            sums = [a + b for a, b in zip(sums, new)]
            stores[i][0].start()
        if i > 0:
            stores[i - 1][1].start()
    keep_ref[...], send_ref[...] = split_cores(t_mm(ctx_ref[...], da_ref[...]), core_ref[0], unit)
    sums_ref[...] = sums_in_ref[...]
    for i in range(3):
        sums_ref[2 + i : 3 + i, :] = sums[i]
    for group in stores:
        for copy in group:
            copy.wait()


def norm_backward(unit, core, normed, inverse, dn1, ctx, weights, table, sums):
    rows = normed.shape[0]
    eight = pl.BlockSpec((8, D), lambda i: (0, 0))
    half = pl.BlockSpec((D // 2, D), lambda i: (0, 0))
    anywhere = pl.BlockSpec(memory_space=pl.ANY)
    return pl.pallas_call(
        lambda *refs: norm_backward_kernel(unit, *refs),
        grid=(1,),
        in_specs=[
            pl.BlockSpec(memory_space=pltpu.SMEM),
            pl.BlockSpec((D, D), lambda i: (0, 0)),
            eight,
            eight,
        ]
        + [anywhere] * 4,
        out_specs=[half, half, eight, anywhere, anywhere],
        out_shape=[like((D // 2, SET), LOW)] * 2
        + [like((8, D), F32), like((rows, D), LOW), like((rows, D), LOW)],
        scratch_shapes=[
            pltpu.VMEM((rows, D), F32),
            pltpu.VMEM((rows, PAIR), F32),
            pltpu.VMEM((rows, D), F32),
            pltpu.VMEM((rows, D), LOW),
            pltpu.VMEM((rows, D), LOW),
            pltpu.VMEM((rows, D), LOW),
            pltpu.SemaphoreType.DMA((rows // ROWS, 4)),
            pltpu.SemaphoreType.DMA((rows // ROWS, 2)),
        ],
        compiler_params=pltpu.CompilerParams(vmem_limit_bytes=VMEM),
        cost_estimate=cost(4 * rows * D * D, 17 * MIB, 0),
        name="norm_backward",
    )(core, weights, table, sums, normed, inverse, dn1, ctx)


def after(values, *others):
    return lax.optimization_barrier((values, others))[0]


def whole(array):
    return pl.BlockSpec(array.shape, lambda *_: (0,) * len(array.shape))


def pack_kernel(wq_ref, wk_ref, wv_ref, wout_ref, wi_ref, wo_ref, *refs):
    vectors, (set_ref, rest_ref) = refs[:9], refs[9:]
    unit = wq_ref.shape[0]
    set_ref[:, :D] = wout_ref[...]
    for g in range(GROUPS):
        for part, ref in enumerate((wq_ref, wk_ref, wv_ref)):
            to = D + g * TRIO + part * GROUP
            set_ref[:, to : to + GROUP] = ref[:, g * GROUP : (g + 1) * GROUP]
    table = jnp.zeros((unit, PAIR), F32)
    row = lax.broadcasted_iota(jnp.int32, (unit, PAIR), 0)
    for i, ref in enumerate(vectors):
        size = ref.shape[1]
        line = jnp.concatenate([ref[...].astype(F32), jnp.zeros((1, PAIR - size), F32)], axis=1)
        table = jnp.where(row == i, line, table)
    set_ref[:, 4 * D :] = table.astype(LOW)
    for j in range(CHUNKS):
        rest_ref[:, j * D : (j + 1) * D] = wo_ref[j * unit : (j + 1) * unit, :]
    rest_ref[:, FF:] = wi_ref[...]


def pack(wq, wk, wv, wout, wi, wo, vectors):
    unit = wq.shape[0]
    args = (wq, wk, wv, wout, wi, wo, *(v.reshape(1, -1) for v in vectors))
    shapes = [like((unit, SET), LOW), like((unit, 2 * FF), LOW)]
    return pl.pallas_call(
        pack_kernel,
        grid=(1,),
        in_specs=[whole(a) for a in args],
        out_specs=[whole(a) for a in shapes],
        out_shape=shapes,
        compiler_params=pltpu.CompilerParams(vmem_limit_bytes=VMEM),
        name="pack",
    )(*args)


def stack_kernel(*refs):
    for i, ref in enumerate(refs[:-1]):
        refs[-1][i] = ref[...]


def stack(pieces):
    shape = like((len(pieces), *pieces[0].shape), pieces[0].dtype)
    return pl.pallas_call(
        stack_kernel,
        grid=(1,),
        in_specs=[pl.BlockSpec(memory_space=pltpu.VMEM)] * len(pieces),
        out_specs=whole(shape),
        out_shape=shape,
        compiler_params=pltpu.CompilerParams(vmem_limit_bytes=8 * MIB),
        name="stack",
    )(*pieces)


class Slice:
    def __init__(self):
        self.sizes = tuple(lax.axis_size(name) for name in AXES)
        self.dp, self.line, self.side, self.core = (lax.axis_index(name) for name in AXES)
        self.offsets = [(a, b) for a in range(self.sizes[0]) for b in range(self.sizes[2])]

    def to_core(self, array):
        return lax.ppermute(array, "core", [(0, 1), (1, 0)])

    def to_plane(self, array, offset):
        dps, _, sides, _ = self.sizes
        pairs = [
            (i * sides + j, (i + offset[0]) % dps * sides + (j + offset[1]) % sides)
            for i in range(dps)
            for j in range(sides)
        ]
        return lax.ppermute(array, ("dp", "side"), pairs)

    def to_line(self, array, shift):
        count = self.sizes[1]
        return lax.ppermute(array, "line", [(i, (i + shift) % count) for i in range(count)])

    def gather(self, mine):
        dps, lines, sides, _ = self.sizes
        unit, columns = mine.shape
        line = stack([mine] + [self.to_line(mine, s) for s in range(1, lines)])
        here = [line if o == (0, 0) else self.to_plane(line, o) for o in self.offsets]
        there = [self.to_core(a) for a in here]
        place = jnp.stack([self.dp, self.line, self.side, self.core]).astype(jnp.int32)
        pieces = here + there


        def kernel(place_ref, *refs):
            out_ref = refs[-1]
            for i in range(len(pieces)):
                a, b = self.offsets[i % len(here)]
                dp = lax.rem(place_ref[0] + dps - a, dps)
                side = lax.rem(place_ref[2] + sides - b, sides)
                core = place_ref[3] if i < len(here) else 1 - place_ref[3]
                for s in range(lines):
                    along = lax.rem(place_ref[1] + lines - s, lines)
                    out_ref[((dp * lines + along) * sides + side) * 2 + core] = refs[i][s]

        count = dps * lines * sides * 2
        return pl.pallas_call(
            kernel,
            in_specs=[pl.BlockSpec(memory_space=pltpu.SMEM)]
            + [pl.BlockSpec(memory_space=pltpu.VMEM)] * len(pieces),
            out_specs=pl.BlockSpec(memory_space=pltpu.VMEM),
            out_shape=like((count, unit, columns), mine.dtype),
            compiler_params=pltpu.CompilerParams(vmem_limit_bytes=8 * MIB),
            name="place",
        )(place, *pieces).reshape(-1, columns)


    def chips_sum(self, grad):
        return lax.psum_scatter(grad.reshape(-1, *grad.shape[3:]), ("core", "dp", "side"), scatter_dimension=0)

    def line_sum(self, grad):
        return lax.psum_scatter(grad, "line", scatter_dimension=0)

    def join_cores(self, keep, send, unit):
        keep, send = (part.reshape(-1, 1, unit, part.shape[1]) for part in (keep, send))
        mine = self.core == 0
        pair = [jnp.where(mine, keep, send), jnp.where(mine, send, keep)]
        return jnp.concatenate(pair, axis=1).reshape(-1, keep.shape[3])


    def block(self, grad, got, dp, side, columns=None):
        dps, lines, sides, _ = self.sizes
        first, last = columns or (0, grad.shape[1])
        start = (0 if dp is None else dp, 0, 0 if side is None else side, 0, first)
        size = (dps if dp is None else 1, lines, sides if side is None else 1)
        total = 0.0
        for part in (grad, got):
            part = part.reshape(dps, lines, sides, -1, grad.shape[1])
            total += lax.dynamic_slice(part, start, (*size, part.shape[3], last - first)).astype(F32)
        return total


    def plane_messages(self, grad, got):
        dps, _, sides, _ = self.sizes
        return [
            self.block(grad, got, lax.rem(self.dp + a, dps), lax.rem(self.side + b, sides))[0, :, 0].astype(LOW)
            for a, b in self.offsets[1:]
        ]

    def plane_exchange(self, messages):
        return [self.to_plane(m, o) for m, o in zip(messages, self.offsets[1:])]

    def plane_done(self, grad, got, parts):
        total = self.block(grad, got, self.dp, self.side)[0, :, 0]
        return self.along_line((total + sum(p.astype(F32) for p in parts)).astype(LOW))


    def halves(self, grad):
        columns = grad.shape[1]
        return (0, columns // 2), (columns // 2, columns)

    def first_messages(self, grad, got):
        one, two = self.halves(grad)
        return (
            self.block(grad, got, None, 1 - self.side, one).astype(LOW),
            self.block(grad, got, 1 - self.dp, None, two).astype(LOW),
        )

    def first_exchange(self, messages):
        return self.to_plane(messages[0], (0, 1)), self.to_plane(messages[1], (1, 0))

    def second_messages(self, grad, got, more):
        one, two = self.halves(grad)
        a = self.block(grad, got, 1 - self.dp, self.side, one)
        b = self.block(grad, got, self.dp, 1 - self.side, two)
        a += lax.dynamic_slice_in_dim(more[0], 1 - self.dp, 1, 0).astype(F32)
        b += lax.dynamic_slice_in_dim(more[1], 1 - self.side, 1, 2).astype(F32)
        return a.astype(LOW), b.astype(LOW)

    def second_exchange(self, messages):
        return self.to_plane(messages[0], (1, 0)), self.to_plane(messages[1], (0, 1))

    def second_done(self, grad, got, more, most):
        one, two = self.halves(grad)
        a = self.block(grad, got, self.dp, self.side, one) + most[0].astype(F32)
        b = self.block(grad, got, self.dp, self.side, two) + most[1].astype(F32)
        a += lax.dynamic_slice_in_dim(more[0], self.dp, 1, 0).astype(F32)
        b += lax.dynamic_slice_in_dim(more[1], self.side, 1, 2).astype(F32)
        return self.along_line(jnp.concatenate([a[0, :, 0], b[0, :, 0]], axis=2).astype(LOW))

    def along_line(self, total):
        lines = self.sizes[1]
        at = [lax.rem(self.line + s, lines) for s in range(lines)]
        return [lax.dynamic_index_in_dim(total, i, 0, keepdims=False) for i in at]

    def line_exchange(self, messages):
        return messages[:1] + [self.to_line(m, s) for s, m in enumerate(messages) if s]


def finish_kernel(count, *refs):
    parts, (wout_ref, wq_ref, wk_ref, wv_ref), vectors = refs[:count], refs[count : count + 4], refs[count + 4 :]
    total = sum(ref[...].astype(F32) for ref in parts)
    wout_ref[...] = total[:, :D]
    for g in range(GROUPS):
        for part, ref in enumerate((wq_ref, wk_ref, wv_ref)):
            at = D + g * TRIO + part * GROUP
            ref[:, g * GROUP : (g + 1) * GROUP] = total[:, at : at + GROUP]
    for i, ref in enumerate(vectors):
        ref[...] = total[i : i + 1, 4 * D : 4 * D + ref.shape[1]]


def finish(parts):
    unit = parts[0].shape[0]
    shapes = [like((unit, D), F32)] * 4 + [like((1, unit), F32)] * 8 + [like((1, CHUNKS * unit), F32)]
    outs = pl.pallas_call(
        lambda *refs: finish_kernel(len(parts), *refs),
        grid=(1,),
        in_specs=[pl.BlockSpec(memory_space=pltpu.VMEM)] * len(parts),
        out_specs=[whole(a) for a in shapes],
        out_shape=shapes,
        compiler_params=pltpu.CompilerParams(vmem_limit_bytes=8 * MIB),
        name="finish",
    )(*parts)
    return outs[:4], [v.reshape(-1) for v in outs[4:]]


def vector_rows(table, b_inner, count):
    unit = D // count
    eight = table.reshape(8, count, unit).transpose(1, 0, 2)
    inner = b_inner.reshape(count, 1, CHUNKS * unit)
    eight = jnp.pad(eight, ((0, 0), (0, 0), (0, PAIR - unit)))
    inner = jnp.pad(inner, ((0, 0), (0, unit - 9), (0, PAIR - CHUNKS * unit)))
    return jnp.concatenate([eight, inner], axis=1).astype(LOW)


def on_device(block_input, segment_ids, cotangent, *params):
    w_query, w_key, w_value, w_out, w_inner, w_outer = (params[i] for i in MATRICES)
    vectors = [params[i] for i in VECTORS]
    unit = w_query.shape[0]
    count = D // unit
    mesh = Slice()
    quick = mesh.sizes == (2, 4, 2, 2) and unit == 24
    x = block_input.reshape(-1, D)
    cot = cotangent.reshape(-1, D)

    if quick:
        mine, rest_mine = pack(w_query, w_key, w_value, w_out, w_inner, w_outer, vectors)
        rest = lax.all_gather(rest_mine, AXES, axis=0, tiled=True)
        weights = mesh.gather(mine)
        side = weights[:, 4 * D :].reshape(count, unit, PAIR)
        table = side[:, :8, :unit].transpose(1, 0, 2).reshape(8, D).astype(F32)
        b_inner = side[:, 8, : CHUNKS * unit].reshape(1, FF).astype(F32)
    else:
        trios = [w[:, g : g + GROUP] for g in range(0, D, GROUP) for w in (w_query, w_key, w_value)]
        full = lax.all_gather(jnp.concatenate([w_out, *trios, w_inner], axis=1), AXES, axis=0, tiled=True)
        outer = lax.all_gather(w_outer, AXES, axis=0, tiled=True)
        vector = lax.all_gather(jnp.concatenate(vectors), AXES, axis=0).astype(F32)
        weights = full[:, : 4 * D]
        table = jnp.concatenate([vector[:, i * unit : (i + 1) * unit].reshape(1, D) for i in range(8)])
        b_inner = vector[:, 8 * unit :].reshape(1, FF)
        unit = 24
        outer = outer.reshape(-1, CHUNKS, unit, D).transpose(0, 2, 1, 3).reshape(D, FF)
        rest = jnp.concatenate([outer, full[:, 4 * D :]], axis=1)

    core = mesh.core[None].astype(jnp.int32)
    qkv, ctx, probs, xt, normed, inverse, n1low, n1t = attention_forward(x, segment_ids, weights, table)
    slope, g_outer, sums, result, db, dh2 = ffn_forward(
        unit, normed, n1low, cot, rest, b_inner, table, mesh.sizes if quick else None
    )
    if quick:
        db = after(db, g_outer)
        g_outer = mesh.chips_sum(g_outer)
    keep, send, g_b_inner, dn1 = ffn_backward(unit, core, n1t, slope, db, dh2, rest)
    if not quick:
        g_inner = mesh.join_cores(keep, send, unit)
        keep, send, sums, dctx, da = norm_backward(unit, core, normed, inverse, dn1, ctx, weights, table, sums)
        keep, send, dqkv, sums = attention_backward(unit, core, xt, qkv, ctx, probs, dctx, sums, keep, send)
        late = mesh.join_cores(keep, send, unit)
        dx = input_grad(da, dqkv, weights)
        wide = jnp.concatenate([late[:, : 4 * D], g_inner], axis=1)
        wide = lax.psum_scatter(wide, AXES, scatter_dimension=0, tiled=True).astype(F32)
        g_outer = lax.psum_scatter(g_outer, AXES, scatter_dimension=0, tiled=True).astype(F32)
        vector = jnp.concatenate([*sums.reshape(8, count, -1), g_b_inner.reshape(count, -1)], axis=1)
        vector = lax.psum_scatter(vector.reshape(-1), AXES, scatter_dimension=0, tiled=True)
        size = D // count
        vectors = [vector[i * size : (i + 1) * size] for i in range(8)] + [vector[8 * size :]]
        matrices = [wide[:, :D]] + [
            jnp.concatenate([wide[:, g + part : g + part + GROUP] for g in range(D, 4 * D, TRIO)], axis=1)
            for part in range(0, TRIO, GROUP)
        ]
        g_inner = wide[:, 4 * D :]
    else:
        g_inner = keep
        dn1 = after(dn1, send)
        got = mesh.to_core(send)
        keep, send, sums, dctx, da = norm_backward(unit, core, normed, inverse, dn1, ctx, weights, table, sums)
        inner_got, sums = after((got, sums), dctx)
        message = mesh.first_messages(g_inner, inner_got)
        sums = after(sums, message)
        more = mesh.first_exchange(message)
        late, send, dqkv, sums = attention_backward(unit, core, xt, qkv, ctx, probs, dctx, sums, keep, send)
        late, send, more, g_outer = after((late, send, more, g_outer), dqkv)
        g_outer = mesh.line_sum(g_outer)
        g_b_inner = after(g_b_inner, dqkv)
        vector = vector_rows(sums, g_b_inner, count).reshape(-1, 2, unit, PAIR)
        at = (mesh.core, 1 - mesh.core)
        vector = [lax.dynamic_index_in_dim(vector, i, 1, keepdims=False).reshape(-1, PAIR) for i in at]
        late = lax.dynamic_update_slice(late, vector[0], (0, 4 * D))
        send = lax.dynamic_update_slice(send, vector[1], (0, 4 * D))
        got = mesh.to_core(send)
        message = mesh.second_messages(g_inner, inner_got, more)
        got, dqkv = after((got, dqkv), message)
        most = mesh.second_exchange(message)
        message = mesh.plane_messages(late, got)
        most, dqkv = after((most, dqkv), message)
        parts = mesh.plane_exchange(message)
        lines = mesh.line_exchange(mesh.second_done(g_inner, inner_got, more, most))
        dx = input_grad(da, dqkv, weights)
        parts, g_inner, g_outer = after((parts, lines, g_outer), dx)
        message = mesh.plane_done(late, got, parts)
        g_outer, g_inner = after((g_outer, g_inner), message)
        matrices, vectors = finish(mesh.line_exchange(message))
        g_outer = g_outer.astype(F32)
        g_inner = sum(p.astype(F32) for p in g_inner)
    g_out, *matrices = matrices

    shards = [None] * len(params)
    for i, value in zip(MATRICES, (*matrices, g_out, g_inner, g_outer)):
        shards[i] = value
    for i, value in zip(VECTORS, vectors):
        shards[i] = value
    return (result.reshape(block_input.shape), dx.reshape(block_input.shape), *shards)


def solution(mesh):
    sizes = (mesh.shape["dp"], mesh.shape["fsdp"] // 4, 2, 2)
    parts = Mesh(np.asarray(mesh.devices).reshape(sizes), AXES)
    vector, matrix, rows = P(AXES), P(AXES, None), P(AXES, None, None)
    params = tuple(vector if i in VECTORS else matrix for i in range(15))
    return jax.shard_map(
        on_device,
        mesh=parts,
        in_specs=(rows, matrix, rows) + params,
        out_specs=(rows, rows) + params,
        check_vma=False,
    )
```
